32 devices in a mesh: shard: 8 (over z, y), tensor: 4 (over x, core).
Axes of the slice: x: 2, y: 2, z: 4, core: 2. Of those that a mesh axis runs over, the one named last changes fastest.
Arguments:
- grad: bfloat16 [138, 128, 896], P(None, 'shard', 'tensor'), may hold values from -2000 to 2000
- owner: int32 [138], replicated, may hold values from 0 to 7, as said below
- counts: int32 [8], replicated, may hold values from 1 to 128
- master: float32 [160, 896, 128], P('shard', 'tensor'), may hold values from -6 to 6
- moment1: float32 [160, 896, 128], P('shard', 'tensor'), may hold values from -3 to 3
- moment2: float32 [160, 896, 128], P('shard', 'tensor'), may hold values from 0.05 to 1
- average: float32 [160, 896, 128], P('shard', 'tensor'), may hold values from -6 to 6
Outputs:
- new_weight: bfloat16 [138, 128, 896], P(None, 'shard', 'tensor')
- new_master: float32 [160, 896, 128], P('shard', 'tensor')
- new_moment1: float32 [160, 896, 128], P('shard', 'tensor')
- new_moment2: float32 [160, 896, 128], P('shard', 'tensor')
- new_average: float32 [160, 896, 128], P('shard', 'tensor')
The draws below stay inside these ranges and needn't reach their ends.
Inputs may be any that keep to these rules, and one draw needn't show every extreme that they name: No owner holds more than 20 slabs, and one owner holds exactly 20; every other owner holds at most 17 slabs, and some owner other than that one holds exactly 17.
All inputs are finite; a program needn't handle non-finite values.
Results may differ from the reference program's by a relative error of at most 0.001.
Values may be sent and summed in bfloat16 or wider, within the bound.
A program may use at most 128 MiB of HBM per device.

```python
import math
import jax
import jax.numpy as jnp
from jax import lax

D = 896
SLAB_ROWS = 128
STEP = 20
LAYER_SLABS = 130
EMB = 8
SLABS = 138
MOST = 20
SLOTS = 160
N_SHARD = 8


def draw_owner(key, part):
    key_order = jax.random.fold_in(key, 11)
    key_heavy = jax.random.fold_in(key, 12)
    key_light = jax.random.fold_in(key, 13)
    placing = jax.random.permutation(key_order, SLABS)
    heavy = jax.random.randint(key_heavy, (), 0, N_SHARD)
    others = jax.random.permutation(key_light, N_SHARD - 1)
    position = jnp.arange(SLABS, dtype=jnp.int32)
    light = others[(position - MOST) % (N_SHARD - 1)]
    light = light + (light >= heavy).astype(jnp.int32)
    chosen = jnp.where(position < MOST, heavy, light).astype(jnp.int32)
    owner = jnp.zeros((SLABS,), jnp.int32).at[placing].set(chosen)
    return owner.astype(jnp.int32)


def draw_grad(key, part):
    key_base = jax.random.fold_in(key, 21)
    key_rows = jax.random.fold_in(key, 22)
    key_cols = jax.random.fold_in(key, 23)
    row_scale = jnp.exp(jax.random.uniform(key_rows, (SLABS, SLAB_ROWS, 1), jnp.float32) * math.log(10.0))
    col_scale = jnp.exp(jax.random.uniform(key_cols, (1, 1, D), jnp.float32) * math.log(10.0))
    ramp = jnp.arange(SLAB_ROWS, dtype=jnp.float32) / (SLAB_ROWS - 1)
    base = jnp.clip(jax.random.normal(key_base, (SLABS, SLAB_ROWS, D), jnp.float32), -6.0, 6.0)
    rising = jnp.exp(ramp * math.log(3.0))
    values = base * row_scale * col_scale * rising[None, :, None]
    return values.astype(jnp.bfloat16)


def set_ends(entries, stream_key, low, high):
    shape = entries.shape
    index_at = [jax.random.randint(jax.random.fold_in(stream_key, axis), (), 0, shape[axis]) for axis in range(len(shape))]
    entries = entries.at[tuple(index_at)].set(low)
    longest = shape.index(max(shape))
    index_at[longest] = (index_at[longest] + 1) % shape[longest]
    return entries.at[tuple(index_at)].set(high)


def block_levels(own_key, shape, pieces, smallest, largest):
    level, own = 1.0, jax.random.fold_in(own_key, 6)
    for dim, blocks in pieces:
        steps = jnp.exp(jax.random.uniform(jax.random.fold_in(own, dim), (blocks,), jnp.float32, smallest / len(pieces), largest / len(pieces)))
        level = level * jnp.repeat(steps, shape[dim] // blocks).reshape([-1 if axis == dim else 1 for axis in range(len(shape))])
    return level


def noise(key, shape, spread, reach, shards=(), kind=jnp.bfloat16):
    drawn = jax.random.normal(key, shape, jnp.float32) * spread
    if len(shards) > 0:
        drawn = block_levels(key, shape, shards, -0.22, 0.18) * drawn
    return jnp.clip(drawn, min=-reach, max=reach).astype(kind)


def setup_inputs(seed: int = 0) -> dict:
    seeds = jax.random.split(jax.random.key(seed), 8)
    grad = draw_grad(jax.random.fold_in(seeds[7], 71), 0)
    owner = draw_owner(jax.random.fold_in(seeds[7], 71), 0)
    counts = set_ends(jax.random.randint(seeds[2], (EMB,), 1, 129), jax.random.fold_in(seeds[2], 1), 1, 128).astype(jnp.int32)
    master = noise(seeds[3], (SLOTS, D, SLAB_ROWS), 1.0, 6.0, ((0, 8), (1, 4)), jnp.float32)
    moment1 = noise(seeds[4], (SLOTS, D, SLAB_ROWS), 0.5, 3.0, ((0, 8), (1, 4)), jnp.float32)
    moment2 = jnp.clip(jnp.exp(math.log(1.0) - 2.9957323 * jax.random.uniform(seeds[5], (SLOTS, D, SLAB_ROWS), jnp.float32) ** block_levels(seeds[5], (SLOTS, D, SLAB_ROWS), ((0, 8), (1, 4)), -0.2, 0.2)), 0.05, 1.0)
    average = noise(seeds[6], (SLOTS, D, SLAB_ROWS), 1.0, 6.0, ((0, 8), (1, 4)), jnp.float32)
    return dict(grad=grad, owner=owner, counts=counts, master=master, moment1=moment1, moment2=moment2, average=average)


BETA_ONE = 0.9
BETA_TWO = 0.95
ADAM_EPS = 1e-08
LEARN_RATE = 0.02
WEIGHT_DECAY = 0.1
AVERAGE_DECAY = 0.99

def slot_tables(owner, owner_count, capacity):
    slab_count = owner.shape[0]
    owner_ids = jnp.arange(owner_count, dtype=jnp.int32)
    owner_hits = (owner[:, None] == owner_ids[None, :]).astype(jnp.int32)
    earlier = jnp.cumsum(owner_hits, axis=0) - owner_hits
    slot_rank = lax.optimization_barrier(jnp.sum(earlier * owner_hits, axis=1)).astype(jnp.int32)
    slot_ids = jnp.arange(capacity, dtype=jnp.int32)
    matched = (owner[None, None, :] == owner_ids[None, :, None]) & (slot_rank[None, None, :] == slot_ids[:, None, None])
    filled = jnp.any(matched, axis=2)
    source = lax.optimization_barrier(jnp.sum(jnp.where(matched, jnp.arange(slab_count, dtype=jnp.int32)[None, None, :], 0), axis=2)).astype(jnp.int32)
    return (slot_rank, filled, source)

def adam_step(gradient, clip_scale, weight_old, first_old, second_old, average_old, live_rows):
    clipped = gradient * clip_scale
    first_new = BETA_ONE * first_old + (1.0 - BETA_ONE) * clipped
    second_new = BETA_TWO * second_old + (1.0 - BETA_TWO) * clipped * clipped
    update = first_new / (1.0 - BETA_ONE ** STEP) / (jnp.sqrt(second_new / (1.0 - BETA_TWO ** STEP)) + ADAM_EPS)
    weight_new = weight_old - LEARN_RATE * (update + WEIGHT_DECAY * weight_old)
    average_new = AVERAGE_DECAY * average_old + (1.0 - AVERAGE_DECAY) * weight_new
    return (jnp.where(live_rows, weight_new, weight_old), jnp.where(live_rows, first_new, first_old), jnp.where(live_rows, second_new, second_old), jnp.where(live_rows, average_new, average_old))

def reference(grad, owner, counts, master, moment1, moment2, average):
    slot_rank, filled, source = slot_tables(owner, N_SHARD, MOST)
    full_counts = jnp.concatenate([jnp.full((LAYER_SLABS,), SLAB_ROWS, jnp.int32), counts.astype(jnp.int32)])
    row_index = jnp.arange(SLAB_ROWS, dtype=jnp.int32)
    train_live = (row_index[None, :] < full_counts[:, None])[:, :, None]
    values = grad.astype(jnp.float32)
    square_total = jnp.sum(jnp.where(train_live, values * values, 0.0))
    max_norm = 0.5 * math.sqrt(SLABS * SLAB_ROWS * D)
    clip_scale = jnp.minimum(1.0, max_norm / (jnp.sqrt(square_total) + 1e-06))
    flat_source = source.T.reshape(-1)
    flat_filled = filled.T.reshape(-1)
    slot_grad = jnp.transpose(jnp.take(values, flat_source, axis=0), (0, 2, 1))
    slot_live = (flat_filled[:, None] & (row_index[None, :] < jnp.take(full_counts, flat_source)[:, None]))[:, None, :]
    results = adam_step(slot_grad, clip_scale, master, moment1, moment2, average, slot_live)
    keep = flat_filled[:, None, None]
    new_master = jnp.where(keep, results[0], 0.0)
    new_moment1 = jnp.where(keep, results[1], 0.0)
    new_moment2 = jnp.where(keep, results[2], 0.0)
    new_average = jnp.where(keep, results[3], 0.0)
    picked = jnp.take(new_master, owner * MOST + slot_rank, axis=0)
    new_weight = jnp.transpose(picked, (0, 2, 1)).astype(jnp.bfloat16)
    return (new_weight, new_master, new_moment1, new_moment2, new_average)
```

```python
import functools
import math

import jax
import jax.numpy as jnp
from jax import lax
from jax.experimental import pallas as pl
from jax.experimental.pallas import tpu as pltpu
from jax.sharding import PartitionSpec as P

D = 896
STEP = 20


BETA_ONE = 0.9
BETA_TWO = 0.95
ADAM_EPS = 1e-08
LEARN_RATE = 0.02
WEIGHT_DECAY = 0.1
AVERAGE_DECAY = 0.99

LANES = 128
PLACES = (0, 2, 3, 4, 1, 5, 6)
SPARE_SLOTS = 3
SPARE_BLOCKS = 5
MESH = pl.DeviceIdType.MESH


def slot_tables(owner, owner_count, capacity):
    slab_count = owner.shape[0]
    owner_ids = jnp.arange(owner_count, dtype=jnp.int32)
    slabs = jnp.arange(slab_count, dtype=jnp.int32)
    before = (owner[:, None] == owner[None, :]) & (slabs[None, :] < slabs[:, None])
    slot_rank = jnp.sum(before.astype(jnp.int32), axis=1)
    place = owner * capacity + slot_rank
    slot_ids = jnp.arange(owner_count * capacity, dtype=jnp.int32)
    matched = place[None, :] == slot_ids[:, None]
    marked = jnp.sum(jnp.where(matched, slabs[None, :] + 1, 0), axis=1)
    return (place, marked)


def peer_of(step, count):
    half = count // 2
    away = (step + 1) // 2
    return jnp.where(step % 2 == 1, half - away, half + away)


def subsets(distances):
    found = [()]
    for d in distances:
        found = found + [c + (d,) for c in found]
    return found


def flipped(index, distances):
    for d in distances:
        index = index + d * (1 - 2 * lax.rem(index // d, 2))
    return index


def exchange_kernel(with_sum, with_spare, *refs):
    refs = list(refs)
    out_ref = refs.pop(0)
    spare_in = refs.pop(0) if with_spare and with_sum else None
    part_ref = refs.pop(0) if with_sum else None
    in_ref = refs.pop(0)
    spare_out = refs.pop(0) if with_spare and not with_sum else None
    total_ref = refs.pop(0) if with_sum else None
    if with_sum:
        shard_parts, mid_part, tensor_parts = refs[:3]
        refs = refs[3:]
    local_sem, send_sem, recv_sem = refs[:3]
    refs = refs[3:]
    if with_sum:
        small_send, small_recv, tens_send, tens_recv = refs[:4]
        refs = refs[4:]
    if with_spare:
        spare_local, spare_send, spare_recv = refs[:3]
        refs = refs[3:]
        if not with_sum:
            held, landed = refs
    count = lax.axis_size("shard")
    columns = lax.axis_size("tensor")
    me = lax.axis_index("shard")
    col = lax.axis_index("tensor")

    def each(total, body):
        def step(k, carry):
            body(k)
            return carry
        lax.fori_loop(0, total, step, 0)

    def shard_peer(k):
        return lax.rem(me + peer_of(k, count), count)

    def tensor_peer(k):
        return lax.rem(col + k + 1, columns)

    rows = out_ref.shape[1]
    spare_rows = with_spare
    direct = pl.ds(0, rows - spare_rows)
    beyond = pl.ds(rows - spare_rows, spare_rows)
    distances = []
    while with_spare and 2 ** len(distances) < count:
        distances.append(2 ** len(distances))
    if spare_in is not None:
        keep_own = pltpu.make_async_copy(spare_in, in_ref.at[me, beyond], spare_local)
        keep_own.start()
    if spare_out is not None:
        keep_own = pltpu.make_async_copy(out_ref.at[:, beyond], held, spare_local)
        keep_own.start()
    own = pltpu.make_async_copy(
        out_ref.at[me, direct], in_ref.at[me, direct], local_sem
    )
    own.start()
    barrier = pltpu.get_barrier_semaphore()
    each(count - 1, lambda k: pl.semaphore_signal(
        barrier, inc=1, device_id=(shard_peer(k), col), device_id_type=MESH))
    greeted = count - 1
    if with_sum:
        each(columns - 1, lambda k: pl.semaphore_signal(
            barrier, inc=1, device_id=(me, tensor_peer(k)), device_id_type=MESH))
        greeted += columns - 1
    pl.semaphore_wait(barrier, greeted)

    def small(k):
        peer = shard_peer(k)
        return pltpu.make_async_remote_copy(
            part_ref, shard_parts.at[me], small_send.at[peer], small_recv.at[me],
            device_id=(peer, col), device_id_type=MESH)

    def small_in(k):
        peer = shard_peer(k)
        return pltpu.make_async_remote_copy(
            part_ref, shard_parts.at[peer], small_send.at[peer], small_recv.at[peer],
            device_id=(peer, col), device_id_type=MESH)

    def tens(k):
        peer = tensor_peer(k)
        return pltpu.make_async_remote_copy(
            mid_part, tensor_parts.at[col], tens_send.at[peer], tens_recv.at[col],
            device_id=(me, peer), device_id_type=MESH)

    def tens_in(k):
        peer = tensor_peer(k)
        return pltpu.make_async_remote_copy(
            mid_part, tensor_parts.at[peer], tens_send.at[peer], tens_recv.at[peer],
            device_id=(me, peer), device_id_type=MESH)

    def big(k):
        peer = shard_peer(k)
        return pltpu.make_async_remote_copy(
            out_ref.at[peer, direct], in_ref.at[me, direct], send_sem.at[peer], recv_sem.at[me],
            device_id=(peer, col), device_id_type=MESH)

    def big_in(k):
        peer = shard_peer(k)
        return pltpu.make_async_remote_copy(
            out_ref.at[peer, direct], in_ref.at[peer, direct], send_sem.at[peer], recv_sem.at[peer],
            device_id=(peer, col), device_id_type=MESH)

    def gather(number, chosen, d):
        unit = flipped(me, chosen)
        source = in_ref.at[unit, beyond] if chosen else spare_in
        return pltpu.make_async_remote_copy(
            source, in_ref.at[unit, beyond], spare_send.at[number], spare_recv.at[number],
            device_id=(flipped(me, (d,)), col), device_id_type=MESH)

    def gather_in(number, chosen, d):
        unit = flipped(me, chosen + (d,))
        return pltpu.make_async_remote_copy(
            spare_in, in_ref.at[unit, beyond], spare_send.at[number], spare_recv.at[number],
            device_id=(flipped(me, (d,)), col), device_id_type=MESH)

    def scatter(number, chosen, d):
        return pltpu.make_async_remote_copy(
            held.at[flipped(me, chosen + (d,))], landed.at[number],
            spare_send.at[number], spare_recv.at[number],
            device_id=(flipped(me, (d,)), col), device_id_type=MESH)

    steps = []
    if spare_in is not None:
        for at in range(len(distances)):
            d = distances[-1 - at]
            steps.append((d, subsets(distances[len(distances) - at:])))
    if spare_out is not None:
        for at, d in enumerate(distances):
            steps.append((d, subsets(distances[at + 1:])))
    number = 0
    numbered = []
    for d, chosen in steps:
        numbered.append([(number + i, c, d) for i, c in enumerate(chosen)])
        number += len(chosen)

    def spare_start(step):
        for one in step:
            (gather if spare_in is not None else scatter)(*one).start()

    def spare_finish(step):
        for one in step:
            if spare_in is not None:
                gather_in(*one).wait()
            else:
                scatter(*one).wait()
                mine = flipped(me, one[1])
                added = held[mine].astype(jnp.float32) + landed[one[0]].astype(jnp.float32)
                held[mine] = added.astype(held.dtype)

    if with_sum:
        each(count - 1, lambda k: small(k).start())
    if with_spare:
        if not with_sum:
            keep_own.wait()
        spare_start(numbered[0])
    def sum_shard():
        each(count - 1, lambda k: small_in(k).wait())
        mid_part[...] = part_ref[...]

        def add_shard(k):
            mid_part[...] += shard_parts[shard_peer(k)]
        each(count - 1, add_shard)
        each(columns - 1, lambda k: tens(k).start())

    stages = max(len(numbered), 1)
    share = (count - 1) // stages
    each(share, lambda k: big(k).start())
    for at in range(1, stages):
        spare_finish(numbered[at - 1])
        spare_start(numbered[at])
        if with_sum and at == 1:
            sum_shard()
        more = share if at + 1 < stages else count - 1 - at * share
        each(more, lambda k, at=at: big(k + at * share).start())
    if with_spare:
        spare_finish(numbered[-1])
        if with_sum:
            keep_own.wait()
        else:
            spare_out[...] = held[me]
    if with_sum:
        if stages == 1:
            sum_shard()
        each(columns - 1, lambda k: tens_in(k).wait())
        total_ref[...] = mid_part[...]

        def add_tensor(k):
            total_ref[...] += tensor_parts[tensor_peer(k)]
        each(columns - 1, add_tensor)
    each(count - 1, lambda k: big_in(k).wait())
    own.wait()


def exchange(blocks, part, collective_id, mesh_sizes, spare=None):
    count, columns = mesh_sizes
    with_sum = part is not None
    any_spec = pl.BlockSpec(memory_space=pl.ANY)
    vmem_spec = pl.BlockSpec(memory_space=pltpu.VMEM)
    out_shape = [jax.ShapeDtypeStruct(blocks.shape, blocks.dtype)]
    scratch = [
        pltpu.SemaphoreType.DMA(()),
        pltpu.SemaphoreType.DMA((count,)),
        pltpu.SemaphoreType.DMA((count,)),
    ]
    operands = [blocks]
    in_specs = [any_spec]
    out_specs = [any_spec]
    if spare is not None and with_sum:
        operands.append(spare)
        in_specs.append(any_spec)
    if spare is not None and not with_sum:
        out_shape.append(jax.ShapeDtypeStruct(spare.shape, spare.dtype))
        out_specs.append(vmem_spec)
    if with_sum:
        out_shape.append(jax.ShapeDtypeStruct(part.shape, part.dtype))
        out_specs.append(vmem_spec)
        in_specs.append(vmem_spec)
        operands.append(part)
        scratch = [
            pltpu.VMEM((count,) + part.shape, part.dtype),
            pltpu.VMEM(part.shape, part.dtype),
            pltpu.VMEM((columns,) + part.shape, part.dtype),
        ] + scratch + [
            pltpu.SemaphoreType.DMA((count,)),
            pltpu.SemaphoreType.DMA((count,)),
            pltpu.SemaphoreType.DMA((columns,)),
            pltpu.SemaphoreType.DMA((columns,)),
        ]
    if spare is not None:
        scratch = scratch + [
            pltpu.SemaphoreType.DMA(()),
            pltpu.SemaphoreType.DMA((count,)),
            pltpu.SemaphoreType.DMA((count,)),
        ]
        if not with_sum:
            scratch = scratch + [
                pltpu.VMEM((count,) + spare.shape, spare.dtype),
                pltpu.VMEM((count,) + spare.shape, spare.dtype),
            ]
    spare_rows = 0 if spare is None else spare.shape[0]
    return pl.pallas_call(
        functools.partial(exchange_kernel, with_sum, spare_rows),
        out_shape=out_shape,
        in_specs=in_specs,
        out_specs=out_specs,
        scratch_shapes=scratch,
        compiler_params=pltpu.CompilerParams(
            collective_id=collective_id, has_side_effects=True
        ),
    )(*operands)


def adam_update(gradient, clip_scale, limit, weight_old, first_old, second_old, average_old):
    lane = lax.broadcasted_iota(jnp.int32, gradient.shape, 1)
    live = lane < limit
    keep = lane >= jnp.where(limit < 0, gradient.shape[1], 0)
    clipped = gradient * clip_scale
    first_new = BETA_ONE * first_old + (1.0 - BETA_ONE) * clipped
    second_new = BETA_TWO * second_old + (1.0 - BETA_TWO) * clipped * clipped
    update = (first_new * (1.0 / (1.0 - BETA_ONE**STEP))) / (
        jnp.sqrt(second_new * (1.0 / (1.0 - BETA_TWO**STEP))) + ADAM_EPS
    )
    weight_new = weight_old - LEARN_RATE * (update + WEIGHT_DECAY * weight_old)
    average_new = AVERAGE_DECAY * average_old + (1.0 - AVERAGE_DECAY) * weight_new
    pairs = ((weight_new, weight_old), (first_new, first_old), (second_new, second_old),
             (average_new, average_old))
    return [jnp.where(keep, jnp.where(live, new, old), 0.0) for new, old in pairs]


def picker(rows, columns, shift=0):
    row = lax.broadcasted_iota(jnp.int32, (rows, columns), 0)
    column = lax.broadcasted_iota(jnp.int32, (rows, columns), 1)
    return (row + shift == column).astype(jnp.bfloat16)


def turned(pick, block):
    return lax.dot_general(
        pick, block, (((1,), (1,)), ((), ())), preferred_element_type=jnp.float32
    )


def adam_kernel(max_norm, part_rows, limit_ref, total_ref, grad_ref, *refs):
    old_refs, weight_out, new_refs = refs[:4], refs[4], refs[5:]
    per_step, columns, slab_rows = new_refs[0].shape
    total = total_ref[0:1, :]
    clip_scale = jnp.minimum(1.0, max_norm / (jnp.sqrt(total) + 1e-06))

    def advance(slot, window, gradient):
        limit = limit_ref[pl.program_id(0) * per_step + slot]
        results = adam_update(
            gradient, clip_scale, limit, *[ref[slot, window, :] for ref in old_refs]
        )
        for ref, value in zip(new_refs, results):
            ref[slot, window, :] = value
        return results[0].astype(jnp.bfloat16)

    eye = picker(slab_rows, slab_rows)
    if part_rows is None:
        for slot in range(per_step):
            weight = advance(slot, pl.ds(0, columns),
                             turned(picker(columns, columns), grad_ref[slot]))
            weight_out[slot] = turned(eye, weight).astype(jnp.bfloat16)
        return

    rest = columns - LANES
    share = rest // 3

    def packed(index):
        rows = pl.ds(PLACES[index] * part_rows, part_rows)
        return grad_ref[:, rows, :].reshape(slab_rows, LANES)

    def send(index, weight):
        rows = pl.ds(PLACES[index] * part_rows, part_rows)
        block = turned(eye, weight).astype(jnp.bfloat16)
        weight_out[:, rows, :] = block.reshape(-1, part_rows, LANES)

    main_pick = picker(LANES, LANES)
    rest_pick = picker(rest, LANES)
    share_pick = picker(share, LANES, rest)
    rests = []
    for slot in range(4):
        send(slot, advance(slot, pl.ds(0, LANES), turned(main_pick, packed(slot))))
        if slot < 3:
            gradient = turned(rest_pick, packed(4 + slot))
        else:
            gradient = jnp.concatenate(
                [turned(share_pick, packed(4 + k)) for k in range(3)], axis=0
            )
        rests.append(advance(slot, pl.ds(LANES, rest), gradient))
    for k in range(3):
        piece = rests[3][k * share:(k + 1) * share]
        send(4 + k, jnp.concatenate([rests[k], piece], axis=0))


def adam(limits, total, arrived, master, moment1, moment2, average, max_norm, part_rows):
    capacity, columns, slab_rows = master.shape
    per_step = 1 if part_rows is None else 4
    state = pl.BlockSpec((per_step, columns, slab_rows), lambda s, _: (s, 0, 0))
    if part_rows is None:
        rows = pl.BlockSpec((per_step, slab_rows, columns), lambda s, _: (s, 0, 0))
    else:
        rows = pl.BlockSpec(
            (slab_rows // part_rows, 7 * part_rows, LANES), lambda s, _: (0, s, 0)
        )
    whole = pl.BlockSpec(total.shape, lambda s, _: (0, 0))
    return pl.pallas_call(
        functools.partial(adam_kernel, max_norm, part_rows),
        grid_spec=pltpu.PrefetchScalarGridSpec(
            num_scalar_prefetch=1,
            grid=(capacity // per_step,),
            in_specs=[whole, rows, state, state, state, state],
            out_specs=[rows, state, state, state, state],
        ),
        out_shape=[jax.ShapeDtypeStruct(arrived.shape, jnp.bfloat16)]
        + [jax.ShapeDtypeStruct(master.shape, jnp.float32)] * 4,
        compiler_params=pltpu.CompilerParams(vmem_limit_bytes=60 << 20),
    )(limits, total, arrived, master, moment1, moment2, average)


def prepare_kernel(owner_count, capacity, me_ref, owner_ref, counts_ref, grad_hbm, packed_ref,
                   spare_ref, part_ref, source_ref, limit_ref, filled_ref, grad_ref, grad_sem):
    slab_count, part_rows, columns = grad_ref.shape
    load = pltpu.make_async_copy(grad_hbm, grad_ref, grad_sem)
    load.start()
    emb = counts_ref.shape[0]
    layer_slabs = slab_count - emb
    slab_rows = part_rows * owner_count
    rest = columns - LANES
    share = rest // 3

    def clear(k, carry):
        source_ref[k] = -1
        return carry
    lax.fori_loop(0, owner_count * capacity, clear, 0, unroll=8)
    for o in range(owner_count):
        filled_ref[o] = 0

    def deal(i, carry):
        o = owner_ref[i]
        rank = filled_ref[o]
        filled_ref[o] = rank + 1
        source_ref[o * capacity + rank] = i
        return carry
    lax.fori_loop(0, slab_count, deal, 0, unroll=6)

    for s in range(capacity):
        slab = source_ref[me_ref[0] * capacity + s]
        count = counts_ref[jnp.maximum(slab - layer_slabs, 0)]
        limit_ref[s] = jnp.where(slab < 0, -1, jnp.where(slab < layer_slabs, slab_rows, count))

    load.wait()
    groups = capacity // 4

    def pack(t, carry):
        p = t // groups
        g = t % groups
        base = g * (7 * part_rows)
        for j in range(4):
            slab = jnp.maximum(source_ref[p * capacity + g * 4 + j], 0)
            rows = pl.ds(pl.multiple_of(base + PLACES[j] * part_rows, part_rows), part_rows)
            packed_ref[p, rows, :] = grad_ref[slab, :, 0:LANES]
            if j < 3:
                rows = pl.ds(pl.multiple_of(base + PLACES[4 + j] * part_rows, part_rows), part_rows)
                packed_ref[p, rows, 0:rest] = grad_ref[slab, :, LANES:columns]
            else:
                for k in range(3):
                    rows = pl.ds(
                        pl.multiple_of(base + PLACES[4 + k] * part_rows, part_rows), part_rows
                    )
                    first = LANES + k * share
                    packed_ref[p, rows, rest:LANES] = grad_ref[slab, :, first:first + share]
        return carry
    lax.fori_loop(0, owner_count * groups, pack, 0, unroll=2)

    fullest = 0
    for o in range(1, owner_count):
        fullest = jnp.where(filled_ref[o] > capacity - SPARE_SLOTS, o, fullest)
    spare_rows = spare_ref.shape[0]
    spare_ref[...] = packed_ref[fullest, pl.ds(packed_ref.shape[1] - spare_rows, spare_rows), :]

    def squares(i, carry):
        values = grad_ref[i].astype(jnp.float32)
        return carry + values * values
    acc = lax.fori_loop(
        0, layer_slabs, squares, jnp.zeros((part_rows, columns), jnp.float32), unroll=10
    )
    row = lax.broadcasted_iota(jnp.int32, (part_rows, columns), 0) + me_ref[0] * part_rows
    for e in range(emb):
        values = grad_ref[layer_slabs + e].astype(jnp.float32)
        acc += jnp.where(row < counts_ref[e], values * values, 0.0)
    part_ref[...] = jnp.broadcast_to(jnp.sum(acc, keepdims=True), part_ref.shape)


def prepare(me, owner, counts, grad, owner_count, capacity):
    part_rows = grad.shape[1]
    smem = pl.BlockSpec(memory_space=pltpu.SMEM)
    vmem = pl.BlockSpec(memory_space=pltpu.VMEM)
    packed_shape = (owner_count, capacity // 4 * 7 * part_rows, LANES)
    return pl.pallas_call(
        functools.partial(prepare_kernel, owner_count, capacity),
        in_specs=[smem, smem, smem, pl.BlockSpec(memory_space=pltpu.HBM)],
        out_specs=[vmem, vmem, vmem, smem, smem],
        out_shape=[
            pltpu.VMEM(packed_shape, grad.dtype),
            pltpu.VMEM((SPARE_BLOCKS * part_rows, LANES), grad.dtype),
            pltpu.VMEM((8, LANES), jnp.float32),
            jax.ShapeDtypeStruct((owner_count * capacity,), jnp.int32),
            jax.ShapeDtypeStruct((capacity,), jnp.int32),
        ],
        scratch_shapes=[
            pltpu.SMEM((owner_count,), jnp.int32),
            pltpu.VMEM(grad.shape, grad.dtype),
            pltpu.SemaphoreType.DMA(()),
        ],
        compiler_params=pltpu.CompilerParams(vmem_limit_bytes=60 << 20),
    )(me, owner, counts, grad)


GROUP = 4
TILES = 7


def step_kernel(max_norm, limit_ref, packed_ref, spare_in, part_ref, *refs):
    old_hbm, refs = refs[:4], refs[4:]
    returned, spare_out, states, refs = refs[0], refs[1], refs[2:6], refs[6:]
    arrived, weights, shard_parts, mid_part, tensor_parts, held, landed, refs = refs[:7] + (refs[7:],)
    (state_sem, own_sem, back_sem, keep_sem, small_send, small_recv, tens_send, tens_recv,
     grad_send, grad_recv, weight_send, weight_recv, gather_send, gather_recv,
     scatter_send, scatter_recv) = refs
    count = lax.axis_size("shard")
    columns = lax.axis_size("tensor")
    me = lax.axis_index("shard")
    col = lax.axis_index("tensor")
    capacity, width, slab_rows = states[0].shape
    part_rows = slab_rows // count
    groups = capacity // GROUP
    group_rows = TILES * part_rows
    spare_rows = spare_in.shape[0]
    direct_rows = packed_ref.shape[1] - spare_rows
    last_rows = direct_rows - (groups - 1) * group_rows
    direct = pl.ds(0, direct_rows)
    beyond = pl.ds(direct_rows, spare_rows)
    last = groups - 1

    def each(total, body):
        def step(k, carry):
            body(k)
            return carry
        lax.fori_loop(0, total, step, 0)

    def shard_peer(k):
        return lax.rem(me + peer_of(k, count), count)

    def tensor_peer(k):
        return lax.rem(col + k + 1, columns)

    loads = [pltpu.make_async_copy(old, new, state_sem.at[i])
             for i, (old, new) in enumerate(zip(old_hbm, states))]
    for load in loads:
        load.start()
    own = pltpu.make_async_copy(packed_ref.at[me, direct], arrived.at[me, direct], own_sem)
    own.start()
    keep = pltpu.make_async_copy(spare_in, arrived.at[me, beyond], keep_sem)
    keep.start()

    barrier = pltpu.get_barrier_semaphore()
    each(count - 1, lambda k: pl.semaphore_signal(
        barrier, inc=1, device_id=(shard_peer(k), col), device_id_type=MESH))
    each(columns - 1, lambda k: pl.semaphore_signal(
        barrier, inc=1, device_id=(me, tensor_peer(k)), device_id_type=MESH))
    pl.semaphore_wait(barrier, count + columns - 2)

    def small(k, sender):
        peer = shard_peer(k)
        slot = me if sender else peer
        return pltpu.make_async_remote_copy(
            part_ref, shard_parts.at[slot], small_send.at[peer], small_recv.at[slot],
            device_id=(peer, col), device_id_type=MESH)

    def tens(k, sender):
        peer = tensor_peer(k)
        slot = col if sender else peer
        return pltpu.make_async_remote_copy(
            mid_part, tensor_parts.at[slot], tens_send.at[peer], tens_recv.at[slot],
            device_id=(me, peer), device_id_type=MESH)

    def block(source, target, send, recv, k, group, rows, sender):
        peer = shard_peer(k)
        slot = me if sender else peer
        window = pl.ds(pl.multiple_of(group * group_rows, part_rows), rows)
        return pltpu.make_async_remote_copy(
            source.at[peer, window], target.at[slot, window],
            send.at[group, peer], recv.at[group, slot],
            device_id=(peer, col), device_id_type=MESH)

    def grad_block(k, group, rows, sender):
        return block(packed_ref, arrived, grad_send, grad_recv, k, group, rows, sender)

    def weight_block(k, group, rows, sender):
        return block(weights, returned, weight_send, weight_recv, k, group, rows, sender)

    distances = []
    while 2 ** len(distances) < count:
        distances.append(2 ** len(distances))

    def numbered(pairs):
        found, number = [], 0
        for d, chosen in pairs:
            found.append([(number + i, c, d) for i, c in enumerate(chosen)])
            number += len(chosen)
        return found
    gather_steps = numbered([
        (distances[-1 - at], subsets(distances[len(distances) - at:]))
        for at in range(len(distances))
    ])
    scatter_steps = numbered([
        (d, subsets(distances[at + 1:])) for at, d in enumerate(distances)
    ])

    def gather(number, chosen, d, sender):
        unit = flipped(me, chosen if sender else chosen + (d,))
        source = arrived.at[unit, beyond] if chosen and sender else spare_in
        return pltpu.make_async_remote_copy(
            source, arrived.at[unit, beyond], gather_send.at[number], gather_recv.at[number],
            device_id=(flipped(me, (d,)), col), device_id_type=MESH)

    def scatter(number, chosen, d):
        return pltpu.make_async_remote_copy(
            held.at[flipped(me, chosen + (d,))], landed.at[number],
            scatter_send.at[number], scatter_recv.at[number],
            device_id=(flipped(me, (d,)), col), device_id_type=MESH)

    def gather_start(at):
        for one in gather_steps[at]:
            gather(*one, True).start()

    def gather_finish(at):
        for one in gather_steps[at]:
            gather(*one, True).wait_send()
            gather(*one, False).wait_recv()

    def scatter_start(at):
        for one in scatter_steps[at]:
            scatter(*one).start()

    def scatter_finish(at):
        for one in scatter_steps[at]:
            scatter(*one).wait()
            mine = flipped(me, one[1])
            added = held[mine].astype(jnp.float32) + landed[one[0]].astype(jnp.float32)
            held[mine] = added.astype(held.dtype)

    each(count - 1, lambda k: small(k, True).start())
    gather_start(0)
    each(count - 1, lambda k: grad_block(k, 0, group_rows, True).start())
    each(count - 1, lambda k: grad_block(k, 1, group_rows, True).start())
    each(count - 1, lambda k: grad_block(k, last, last_rows, True).start())
    for g in range(2, last):
        each(count - 1, lambda k, g=g: grad_block(k, g, group_rows, True).start())

    def add_shard(k):
        small(k, False).wait()
        mid_part[...] += shard_parts[shard_peer(k)]

    mid_part[...] = part_ref[...]
    each(count - 1, add_shard)
    each(columns - 1, lambda k: tens(k, True).start())
    gather_finish(0)
    gather_start(1)
    own.wait()
    keep.wait()
    for load in loads:
        load.wait()
    total = mid_part[0:1, :]
    each(columns - 1, lambda k: tens(k, False).wait())
    for k in range(columns - 1):
        total = total + tensor_parts[tensor_peer(k), 0:1, :]
    clip_scale = jnp.minimum(1.0, max_norm / (jnp.sqrt(total) + 1e-06))
    gather_finish(1)
    gather_start(2)

    rest = width - LANES
    share = rest // 3
    eye = picker(slab_rows, slab_rows)

    def compute(group):
        base = group * group_rows

        def rows_of(index):
            return pl.ds(pl.multiple_of(base + PLACES[index] * part_rows, part_rows), part_rows)

        def advance(slot, window, gradient):
            place = group * GROUP + slot
            results = adam_update(
                gradient, clip_scale, limit_ref[place], *[ref[place, window, :] for ref in states]
            )
            for ref, value in zip(states, results):
                ref[place, window, :] = value
            return results[0].astype(jnp.bfloat16)

        def packed(index):
            return arrived[:, rows_of(index), :].reshape(slab_rows, LANES)

        def send(index, weight):
            done = turned(eye, weight).astype(jnp.bfloat16)
            weights[:, rows_of(index), :] = done.reshape(count, part_rows, LANES)

        rest_pick = picker(rest, LANES)
        share_pick = picker(share, LANES, rest)
        rests = []
        for slot in range(GROUP):
            send(slot, advance(slot, pl.ds(0, LANES), turned(eye, packed(slot))))
            if slot < 3:
                gradient = turned(rest_pick, packed(4 + slot))
            else:
                gradient = jnp.concatenate(
                    [turned(share_pick, packed(4 + k)) for k in range(3)], axis=0
                )
            rests.append(advance(slot, pl.ds(LANES, rest), gradient))
        for k in range(3):
            piece = rests[3][k * share:(k + 1) * share]
            send(4 + k, jnp.concatenate([rests[k], piece], axis=0))

    back = pltpu.make_async_copy(weights.at[me, direct], returned.at[me, direct], back_sem)
    early = min(2, last)

    def turn(t, carry):
        at_last = t == early
        group = jnp.where(at_last, last, jnp.where(t > early, t - 1, t))

        @pl.when(jnp.logical_not(at_last))
        def _():
            each(count - 1, lambda k: grad_block(k, group, group_rows, False).wait())

        @pl.when(at_last)
        def _():
            each(count - 1, lambda k: grad_block(k, last, last_rows, False).wait())
            gather_finish(2)

        compute(group)

        @pl.when(jnp.logical_not(at_last))
        def _():
            each(count - 1, lambda k: weight_block(k, group, group_rows, True).start())

        @pl.when(at_last)
        def _():
            held[...] = weights[:, beyond, :]
            scatter_start(0)
            each(count - 1, lambda k: weight_block(k, last, last_rows, True).start())

        @pl.when(t == early + 1)
        def _():
            scatter_finish(0)
            scatter_start(1)

        @pl.when(t == early + 2)
        def _():
            scatter_finish(1)
            scatter_start(2)
        return carry

    lax.fori_loop(0, groups, turn, 0)
    back.start()
    scatter_finish(2)
    spare_out[...] = held[me]
    for g in range(groups):
        rows = group_rows if g < last else last_rows
        each(count - 1, lambda k, g=g, rows=rows: weight_block(k, g, rows, False).wait())
    back.wait()


def step(limits, packed, spare, part, states, max_norm, mesh_sizes):
    count, columns = mesh_sizes
    capacity, width, slab_rows = states[0].shape
    groups = capacity // GROUP
    vmem = pl.BlockSpec(memory_space=pltpu.VMEM)
    smem = pl.BlockSpec(memory_space=pltpu.SMEM)
    hbm = pl.BlockSpec(memory_space=pltpu.HBM)
    dma = pltpu.SemaphoreType.DMA
    return pl.pallas_call(
        functools.partial(step_kernel, max_norm),
        in_specs=[smem, vmem, vmem, vmem] + [hbm] * 4,
        out_specs=[vmem] * 6,
        out_shape=[
            pltpu.VMEM(packed.shape, packed.dtype),
            pltpu.VMEM(spare.shape, spare.dtype),
        ] + [pltpu.VMEM(s.shape, s.dtype) for s in states],
        scratch_shapes=[
            pltpu.VMEM(packed.shape, packed.dtype),
            pltpu.VMEM(packed.shape, packed.dtype),
            pltpu.VMEM((count,) + part.shape, part.dtype),
            pltpu.VMEM(part.shape, part.dtype),
            pltpu.VMEM((columns,) + part.shape, part.dtype),
            pltpu.VMEM((count,) + spare.shape, spare.dtype),
            pltpu.VMEM((count,) + spare.shape, spare.dtype),
            dma((4,)), dma(()), dma(()), dma(()),
            dma((count,)), dma((count,)), dma((columns,)), dma((columns,)),
            dma((groups, count)), dma((groups, count)), dma((groups, count)), dma((groups, count)),
            dma((count,)), dma((count,)), dma((count,)), dma((count,)),
        ],
        compiler_params=pltpu.CompilerParams(
            collective_id=2, has_side_effects=True, vmem_limit_bytes=40 << 20
        ),
    )(limits, packed, spare, part, *states)


def unpack_kernel(capacity, source_ref, packed_ref, spare_ref, *refs):
    fresh, weight_hbm, kept, weight_ref, weight_sem, kept_sem = (
        refs[:4], refs[4], refs[5:9], refs[9], refs[10], refs[11]
    )
    stores = [pltpu.make_async_copy(new, out, kept_sem.at[i])
              for i, (new, out) in enumerate(zip(fresh, kept))]
    for store in stores:
        store.start()
    slab_count, part_rows, columns = weight_hbm.shape
    rest = columns - LANES
    share = rest // 3
    groups = capacity // 4

    def unpack(t, carry):
        p = t // groups
        g = t % groups
        base = g * (7 * part_rows)

        def piece(index):
            rows = pl.ds(pl.multiple_of(base + PLACES[index] * part_rows, part_rows), part_rows)
            return packed_ref[p, rows, :]
        blocks = [piece(index) for index in range(7)]
        for j in range(4):
            slab = source_ref[p * capacity + g * 4 + j]
            slab = jnp.where(slab < 0, slab_count, slab)
            weight_ref[slab, :, 0:LANES] = blocks[j]
            if j < 3:
                weight_ref[slab, :, LANES:columns] = blocks[4 + j][:, 0:rest]
            else:
                weight_ref[slab, :, LANES:columns] = jnp.concatenate(
                    [blocks[4 + k][:, rest:LANES] for k in range(3)], axis=1
                )
        return carry
    lax.fori_loop(0, packed_ref.shape[0] * groups, unpack, 0, unroll=2)
    fullest = 0
    for p in range(1, packed_ref.shape[0]):
        first_spare = source_ref[p * capacity + capacity - SPARE_SLOTS]
        fullest = jnp.where(first_spare >= 0, p, fullest)
    last = (groups - 1) * (7 * part_rows)
    spare = [None, None] + [
        spare_ref[pl.ds(k * part_rows, part_rows), :] for k in range(SPARE_BLOCKS)
    ]
    spare[1] = packed_ref[fullest, pl.ds(last + part_rows, part_rows), :]
    for j in range(1, 4):
        slab = source_ref[fullest * capacity + capacity - 4 + j]
        slab = jnp.where(slab < 0, slab_count, slab)
        weight_ref[slab, :, 0:LANES] = spare[PLACES[j]]
        if j < 3:
            weight_ref[slab, :, LANES:columns] = spare[PLACES[4 + j]][:, 0:rest]
        else:
            weight_ref[slab, :, LANES:columns] = jnp.concatenate(
                [spare[PLACES[4 + k]][:, rest:LANES] for k in range(3)], axis=1
            )
    store = pltpu.make_async_copy(weight_ref.at[pl.ds(0, slab_count)], weight_hbm, weight_sem)
    store.start()
    store.wait()
    for store in stores:
        store.wait()


def unpack(source, packed, spare, states, weight_shape, capacity):
    slab_count, part_rows, columns = weight_shape
    vmem = pl.BlockSpec(memory_space=pltpu.VMEM)
    hbm = pl.BlockSpec(memory_space=pltpu.HBM)
    return pl.pallas_call(
        functools.partial(unpack_kernel, capacity),
        in_specs=[pl.BlockSpec(memory_space=pltpu.SMEM), vmem, vmem] + [vmem] * 4,
        out_specs=[hbm] * 5,
        out_shape=[jax.ShapeDtypeStruct(weight_shape, packed.dtype)]
        + [jax.ShapeDtypeStruct(s.shape, s.dtype) for s in states],
        scratch_shapes=[
            pltpu.VMEM((slab_count + 1, part_rows, columns), packed.dtype),
            pltpu.SemaphoreType.DMA(()),
            pltpu.SemaphoreType.DMA((4,)),
        ],
        compiler_params=pltpu.CompilerParams(vmem_limit_bytes=40 << 20),
    )(source, packed, spare, *states)


def per_device(mesh_sizes, grad, owner, counts, master, moment1, moment2, average):
    owner_count = mesh_sizes[0]
    slab_count, part_rows, columns = grad.shape
    capacity = master.shape[0]
    slab_rows = part_rows * owner_count
    max_norm = 0.5 * math.sqrt(slab_count * slab_rows * D)
    layer_slabs = slab_count - counts.shape[0]
    self_index = lax.axis_index("shard")
    states = (master, moment1, moment2, average)

    if part_rows % 16 == 0 and capacity % 4 == 0 and (columns - LANES) * 4 == 3 * LANES and (
        owner_count & (owner_count - 1) == 0
    ):
        grad, *states = [pltpu.with_memory_space_constraint(x, pltpu.HBM) for x in (grad,) + states]
        outgoing, spare, part, source, limits = prepare(
            self_index.astype(jnp.int32)[None], owner, counts, grad, owner_count, capacity
        )
        returned, spare, *states = step(
            limits, outgoing, spare, part, states, max_norm, mesh_sizes
        )
        return tuple(unpack(source, returned, spare, states, grad.shape, capacity))

    full_counts = jnp.concatenate([jnp.full((layer_slabs,), slab_rows, jnp.int32), counts])
    row_index = self_index * part_rows + jnp.arange(part_rows, dtype=jnp.int32)
    train_live = row_index[None, :] < full_counts[:, None]
    values = grad.astype(jnp.float32)
    part = jnp.sum(jnp.where(train_live[:, :, None], values * values, 0.0))
    part = jnp.broadcast_to(part, (8, LANES))

    place, marked = slot_tables(owner, owner_count, capacity)
    source = jnp.maximum(marked - 1, 0)
    own_marked = lax.dynamic_slice_in_dim(marked, self_index * capacity, capacity)
    own_live = jnp.take(full_counts, jnp.maximum(own_marked - 1, 0), mode="clip")
    limits = jnp.where(own_marked > 0, own_live, -1)

    outgoing = jnp.take(grad, source, axis=0, mode="clip")
    outgoing = outgoing.reshape(owner_count, capacity * part_rows, columns)
    arrived, total = exchange(outgoing, part, 0, mesh_sizes)
    arrived = arrived.reshape(owner_count, capacity, part_rows, columns)
    arrived = arrived.transpose(1, 0, 2, 3).reshape(capacity, slab_rows, columns)
    weights, *new_states = adam(limits, total, arrived, *states, max_norm, None)
    weights = weights.reshape(capacity, owner_count, part_rows, columns)
    weights = weights.transpose(1, 0, 2, 3)
    weights = weights.reshape(owner_count, capacity * part_rows, columns)
    (returned,) = exchange(weights, None, 1, mesh_sizes)
    returned = returned.reshape(owner_count * capacity, part_rows, columns)
    new_weight = jnp.take(returned, place, axis=0, mode="clip")
    return (new_weight, *new_states)


def solution(mesh):
    sizes = (mesh.shape["shard"], mesh.shape["tensor"])
    return jax.shard_map(
        functools.partial(per_device, sizes),
        mesh=mesh,
        in_specs=(
            P(None, "shard", "tensor"),
            P(),
            P(),
            P("shard", "tensor", None),
            P("shard", "tensor", None),
            P("shard", "tensor", None),
            P("shard", "tensor", None),
        ),
        out_specs=(
            P(None, "shard", "tensor"),
            P("shard", "tensor", None),
            P("shard", "tensor", None),
            P("shard", "tensor", None),
            P("shard", "tensor", None),
        ),
        check_vma=False,
    )
```

```python
import functools
import math

import jax
import jax.numpy as jnp
from jax import lax
from jax.experimental import pallas as pl
from jax.experimental.pallas import tpu as pltpu
from jax.sharding import PartitionSpec as P

D = 896
STEP = 20


BETA_ONE = 0.9
BETA_TWO = 0.95
ADAM_EPS = 1e-08
LEARN_RATE = 0.02
WEIGHT_DECAY = 0.1
AVERAGE_DECAY = 0.99

LANES = 128
PLACES = (0, 2, 3, 4, 1, 5, 6)
SPARE_SLOTS = 3
SPARE_BLOCKS = 5
MESH = pl.DeviceIdType.MESH


def slot_tables(owner, owner_count, capacity):
    slab_count = owner.shape[0]
    owner_ids = jnp.arange(owner_count, dtype=jnp.int32)
    slabs = jnp.arange(slab_count, dtype=jnp.int32)
    before = (owner[:, None] == owner[None, :]) & (slabs[None, :] < slabs[:, None])
    slot_rank = jnp.sum(before.astype(jnp.int32), axis=1)
    place = owner * capacity + slot_rank
    slot_ids = jnp.arange(owner_count * capacity, dtype=jnp.int32)
    matched = place[None, :] == slot_ids[:, None]
    marked = jnp.sum(jnp.where(matched, slabs[None, :] + 1, 0), axis=1)
    return (place, marked)


def peer_of(step, count):
    half = count // 2
    away = (step + 1) // 2
    return jnp.where(step % 2 == 1, half - away, half + away)


def subsets(distances):
    found = [()]
    for d in distances:
        found = found + [c + (d,) for c in found]
    return found


def flipped(index, distances):
    for d in distances:
        index = index + d * (1 - 2 * lax.rem(index // d, 2))
    return index


def exchange_kernel(with_sum, with_spare, *refs):
    refs = list(refs)
    out_ref = refs.pop(0)
    spare_in = refs.pop(0) if with_spare and with_sum else None
    part_ref = refs.pop(0) if with_sum else None
    in_ref = refs.pop(0)
    spare_out = refs.pop(0) if with_spare and not with_sum else None
    total_ref = refs.pop(0) if with_sum else None
    if with_sum:
        shard_parts, mid_part, tensor_parts = refs[:3]
        refs = refs[3:]
    local_sem, send_sem, recv_sem = refs[:3]
    refs = refs[3:]
    if with_sum:
        small_send, small_recv, tens_send, tens_recv = refs[:4]
        refs = refs[4:]
    if with_spare:
        spare_local, spare_send, spare_recv = refs[:3]
        refs = refs[3:]
        if not with_sum:
            held, landed = refs
    count = lax.axis_size("shard")
    columns = lax.axis_size("tensor")
    me = lax.axis_index("shard")
    col = lax.axis_index("tensor")

    def each(total, body):
        def step(k, carry):
            body(k)
            return carry
        lax.fori_loop(0, total, step, 0)

    def shard_peer(k):
        return lax.rem(me + peer_of(k, count), count)

    def tensor_peer(k):
        return lax.rem(col + k + 1, columns)

    rows = out_ref.shape[1]
    spare_rows = with_spare
    direct = pl.ds(0, rows - spare_rows)
    beyond = pl.ds(rows - spare_rows, spare_rows)
    distances = []
    while with_spare and 2 ** len(distances) < count:
        distances.append(2 ** len(distances))
    if spare_in is not None:
        keep_own = pltpu.make_async_copy(spare_in, in_ref.at[me, beyond], spare_local)
        keep_own.start()
    if spare_out is not None:
        keep_own = pltpu.make_async_copy(out_ref.at[:, beyond], held, spare_local)
        keep_own.start()
    own = pltpu.make_async_copy(
        out_ref.at[me, direct], in_ref.at[me, direct], local_sem
    )
    own.start()
    barrier = pltpu.get_barrier_semaphore()
    each(count - 1, lambda k: pl.semaphore_signal(
        barrier, inc=1, device_id=(shard_peer(k), col), device_id_type=MESH))
    greeted = count - 1
    if with_sum:
        each(columns - 1, lambda k: pl.semaphore_signal(
            barrier, inc=1, device_id=(me, tensor_peer(k)), device_id_type=MESH))
        greeted += columns - 1
    pl.semaphore_wait(barrier, greeted)

    def small(k):
        peer = shard_peer(k)
        return pltpu.make_async_remote_copy(
            part_ref, shard_parts.at[me], small_send.at[peer], small_recv.at[me],
            device_id=(peer, col), device_id_type=MESH)

    def small_in(k):
        peer = shard_peer(k)
        return pltpu.make_async_remote_copy(
            part_ref, shard_parts.at[peer], small_send.at[peer], small_recv.at[peer],
            device_id=(peer, col), device_id_type=MESH)

    def tens(k):
        peer = tensor_peer(k)
        return pltpu.make_async_remote_copy(
            mid_part, tensor_parts.at[col], tens_send.at[peer], tens_recv.at[col],
            device_id=(me, peer), device_id_type=MESH)

    def tens_in(k):
        peer = tensor_peer(k)
        return pltpu.make_async_remote_copy(
            mid_part, tensor_parts.at[peer], tens_send.at[peer], tens_recv.at[peer],
            device_id=(me, peer), device_id_type=MESH)

    def big(k):
        peer = shard_peer(k)
        return pltpu.make_async_remote_copy(
            out_ref.at[peer, direct], in_ref.at[me, direct], send_sem.at[peer], recv_sem.at[me],
            device_id=(peer, col), device_id_type=MESH)

    def big_in(k):
        peer = shard_peer(k)
        return pltpu.make_async_remote_copy(
            out_ref.at[peer, direct], in_ref.at[peer, direct], send_sem.at[peer], recv_sem.at[peer],
            device_id=(peer, col), device_id_type=MESH)

    def gather(number, chosen, d):
        unit = flipped(me, chosen)
        source = in_ref.at[unit, beyond] if chosen else spare_in
        return pltpu.make_async_remote_copy(
            source, in_ref.at[unit, beyond], spare_send.at[number], spare_recv.at[number],
            device_id=(flipped(me, (d,)), col), device_id_type=MESH)

    def gather_in(number, chosen, d):
        unit = flipped(me, chosen + (d,))
        return pltpu.make_async_remote_copy(
            spare_in, in_ref.at[unit, beyond], spare_send.at[number], spare_recv.at[number],
            device_id=(flipped(me, (d,)), col), device_id_type=MESH)

    def scatter(number, chosen, d):
        return pltpu.make_async_remote_copy(
            held.at[flipped(me, chosen + (d,))], landed.at[number],
            spare_send.at[number], spare_recv.at[number],
            device_id=(flipped(me, (d,)), col), device_id_type=MESH)

    steps = []
    if spare_in is not None:
        for at in range(len(distances)):
            d = distances[-1 - at]
            steps.append((d, subsets(distances[len(distances) - at:])))
    if spare_out is not None:
        for at, d in enumerate(distances):
            steps.append((d, subsets(distances[at + 1:])))
    number = 0
    numbered = []
    for d, chosen in steps:
        numbered.append([(number + i, c, d) for i, c in enumerate(chosen)])
        number += len(chosen)

    def spare_start(step):
        for one in step:
            (gather if spare_in is not None else scatter)(*one).start()

    def spare_finish(step):
        for one in step:
            if spare_in is not None:
                gather_in(*one).wait()
            else:
                scatter(*one).wait()
                mine = flipped(me, one[1])
                added = held[mine].astype(jnp.float32) + landed[one[0]].astype(jnp.float32)
                held[mine] = added.astype(held.dtype)

    if with_sum:
        each(count - 1, lambda k: small(k).start())
    if with_spare:
        if not with_sum:
            keep_own.wait()
        spare_start(numbered[0])
    def sum_shard():
        each(count - 1, lambda k: small_in(k).wait())
        mid_part[...] = part_ref[...]

        def add_shard(k):
            mid_part[...] += shard_parts[shard_peer(k)]
        each(count - 1, add_shard)
        each(columns - 1, lambda k: tens(k).start())

    stages = max(len(numbered), 1)
    share = (count - 1) // stages
    each(share, lambda k: big(k).start())
    for at in range(1, stages):
        spare_finish(numbered[at - 1])
        spare_start(numbered[at])
        if with_sum and at == 1:
            sum_shard()
        more = share if at + 1 < stages else count - 1 - at * share
        each(more, lambda k, at=at: big(k + at * share).start())
    if with_spare:
        spare_finish(numbered[-1])
        if with_sum:
            keep_own.wait()
        else:
            spare_out[...] = held[me]
    if with_sum:
        if stages == 1:
            sum_shard()
        each(columns - 1, lambda k: tens_in(k).wait())
        total_ref[...] = mid_part[...]

        def add_tensor(k):
            total_ref[...] += tensor_parts[tensor_peer(k)]
        each(columns - 1, add_tensor)
    each(count - 1, lambda k: big_in(k).wait())
    own.wait()


def exchange(blocks, part, collective_id, mesh_sizes, spare=None):
    count, columns = mesh_sizes
    with_sum = part is not None
    any_spec = pl.BlockSpec(memory_space=pl.ANY)
    vmem_spec = pl.BlockSpec(memory_space=pltpu.VMEM)
    out_shape = [jax.ShapeDtypeStruct(blocks.shape, blocks.dtype)]
    scratch = [
        pltpu.SemaphoreType.DMA(()),
        pltpu.SemaphoreType.DMA((count,)),
        pltpu.SemaphoreType.DMA((count,)),
    ]
    operands = [blocks]
    in_specs = [any_spec]
    out_specs = [any_spec]
    if spare is not None and with_sum:
        operands.append(spare)
        in_specs.append(any_spec)
    if spare is not None and not with_sum:
        out_shape.append(jax.ShapeDtypeStruct(spare.shape, spare.dtype))
        out_specs.append(vmem_spec)
    if with_sum:
        out_shape.append(jax.ShapeDtypeStruct(part.shape, part.dtype))
        out_specs.append(vmem_spec)
        in_specs.append(vmem_spec)
        operands.append(part)
        scratch = [
            pltpu.VMEM((count,) + part.shape, part.dtype),
            pltpu.VMEM(part.shape, part.dtype),
            pltpu.VMEM((columns,) + part.shape, part.dtype),
        ] + scratch + [
            pltpu.SemaphoreType.DMA((count,)),
            pltpu.SemaphoreType.DMA((count,)),
            pltpu.SemaphoreType.DMA((columns,)),
            pltpu.SemaphoreType.DMA((columns,)),
        ]
    if spare is not None:
        scratch = scratch + [
            pltpu.SemaphoreType.DMA(()),
            pltpu.SemaphoreType.DMA((count,)),
            pltpu.SemaphoreType.DMA((count,)),
        ]
        if not with_sum:
            scratch = scratch + [
                pltpu.VMEM((count,) + spare.shape, spare.dtype),
                pltpu.VMEM((count,) + spare.shape, spare.dtype),
            ]
    spare_rows = 0 if spare is None else spare.shape[0]
    return pl.pallas_call(
        functools.partial(exchange_kernel, with_sum, spare_rows),
        out_shape=out_shape,
        in_specs=in_specs,
        out_specs=out_specs,
        scratch_shapes=scratch,
        compiler_params=pltpu.CompilerParams(
            collective_id=collective_id, has_side_effects=True
        ),
    )(*operands)


def adam_update(gradient, clip_scale, limit, weight_old, first_old, second_old, average_old):
    lane = lax.broadcasted_iota(jnp.int32, gradient.shape, 1)
    live = lane < limit
    keep = lane >= jnp.where(limit < 0, gradient.shape[1], 0)
    clipped = gradient * clip_scale
    first_new = BETA_ONE * first_old + (1.0 - BETA_ONE) * clipped
    second_new = BETA_TWO * second_old + (1.0 - BETA_TWO) * clipped * clipped
    update = (first_new * (1.0 / (1.0 - BETA_ONE**STEP))) / (
        jnp.sqrt(second_new * (1.0 / (1.0 - BETA_TWO**STEP))) + ADAM_EPS
    )
    weight_new = weight_old - LEARN_RATE * (update + WEIGHT_DECAY * weight_old)
    average_new = AVERAGE_DECAY * average_old + (1.0 - AVERAGE_DECAY) * weight_new
    pairs = ((weight_new, weight_old), (first_new, first_old), (second_new, second_old),
             (average_new, average_old))
    return [jnp.where(keep, jnp.where(live, new, old), 0.0) for new, old in pairs]


def picker(rows, columns, shift=0):
    row = lax.broadcasted_iota(jnp.int32, (rows, columns), 0)
    column = lax.broadcasted_iota(jnp.int32, (rows, columns), 1)
    return (row + shift == column).astype(jnp.bfloat16)


def turned(pick, block):
    return lax.dot_general(
        pick, block, (((1,), (1,)), ((), ())), preferred_element_type=jnp.float32
    )


def adam_kernel(max_norm, part_rows, limit_ref, total_ref, grad_ref, *refs):
    old_refs, weight_out, new_refs = refs[:4], refs[4], refs[5:]
    per_step, columns, slab_rows = new_refs[0].shape
    total = total_ref[0:1, :]
    clip_scale = jnp.minimum(1.0, max_norm / (jnp.sqrt(total) + 1e-06))

    def advance(slot, window, gradient):
        limit = limit_ref[pl.program_id(0) * per_step + slot]
        results = adam_update(
            gradient, clip_scale, limit, *[ref[slot, window, :] for ref in old_refs]
        )
        for ref, value in zip(new_refs, results):
            ref[slot, window, :] = value
        return results[0].astype(jnp.bfloat16)

    eye = picker(slab_rows, slab_rows)
    if part_rows is None:
        for slot in range(per_step):
            weight = advance(slot, pl.ds(0, columns),
                             turned(picker(columns, columns), grad_ref[slot]))
            weight_out[slot] = turned(eye, weight).astype(jnp.bfloat16)
        return

    rest = columns - LANES
    share = rest // 3

    def packed(index):
        rows = pl.ds(PLACES[index] * part_rows, part_rows)
        return grad_ref[:, rows, :].reshape(slab_rows, LANES)

    def send(index, weight):
        rows = pl.ds(PLACES[index] * part_rows, part_rows)
        block = turned(eye, weight).astype(jnp.bfloat16)
        weight_out[:, rows, :] = block.reshape(-1, part_rows, LANES)

    main_pick = picker(LANES, LANES)
    rest_pick = picker(rest, LANES)
    share_pick = picker(share, LANES, rest)
    rests = []
    for slot in range(4):
        send(slot, advance(slot, pl.ds(0, LANES), turned(main_pick, packed(slot))))
        if slot < 3:
            gradient = turned(rest_pick, packed(4 + slot))
        else:
            gradient = jnp.concatenate(
                [turned(share_pick, packed(4 + k)) for k in range(3)], axis=0
            )
        rests.append(advance(slot, pl.ds(LANES, rest), gradient))
    for k in range(3):
        piece = rests[3][k * share:(k + 1) * share]
        send(4 + k, jnp.concatenate([rests[k], piece], axis=0))


def adam(limits, total, arrived, master, moment1, moment2, average, max_norm, part_rows):
    capacity, columns, slab_rows = master.shape
    per_step = 1 if part_rows is None else 4
    state = pl.BlockSpec((per_step, columns, slab_rows), lambda s, _: (s, 0, 0))
    if part_rows is None:
        rows = pl.BlockSpec((per_step, slab_rows, columns), lambda s, _: (s, 0, 0))
    else:
        rows = pl.BlockSpec(
            (slab_rows // part_rows, 7 * part_rows, LANES), lambda s, _: (0, s, 0)
        )
    whole = pl.BlockSpec(total.shape, lambda s, _: (0, 0))
    return pl.pallas_call(
        functools.partial(adam_kernel, max_norm, part_rows),
        grid_spec=pltpu.PrefetchScalarGridSpec(
            num_scalar_prefetch=1,
            grid=(capacity // per_step,),
            in_specs=[whole, rows, state, state, state, state],
            out_specs=[rows, state, state, state, state],
        ),
        out_shape=[jax.ShapeDtypeStruct(arrived.shape, jnp.bfloat16)]
        + [jax.ShapeDtypeStruct(master.shape, jnp.float32)] * 4,
        compiler_params=pltpu.CompilerParams(vmem_limit_bytes=60 << 20),
    )(limits, total, arrived, master, moment1, moment2, average)


GROUP = 4
TILES = 7


def slot_table(owner, owner_count):
    slab_count = owner.shape[1]
    wide = (owner_count, slab_count)
    hit = owner == lax.broadcasted_iota(jnp.int32, wide, 0)
    earlier = lax.broadcasted_iota(jnp.int32, (slab_count, slab_count), 0) < (
        lax.broadcasted_iota(jnp.int32, (slab_count, slab_count), 1)
    )
    ranks = jnp.dot(
        hit.astype(jnp.bfloat16), earlier.astype(jnp.bfloat16), preferred_element_type=jnp.float32
    )
    rank = jnp.sum(jnp.where(hit, ranks, 0.0), axis=0, keepdims=True).astype(jnp.int32)
    at_slot = rank == lax.broadcasted_iota(jnp.int32, (LANES, slab_count), 0)
    number = lax.broadcasted_iota(jnp.int32, wide, 1) + 1
    marked = lax.dot_general(
        jnp.where(hit, number, 0).astype(jnp.float32).astype(jnp.bfloat16),
        at_slot.astype(jnp.bfloat16),
        (((1,), (1,)), ((), ())), preferred_element_type=jnp.float32,
    )
    return marked.astype(jnp.int32) - 1


def step_kernel(max_norm, owner_hbm, counts_hbm, grad_hbm, *refs):
    old_hbm, refs = refs[:4], refs[4:]
    returned, spare_out, states, slab_ref, refs = refs[0], refs[1], refs[2:6], refs[6], refs[7:]
    owner_ref, counts_ref, owner_sem, counts_sem, refs = refs[:4] + (refs[4:],)
    owner_load = pltpu.make_async_copy(owner_hbm, owner_ref, owner_sem)
    owner_load.start()
    counts_load = pltpu.make_async_copy(counts_hbm, counts_ref, counts_sem)
    counts_load.start()
    grad_ref, table_ref, packed_ref, part_ref, refs = refs[:4] + (refs[4:],)
    arrived, weights, shard_parts, mid_part, tensor_parts, held, landed, refs = refs[:7] + (refs[7:],)
    (grad_sem, table_sem, state_sem, own_sem, back_sem, small_send, small_recv, tens_send, tens_recv,
     grad_send, grad_recv, weight_send, weight_recv, gather_send, gather_recv,
     scatter_send, scatter_recv) = refs
    count = lax.axis_size("shard")
    columns = lax.axis_size("tensor")
    me = lax.axis_index("shard")
    col = lax.axis_index("tensor")
    capacity, width, slab_rows = states[0].shape
    part_rows = slab_rows // count
    groups = capacity // GROUP
    group_rows = TILES * part_rows
    spare_rows = spare_out.shape[0]
    slab_count = grad_ref.shape[0]
    emb = counts_ref.shape[0]
    layer_slabs = slab_count - emb
    rest = width - LANES
    share = rest // 3
    direct_rows = packed_ref.shape[1] - spare_rows
    last_rows = direct_rows - (groups - 1) * group_rows
    direct = pl.ds(0, direct_rows)
    beyond = pl.ds(direct_rows, spare_rows)
    last = groups - 1

    def each(total, body):
        def step(k, carry):
            body(k)
            return carry
        lax.fori_loop(0, total, step, 0)

    def shard_peer(k):
        return lax.rem(me + peer_of(k, count), count)

    def tensor_peer(k):
        return lax.rem(col + k + 1, columns)

    fetch = pltpu.make_async_copy(grad_hbm, grad_ref, grad_sem)
    fetch.start()
    barrier = pltpu.get_barrier_semaphore()
    each(count - 1, lambda k: pl.semaphore_signal(
        barrier, inc=1, device_id=(shard_peer(k), col), device_id_type=MESH))
    each(columns - 1, lambda k: pl.semaphore_signal(
        barrier, inc=1, device_id=(me, tensor_peer(k)), device_id_type=MESH))
    owner_load.wait()
    table_ref[...] = slot_table(owner_ref[...], count)
    tabled = pltpu.make_async_copy(table_ref, slab_ref, table_sem)
    tabled.start()
    counts_load.wait()
    tabled.wait()
    fetch.wait()

    def pack(target, unit, holder, group, tiles, first):
        for j in range(GROUP):
            slab = jnp.clip(slab_ref[holder, group * GROUP + j], 0, slab_count - 1)

            def rows_of(index):
                start = (PLACES[index] - first) * part_rows
                if first == 0:
                    start = group * group_rows + start
                return pl.ds(start, part_rows)
            if PLACES[j] in tiles:
                target[unit, rows_of(j), :] = grad_ref[slab, :, 0:LANES]
            if j < 3:
                if PLACES[4 + j] in tiles:
                    target[unit, rows_of(4 + j), 0:rest] = grad_ref[slab, :, LANES:width]
            else:
                for k in range(3):
                    if PLACES[4 + k] in tiles:
                        begin = LANES + k * share
                        target[unit, rows_of(4 + k), rest:LANES] = (
                            grad_ref[slab, :, begin:begin + share]
                        )

    def pack_group(group):
        tiles = range(TILES) if group < last else range(last_rows // part_rows)
        each(count, lambda p: pack(packed_ref, p, p, group, tiles, 0))

    def small(k, sender):
        peer = shard_peer(k)
        slot = me if sender else peer
        return pltpu.make_async_remote_copy(
            part_ref, shard_parts.at[slot], small_send.at[peer], small_recv.at[slot],
            device_id=(peer, col), device_id_type=MESH)

    def tens(k, sender):
        peer = tensor_peer(k)
        slot = col if sender else peer
        return pltpu.make_async_remote_copy(
            mid_part, tensor_parts.at[slot], tens_send.at[peer], tens_recv.at[slot],
            device_id=(me, peer), device_id_type=MESH)

    def block(source, target, send, recv, k, group, rows, sender):
        peer = shard_peer(k)
        slot = me if sender else peer
        window = pl.ds(pl.multiple_of(group * group_rows, part_rows), rows)
        return pltpu.make_async_remote_copy(
            source.at[peer, window], target.at[slot, window],
            send.at[group, peer], recv.at[group, slot],
            device_id=(peer, col), device_id_type=MESH)

    def grad_block(k, group, rows, sender):
        return block(packed_ref, arrived, grad_send, grad_recv, k, group, rows, sender)

    def weight_block(k, group, rows, sender):
        return block(weights, returned, weight_send, weight_recv, k, group, rows, sender)

    distances = []
    while 2 ** len(distances) < count:
        distances.append(2 ** len(distances))

    def numbered(pairs):
        found, number = [], 0
        for d, chosen in pairs:
            found.append([(number + i, c, d) for i, c in enumerate(chosen)])
            number += len(chosen)
        return found
    gather_steps = numbered([
        (distances[-1 - at], subsets(distances[len(distances) - at:]))
        for at in range(len(distances))
    ])
    scatter_steps = numbered([
        (d, subsets(distances[at + 1:])) for at, d in enumerate(distances)
    ])

    def gather(number, chosen, d, sender):
        unit = flipped(me, chosen if sender else chosen + (d,))
        return pltpu.make_async_remote_copy(
            arrived.at[unit, beyond], arrived.at[unit, beyond], gather_send.at[number], gather_recv.at[number],
            device_id=(flipped(me, (d,)), col), device_id_type=MESH)

    def scatter(number, chosen, d):
        return pltpu.make_async_remote_copy(
            held.at[flipped(me, chosen + (d,))], landed.at[number],
            scatter_send.at[number], scatter_recv.at[number],
            device_id=(flipped(me, (d,)), col), device_id_type=MESH)

    def gather_start(at):
        for one in gather_steps[at]:
            gather(*one, True).start()

    def gather_finish(at):
        for one in gather_steps[at]:
            gather(*one, True).wait_send()
            gather(*one, False).wait_recv()

    def scatter_start(at):
        for one in scatter_steps[at]:
            scatter(*one).start()

    def scatter_finish(at):
        for one in scatter_steps[at]:
            scatter(*one).wait()
            mine = flipped(me, one[1])
            added = held[mine].astype(jnp.float32) + landed[one[0]].astype(jnp.float32)
            held[mine] = added.astype(held.dtype)

    pack_group(0)
    pl.semaphore_wait(barrier, count + columns - 2)
    each(count - 1, lambda k: grad_block(k, 0, group_rows, True).start())

    loads = [pltpu.make_async_copy(old, new, state_sem.at[i])
             for i, (old, new) in enumerate(zip(old_hbm, states))]
    for load in loads:
        load.start()

    fullest = 0
    for o in range(1, count):
        fullest = jnp.where(slab_ref[o, capacity - SPARE_SLOTS] >= 0, o, fullest)
    spare_tiles = range(last_rows // part_rows, TILES)
    pack(held, 0, fullest, last, spare_tiles, last_rows // part_rows)
    arrived[me, beyond, :] = held[0]
    gather_start(0)

    def squares(i, carry):
        values = grad_ref[i].astype(jnp.float32)
        return carry + values * values
    acc = lax.fori_loop(
        0, layer_slabs, squares, jnp.zeros((part_rows, width), jnp.float32), unroll=10
    )
    row = lax.broadcasted_iota(jnp.int32, (part_rows, width), 0) + me * part_rows
    for e in range(emb):
        values = grad_ref[layer_slabs + e].astype(jnp.float32)
        acc += jnp.where(row < counts_ref[e], values * values, 0.0)
    part_ref[...] = jnp.broadcast_to(jnp.sum(acc, keepdims=True), part_ref.shape)
    each(count - 1, lambda k: small(k, True).start())

    for g in (1, last, *range(2, last)):
        pack_group(g)
        rows = group_rows if g < last else last_rows
        each(count - 1, lambda k, g=g, rows=rows: grad_block(k, g, rows, True).start())
    own = pltpu.make_async_copy(packed_ref.at[me, direct], arrived.at[me, direct], own_sem)
    own.start()

    def add_shard(k):
        small(k, False).wait()
        mid_part[...] += shard_parts[shard_peer(k)]

    mid_part[...] = part_ref[...]
    each(count - 1, add_shard)
    each(columns - 1, lambda k: tens(k, True).start())
    gather_finish(0)
    gather_start(1)
    own.wait()
    for load in loads:
        load.wait()
    total = mid_part[0:1, :]
    each(columns - 1, lambda k: tens(k, False).wait())
    for k in range(columns - 1):
        total = total + tensor_parts[tensor_peer(k), 0:1, :]
    clip_scale = jnp.minimum(1.0, max_norm / (jnp.sqrt(total) + 1e-06))
    gather_finish(1)
    gather_start(2)

    eye = picker(slab_rows, slab_rows)

    def compute(group):
        base = group * group_rows

        def rows_of(index):
            return pl.ds(pl.multiple_of(base + PLACES[index] * part_rows, part_rows), part_rows)

        def advance(slot, window, gradient):
            place = group * GROUP + slot
            slab = slab_ref[me, place]
            live = counts_ref[jnp.clip(slab - layer_slabs, 0, emb - 1)]
            limit = jnp.where(slab < 0, -1, jnp.where(slab < layer_slabs, slab_rows, live))
            results = adam_update(
                gradient, clip_scale, limit, *[ref[place, window, :] for ref in states]
            )
            for ref, value in zip(states, results):
                ref[place, window, :] = value
            return results[0].astype(jnp.bfloat16)

        def packed(index):
            return arrived[:, rows_of(index), :].reshape(slab_rows, LANES)

        def send(index, weight):
            done = turned(eye, weight).astype(jnp.bfloat16)
            weights[:, rows_of(index), :] = done.reshape(count, part_rows, LANES)

        rest_pick = picker(rest, LANES)
        share_pick = picker(share, LANES, rest)
        rests = []
        for slot in range(GROUP):
            send(slot, advance(slot, pl.ds(0, LANES), turned(eye, packed(slot))))
            if slot < 3:
                gradient = turned(rest_pick, packed(4 + slot))
            else:
                gradient = jnp.concatenate(
                    [turned(share_pick, packed(4 + k)) for k in range(3)], axis=0
                )
            rests.append(advance(slot, pl.ds(LANES, rest), gradient))
        for k in range(3):
            piece = rests[3][k * share:(k + 1) * share]
            send(4 + k, jnp.concatenate([rests[k], piece], axis=0))

    back = pltpu.make_async_copy(weights.at[me, direct], returned.at[me, direct], back_sem)
    early = min(2, last)

    def turn(t, carry):
        at_last = t == early
        group = jnp.where(at_last, last, jnp.where(t > early, t - 1, t))

        @pl.when(jnp.logical_not(at_last))
        def _():
            each(count - 1, lambda k: grad_block(k, group, group_rows, False).wait())

        @pl.when(at_last)
        def _():
            each(count - 1, lambda k: grad_block(k, last, last_rows, False).wait())
            gather_finish(2)

        compute(group)

        @pl.when(jnp.logical_not(at_last))
        def _():
            each(count - 1, lambda k: weight_block(k, group, group_rows, True).start())

        @pl.when(at_last)
        def _():
            held[...] = weights[:, beyond, :]
            scatter_start(0)
            each(count - 1, lambda k: weight_block(k, last, last_rows, True).start())

        @pl.when(t == early + 1)
        def _():
            scatter_finish(0)
            scatter_start(1)

        @pl.when(t == early + 2)
        def _():
            scatter_finish(1)
            scatter_start(2)
        return carry

    lax.fori_loop(0, groups, turn, 0)
    back.start()
    scatter_finish(2)
    spare_out[...] = held[me]
    for g in range(groups):
        rows = group_rows if g < last else last_rows
        each(count - 1, lambda k, g=g, rows=rows: weight_block(k, g, rows, False).wait())
    back.wait()


def step(owner, counts, grad, states, max_norm, mesh_sizes):
    count, columns = mesh_sizes
    capacity, width, slab_rows = states[0].shape
    part_rows = grad.shape[1]
    groups = capacity // GROUP
    packed = (count, groups * TILES * part_rows, LANES)
    spare = (SPARE_BLOCKS * part_rows, LANES)
    vmem = pl.BlockSpec(memory_space=pltpu.VMEM)
    smem = pl.BlockSpec(memory_space=pltpu.SMEM)
    hbm = pl.BlockSpec(memory_space=pltpu.HBM)
    dma = pltpu.SemaphoreType.DMA
    return pl.pallas_call(
        functools.partial(step_kernel, max_norm),
        in_specs=[hbm] * 7,
        out_specs=[vmem] * 6 + [smem],
        out_shape=[pltpu.VMEM(packed, grad.dtype), pltpu.VMEM(spare, grad.dtype)]
        + [pltpu.VMEM(s.shape, s.dtype) for s in states]
        + [jax.ShapeDtypeStruct((count, LANES), jnp.int32)],
        scratch_shapes=[
            pltpu.VMEM(owner.shape, owner.dtype),
            pltpu.SMEM(counts.shape, counts.dtype),
            dma(()), dma(()),
            pltpu.VMEM(grad.shape, grad.dtype),
            pltpu.VMEM((count, LANES), jnp.int32),
            pltpu.VMEM(packed, grad.dtype),
            pltpu.VMEM((8, LANES), jnp.float32),
            pltpu.VMEM(packed, grad.dtype),
            pltpu.VMEM(packed, grad.dtype),
            pltpu.VMEM((count, 8, LANES), jnp.float32),
            pltpu.VMEM((8, LANES), jnp.float32),
            pltpu.VMEM((columns, 8, LANES), jnp.float32),
            pltpu.VMEM((count,) + spare, grad.dtype),
            pltpu.VMEM((count,) + spare, grad.dtype),
            dma(()), dma(()), dma((4,)), dma(()), dma(()),
            dma((count,)), dma((count,)), dma((columns,)), dma((columns,)),
            dma((groups, count)), dma((groups, count)), dma((groups, count)), dma((groups, count)),
            dma((count,)), dma((count,)), dma((count,)), dma((count,)),
        ],
        compiler_params=pltpu.CompilerParams(
            collective_id=2, has_side_effects=True, vmem_limit_bytes=40 << 20
        ),
    )(owner, counts, grad, *states)


def unpack_kernel(capacity, source_ref, packed_ref, spare_ref, *refs):
    fresh, weight_hbm, kept, weight_ref, weight_sem, kept_sem = (
        refs[:4], refs[4], refs[5:9], refs[9], refs[10], refs[11]
    )
    stores = [pltpu.make_async_copy(new, out, kept_sem.at[i])
              for i, (new, out) in enumerate(zip(fresh, kept))]
    for store in stores:
        store.start()
    slab_count, part_rows, columns = weight_hbm.shape
    rest = columns - LANES
    share = rest // 3
    groups = capacity // 4

    def unpack(t, carry):
        p = t // groups
        g = t % groups
        base = g * (7 * part_rows)

        def piece(index):
            rows = pl.ds(pl.multiple_of(base + PLACES[index] * part_rows, part_rows), part_rows)
            return packed_ref[p, rows, :]
        blocks = [piece(index) for index in range(7)]
        for j in range(4):
            slab = source_ref[p, g * 4 + j]
            slab = jnp.where(slab < 0, slab_count, slab)
            weight_ref[slab, :, 0:LANES] = blocks[j]
            if j < 3:
                weight_ref[slab, :, LANES:columns] = blocks[4 + j][:, 0:rest]
            else:
                weight_ref[slab, :, LANES:columns] = jnp.concatenate(
                    [blocks[4 + k][:, rest:LANES] for k in range(3)], axis=1
                )
        return carry
    lax.fori_loop(0, packed_ref.shape[0] * groups, unpack, 0, unroll=2)
    fullest = 0
    for p in range(1, packed_ref.shape[0]):
        first_spare = source_ref[p, capacity - SPARE_SLOTS]
        fullest = jnp.where(first_spare >= 0, p, fullest)
    last = (groups - 1) * (7 * part_rows)
    spare = [None, None] + [
        spare_ref[pl.ds(k * part_rows, part_rows), :] for k in range(SPARE_BLOCKS)
    ]
    spare[1] = packed_ref[fullest, pl.ds(last + part_rows, part_rows), :]
    for j in range(1, 4):
        slab = source_ref[fullest, capacity - 4 + j]
        slab = jnp.where(slab < 0, slab_count, slab)
        weight_ref[slab, :, 0:LANES] = spare[PLACES[j]]
        if j < 3:
            weight_ref[slab, :, LANES:columns] = spare[PLACES[4 + j]][:, 0:rest]
        else:
            weight_ref[slab, :, LANES:columns] = jnp.concatenate(
                [spare[PLACES[4 + k]][:, rest:LANES] for k in range(3)], axis=1
            )
    store = pltpu.make_async_copy(weight_ref.at[pl.ds(0, slab_count)], weight_hbm, weight_sem)
    store.start()
    store.wait()
    for store in stores:
        store.wait()


def unpack(source, packed, spare, states, weight_shape, capacity):
    slab_count, part_rows, columns = weight_shape
    vmem = pl.BlockSpec(memory_space=pltpu.VMEM)
    hbm = pl.BlockSpec(memory_space=pltpu.HBM)
    return pl.pallas_call(
        functools.partial(unpack_kernel, capacity),
        in_specs=[pl.BlockSpec(memory_space=pltpu.SMEM), vmem, vmem] + [vmem] * 4,
        out_specs=[hbm] * 5,
        out_shape=[jax.ShapeDtypeStruct(weight_shape, packed.dtype)]
        + [jax.ShapeDtypeStruct(s.shape, s.dtype) for s in states],
        scratch_shapes=[
            pltpu.VMEM((slab_count + 1, part_rows, columns), packed.dtype),
            pltpu.SemaphoreType.DMA(()),
            pltpu.SemaphoreType.DMA((4,)),
        ],
        compiler_params=pltpu.CompilerParams(vmem_limit_bytes=40 << 20),
    )(source, packed, spare, *states)


def per_device(mesh_sizes, grad, owner, counts, master, moment1, moment2, average):
    owner_count = mesh_sizes[0]
    slab_count, part_rows, columns = grad.shape
    capacity = master.shape[0]
    slab_rows = part_rows * owner_count
    max_norm = 0.5 * math.sqrt(slab_count * slab_rows * D)
    layer_slabs = slab_count - counts.shape[0]
    self_index = lax.axis_index("shard")
    states = (master, moment1, moment2, average)

    if part_rows % 16 == 0 and capacity % 4 == 0 and (columns - LANES) * 4 == 3 * LANES and (
        owner_count & (owner_count - 1) == 0 and slab_count <= 256 and capacity <= LANES
    ):
        inputs = (owner.reshape(1, -1), counts, grad) + states
        owner, counts, grad, *states = [
            pltpu.with_memory_space_constraint(x, pltpu.HBM) for x in inputs
        ]
        returned, spare, *states, source = step(
            owner, counts, grad, states, max_norm, mesh_sizes
        )
        return tuple(unpack(source, returned, spare, states, grad.shape, capacity))

    full_counts = jnp.concatenate([jnp.full((layer_slabs,), slab_rows, jnp.int32), counts])
    row_index = self_index * part_rows + jnp.arange(part_rows, dtype=jnp.int32)
    train_live = row_index[None, :] < full_counts[:, None]
    values = grad.astype(jnp.float32)
    part = jnp.sum(jnp.where(train_live[:, :, None], values * values, 0.0))
    part = jnp.broadcast_to(part, (8, LANES))

    place, marked = slot_tables(owner, owner_count, capacity)
    source = jnp.maximum(marked - 1, 0)
    own_marked = lax.dynamic_slice_in_dim(marked, self_index * capacity, capacity)
    own_live = jnp.take(full_counts, jnp.maximum(own_marked - 1, 0), mode="clip")
    limits = jnp.where(own_marked > 0, own_live, -1)

    outgoing = jnp.take(grad, source, axis=0, mode="clip")
    outgoing = outgoing.reshape(owner_count, capacity * part_rows, columns)
    arrived, total = exchange(outgoing, part, 0, mesh_sizes)
    arrived = arrived.reshape(owner_count, capacity, part_rows, columns)
    arrived = arrived.transpose(1, 0, 2, 3).reshape(capacity, slab_rows, columns)
    weights, *new_states = adam(limits, total, arrived, *states, max_norm, None)
    weights = weights.reshape(capacity, owner_count, part_rows, columns)
    weights = weights.transpose(1, 0, 2, 3)
    weights = weights.reshape(owner_count, capacity * part_rows, columns)
    (returned,) = exchange(weights, None, 1, mesh_sizes)
    returned = returned.reshape(owner_count * capacity, part_rows, columns)
    new_weight = jnp.take(returned, place, axis=0, mode="clip")
    return (new_weight, *new_states)


def solution(mesh):
    sizes = (mesh.shape["shard"], mesh.shape["tensor"])
    return jax.shard_map(
        functools.partial(per_device, sizes),
        mesh=mesh,
        in_specs=(
            P(None, "shard", "tensor"),
            P(),
            P(),
            P("shard", "tensor", None),
            P("shard", "tensor", None),
            P("shard", "tensor", None),
            P("shard", "tensor", None),
        ),
        out_specs=(
            P(None, "shard", "tensor"),
            P("shard", "tensor", None),
            P("shard", "tensor", None),
            P("shard", "tensor", None),
            P("shard", "tensor", None),
        ),
        check_vma=False,
    )
```

```python
import functools
import math

import jax
import jax.numpy as jnp
from jax import lax
from jax.experimental import pallas as pl
from jax.experimental.pallas import tpu as pltpu
from jax.sharding import PartitionSpec as P

D = 896
STEP = 20


BETA_ONE = 0.9
BETA_TWO = 0.95
ADAM_EPS = 1e-08
LEARN_RATE = 0.02
WEIGHT_DECAY = 0.1
AVERAGE_DECAY = 0.99

LANES = 128
PLACES = (0, 2, 3, 4, 1, 5, 6)
SPARE_SLOTS = 3
SPARE_BLOCKS = 5
MESH = pl.DeviceIdType.MESH


def slot_tables(owner, owner_count, capacity):
    slab_count = owner.shape[0]
    owner_ids = jnp.arange(owner_count, dtype=jnp.int32)
    slabs = jnp.arange(slab_count, dtype=jnp.int32)
    before = (owner[:, None] == owner[None, :]) & (slabs[None, :] < slabs[:, None])
    slot_rank = jnp.sum(before.astype(jnp.int32), axis=1)
    place = owner * capacity + slot_rank
    slot_ids = jnp.arange(owner_count * capacity, dtype=jnp.int32)
    matched = place[None, :] == slot_ids[:, None]
    marked = jnp.sum(jnp.where(matched, slabs[None, :] + 1, 0), axis=1)
    return (place, marked)


def peer_of(step, count):
    half = count // 2
    away = (step + 1) // 2
    return jnp.where(step % 2 == 1, half - away, half + away)


def subsets(distances):
    found = [()]
    for d in distances:
        found = found + [c + (d,) for c in found]
    return found


def flipped(index, distances):
    for d in distances:
        index = index + d * (1 - 2 * lax.rem(index // d, 2))
    return index


def exchange_kernel(with_sum, with_spare, *refs):
    refs = list(refs)
    out_ref = refs.pop(0)
    spare_in = refs.pop(0) if with_spare and with_sum else None
    part_ref = refs.pop(0) if with_sum else None
    in_ref = refs.pop(0)
    spare_out = refs.pop(0) if with_spare and not with_sum else None
    total_ref = refs.pop(0) if with_sum else None
    if with_sum:
        shard_parts, mid_part, tensor_parts = refs[:3]
        refs = refs[3:]
    local_sem, send_sem, recv_sem = refs[:3]
    refs = refs[3:]
    if with_sum:
        small_send, small_recv, tens_send, tens_recv = refs[:4]
        refs = refs[4:]
    if with_spare:
        spare_local, spare_send, spare_recv = refs[:3]
        refs = refs[3:]
        if not with_sum:
            held, landed = refs
    count = lax.axis_size("shard")
    columns = lax.axis_size("tensor")
    me = lax.axis_index("shard")
    col = lax.axis_index("tensor")

    def each(total, body):
        def step(k, carry):
            body(k)
            return carry
        lax.fori_loop(0, total, step, 0)

    def shard_peer(k):
        return lax.rem(me + peer_of(k, count), count)

    def tensor_peer(k):
        return lax.rem(col + k + 1, columns)

    rows = out_ref.shape[1]
    spare_rows = with_spare
    direct = pl.ds(0, rows - spare_rows)
    beyond = pl.ds(rows - spare_rows, spare_rows)
    distances = []
    while with_spare and 2 ** len(distances) < count:
        distances.append(2 ** len(distances))
    if spare_in is not None:
        keep_own = pltpu.make_async_copy(spare_in, in_ref.at[me, beyond], spare_local)
        keep_own.start()
    if spare_out is not None:
        keep_own = pltpu.make_async_copy(out_ref.at[:, beyond], held, spare_local)
        keep_own.start()
    own = pltpu.make_async_copy(
        out_ref.at[me, direct], in_ref.at[me, direct], local_sem
    )
    own.start()
    barrier = pltpu.get_barrier_semaphore()
    each(count - 1, lambda k: pl.semaphore_signal(
        barrier, inc=1, device_id=(shard_peer(k), col), device_id_type=MESH))
    greeted = count - 1
    if with_sum:
        each(columns - 1, lambda k: pl.semaphore_signal(
            barrier, inc=1, device_id=(me, tensor_peer(k)), device_id_type=MESH))
        greeted += columns - 1
    pl.semaphore_wait(barrier, greeted)

    def small(k):
        peer = shard_peer(k)
        return pltpu.make_async_remote_copy(
            part_ref, shard_parts.at[me], small_send.at[peer], small_recv.at[me],
            device_id=(peer, col), device_id_type=MESH)

    def small_in(k):
        peer = shard_peer(k)
        return pltpu.make_async_remote_copy(
            part_ref, shard_parts.at[peer], small_send.at[peer], small_recv.at[peer],
            device_id=(peer, col), device_id_type=MESH)

    def tens(k):
        peer = tensor_peer(k)
        return pltpu.make_async_remote_copy(
            mid_part, tensor_parts.at[col], tens_send.at[peer], tens_recv.at[col],
            device_id=(me, peer), device_id_type=MESH)

    def tens_in(k):
        peer = tensor_peer(k)
        return pltpu.make_async_remote_copy(
            mid_part, tensor_parts.at[peer], tens_send.at[peer], tens_recv.at[peer],
            device_id=(me, peer), device_id_type=MESH)

    def big(k):
        peer = shard_peer(k)
        return pltpu.make_async_remote_copy(
            out_ref.at[peer, direct], in_ref.at[me, direct], send_sem.at[peer], recv_sem.at[me],
            device_id=(peer, col), device_id_type=MESH)

    def big_in(k):
        peer = shard_peer(k)
        return pltpu.make_async_remote_copy(
            out_ref.at[peer, direct], in_ref.at[peer, direct], send_sem.at[peer], recv_sem.at[peer],
            device_id=(peer, col), device_id_type=MESH)

    def gather(number, chosen, d):
        unit = flipped(me, chosen)
        source = in_ref.at[unit, beyond] if chosen else spare_in
        return pltpu.make_async_remote_copy(
            source, in_ref.at[unit, beyond], spare_send.at[number], spare_recv.at[number],
            device_id=(flipped(me, (d,)), col), device_id_type=MESH)

    def gather_in(number, chosen, d):
        unit = flipped(me, chosen + (d,))
        return pltpu.make_async_remote_copy(
            spare_in, in_ref.at[unit, beyond], spare_send.at[number], spare_recv.at[number],
            device_id=(flipped(me, (d,)), col), device_id_type=MESH)

    def scatter(number, chosen, d):
        return pltpu.make_async_remote_copy(
            held.at[flipped(me, chosen + (d,))], landed.at[number],
            spare_send.at[number], spare_recv.at[number],
            device_id=(flipped(me, (d,)), col), device_id_type=MESH)

    steps = []
    if spare_in is not None:
        for at in range(len(distances)):
            d = distances[-1 - at]
            steps.append((d, subsets(distances[len(distances) - at:])))
    if spare_out is not None:
        for at, d in enumerate(distances):
            steps.append((d, subsets(distances[at + 1:])))
    number = 0
    numbered = []
    for d, chosen in steps:
        numbered.append([(number + i, c, d) for i, c in enumerate(chosen)])
        number += len(chosen)

    def spare_start(step):
        for one in step:
            (gather if spare_in is not None else scatter)(*one).start()

    def spare_finish(step):
        for one in step:
            if spare_in is not None:
                gather_in(*one).wait()
            else:
                scatter(*one).wait()
                mine = flipped(me, one[1])
                added = held[mine].astype(jnp.float32) + landed[one[0]].astype(jnp.float32)
                held[mine] = added.astype(held.dtype)

    if with_sum:
        each(count - 1, lambda k: small(k).start())
    if with_spare:
        if not with_sum:
            keep_own.wait()
        spare_start(numbered[0])
    def sum_shard():
        each(count - 1, lambda k: small_in(k).wait())
        mid_part[...] = part_ref[...]

        def add_shard(k):
            mid_part[...] += shard_parts[shard_peer(k)]
        each(count - 1, add_shard)
        each(columns - 1, lambda k: tens(k).start())

    stages = max(len(numbered), 1)
    share = (count - 1) // stages
    each(share, lambda k: big(k).start())
    for at in range(1, stages):
        spare_finish(numbered[at - 1])
        spare_start(numbered[at])
        if with_sum and at == 1:
            sum_shard()
        more = share if at + 1 < stages else count - 1 - at * share
        each(more, lambda k, at=at: big(k + at * share).start())
    if with_spare:
        spare_finish(numbered[-1])
        if with_sum:
            keep_own.wait()
        else:
            spare_out[...] = held[me]
    if with_sum:
        if stages == 1:
            sum_shard()
        each(columns - 1, lambda k: tens_in(k).wait())
        total_ref[...] = mid_part[...]

        def add_tensor(k):
            total_ref[...] += tensor_parts[tensor_peer(k)]
        each(columns - 1, add_tensor)
    each(count - 1, lambda k: big_in(k).wait())
    own.wait()


def exchange(blocks, part, collective_id, mesh_sizes, spare=None):
    count, columns = mesh_sizes
    with_sum = part is not None
    any_spec = pl.BlockSpec(memory_space=pl.ANY)
    vmem_spec = pl.BlockSpec(memory_space=pltpu.VMEM)
    out_shape = [jax.ShapeDtypeStruct(blocks.shape, blocks.dtype)]
    scratch = [
        pltpu.SemaphoreType.DMA(()),
        pltpu.SemaphoreType.DMA((count,)),
        pltpu.SemaphoreType.DMA((count,)),
    ]
    operands = [blocks]
    in_specs = [any_spec]
    out_specs = [any_spec]
    if spare is not None and with_sum:
        operands.append(spare)
        in_specs.append(any_spec)
    if spare is not None and not with_sum:
        out_shape.append(jax.ShapeDtypeStruct(spare.shape, spare.dtype))
        out_specs.append(vmem_spec)
    if with_sum:
        out_shape.append(jax.ShapeDtypeStruct(part.shape, part.dtype))
        out_specs.append(vmem_spec)
        in_specs.append(vmem_spec)
        operands.append(part)
        scratch = [
            pltpu.VMEM((count,) + part.shape, part.dtype),
            pltpu.VMEM(part.shape, part.dtype),
            pltpu.VMEM((columns,) + part.shape, part.dtype),
        ] + scratch + [
            pltpu.SemaphoreType.DMA((count,)),
            pltpu.SemaphoreType.DMA((count,)),
            pltpu.SemaphoreType.DMA((columns,)),
            pltpu.SemaphoreType.DMA((columns,)),
        ]
    if spare is not None:
        scratch = scratch + [
            pltpu.SemaphoreType.DMA(()),
            pltpu.SemaphoreType.DMA((count,)),
            pltpu.SemaphoreType.DMA((count,)),
        ]
        if not with_sum:
            scratch = scratch + [
                pltpu.VMEM((count,) + spare.shape, spare.dtype),
                pltpu.VMEM((count,) + spare.shape, spare.dtype),
            ]
    spare_rows = 0 if spare is None else spare.shape[0]
    return pl.pallas_call(
        functools.partial(exchange_kernel, with_sum, spare_rows),
        out_shape=out_shape,
        in_specs=in_specs,
        out_specs=out_specs,
        scratch_shapes=scratch,
        compiler_params=pltpu.CompilerParams(
            collective_id=collective_id, has_side_effects=True
        ),
    )(*operands)


def adam_update(gradient, clip_scale, limit, weight_old, first_old, second_old, average_old):
    lane = lax.broadcasted_iota(jnp.int32, gradient.shape, 1)
    live = lane < limit
    keep = lane >= jnp.where(limit < 0, gradient.shape[1], 0)
    clipped = gradient * clip_scale
    first_new = BETA_ONE * first_old + (1.0 - BETA_ONE) * clipped
    second_new = BETA_TWO * second_old + (1.0 - BETA_TWO) * clipped * clipped
    update = (first_new * (1.0 / (1.0 - BETA_ONE**STEP))) / (
        jnp.sqrt(second_new * (1.0 / (1.0 - BETA_TWO**STEP))) + ADAM_EPS
    )
    weight_new = weight_old - LEARN_RATE * (update + WEIGHT_DECAY * weight_old)
    average_new = AVERAGE_DECAY * average_old + (1.0 - AVERAGE_DECAY) * weight_new
    pairs = ((weight_new, weight_old), (first_new, first_old), (second_new, second_old),
             (average_new, average_old))
    return [jnp.where(keep, jnp.where(live, new, old), 0.0) for new, old in pairs]


def picker(rows, columns, shift=0):
    row = lax.broadcasted_iota(jnp.int32, (rows, columns), 0)
    column = lax.broadcasted_iota(jnp.int32, (rows, columns), 1)
    return (row + shift == column).astype(jnp.bfloat16)


def turned(pick, block):
    return lax.dot_general(
        pick, block, (((1,), (1,)), ((), ())), preferred_element_type=jnp.float32
    )


def adam_kernel(max_norm, part_rows, limit_ref, total_ref, grad_ref, *refs):
    old_refs, weight_out, new_refs = refs[:4], refs[4], refs[5:]
    per_step, columns, slab_rows = new_refs[0].shape
    total = total_ref[0:1, :]
    clip_scale = jnp.minimum(1.0, max_norm / (jnp.sqrt(total) + 1e-06))

    def advance(slot, window, gradient):
        limit = limit_ref[pl.program_id(0) * per_step + slot]
        results = adam_update(
            gradient, clip_scale, limit, *[ref[slot, window, :] for ref in old_refs]
        )
        for ref, value in zip(new_refs, results):
            ref[slot, window, :] = value
        return results[0].astype(jnp.bfloat16)

    eye = picker(slab_rows, slab_rows)
    if part_rows is None:
        for slot in range(per_step):
            weight = advance(slot, pl.ds(0, columns),
                             turned(picker(columns, columns), grad_ref[slot]))
            weight_out[slot] = turned(eye, weight).astype(jnp.bfloat16)
        return

    rest = columns - LANES
    share = rest // 3

    def packed(index):
        rows = pl.ds(PLACES[index] * part_rows, part_rows)
        return grad_ref[:, rows, :].reshape(slab_rows, LANES)

    def send(index, weight):
        rows = pl.ds(PLACES[index] * part_rows, part_rows)
        block = turned(eye, weight).astype(jnp.bfloat16)
        weight_out[:, rows, :] = block.reshape(-1, part_rows, LANES)

    main_pick = picker(LANES, LANES)
    rest_pick = picker(rest, LANES)
    share_pick = picker(share, LANES, rest)
    rests = []
    for slot in range(4):
        send(slot, advance(slot, pl.ds(0, LANES), turned(main_pick, packed(slot))))
        if slot < 3:
            gradient = turned(rest_pick, packed(4 + slot))
        else:
            gradient = jnp.concatenate(
                [turned(share_pick, packed(4 + k)) for k in range(3)], axis=0
            )
        rests.append(advance(slot, pl.ds(LANES, rest), gradient))
    for k in range(3):
        piece = rests[3][k * share:(k + 1) * share]
        send(4 + k, jnp.concatenate([rests[k], piece], axis=0))


def adam(limits, total, arrived, master, moment1, moment2, average, max_norm, part_rows):
    capacity, columns, slab_rows = master.shape
    per_step = 1 if part_rows is None else 4
    state = pl.BlockSpec((per_step, columns, slab_rows), lambda s, _: (s, 0, 0))
    if part_rows is None:
        rows = pl.BlockSpec((per_step, slab_rows, columns), lambda s, _: (s, 0, 0))
    else:
        rows = pl.BlockSpec(
            (slab_rows // part_rows, 7 * part_rows, LANES), lambda s, _: (0, s, 0)
        )
    whole = pl.BlockSpec(total.shape, lambda s, _: (0, 0))
    return pl.pallas_call(
        functools.partial(adam_kernel, max_norm, part_rows),
        grid_spec=pltpu.PrefetchScalarGridSpec(
            num_scalar_prefetch=1,
            grid=(capacity // per_step,),
            in_specs=[whole, rows, state, state, state, state],
            out_specs=[rows, state, state, state, state],
        ),
        out_shape=[jax.ShapeDtypeStruct(arrived.shape, jnp.bfloat16)]
        + [jax.ShapeDtypeStruct(master.shape, jnp.float32)] * 4,
        compiler_params=pltpu.CompilerParams(vmem_limit_bytes=60 << 20),
    )(limits, total, arrived, master, moment1, moment2, average)


GROUP = 4
GRAD_CUTS = (1, 3)
WEIGHT_CUTS = (1, 3)
TILES = 7


def batches(groups, cuts):
    cuts = sorted({0, groups, *[min(c, groups) for c in cuts]})
    return [list(range(a, b)) for a, b in zip(cuts, cuts[1:])]


def slot_table(owner, owner_count):
    slab_count = owner.shape[1]
    wide = (owner_count, slab_count)
    hit = owner == lax.broadcasted_iota(jnp.int32, wide, 0)
    earlier = lax.broadcasted_iota(jnp.int32, (slab_count, slab_count), 0) < (
        lax.broadcasted_iota(jnp.int32, (slab_count, slab_count), 1)
    )
    ranks = jnp.dot(
        hit.astype(jnp.bfloat16), earlier.astype(jnp.bfloat16), preferred_element_type=jnp.float32
    )
    rank = jnp.sum(jnp.where(hit, ranks, 0.0), axis=0, keepdims=True).astype(jnp.int32)
    at_slot = rank == lax.broadcasted_iota(jnp.int32, (LANES, slab_count), 0)
    number = lax.broadcasted_iota(jnp.int32, wide, 1) + 1
    marked = lax.dot_general(
        jnp.where(hit, number, 0).astype(jnp.float32).astype(jnp.bfloat16),
        at_slot.astype(jnp.bfloat16),
        (((1,), (1,)), ((), ())), preferred_element_type=jnp.float32,
    )
    return marked.astype(jnp.int32) - 1


def step_kernel(max_norm, owner_hbm, counts_hbm, grad_hbm, *refs):
    old_hbm, refs = refs[:4], refs[4:]
    returned, spare_out, states, table_ref, refs = refs[0], refs[1], refs[2:6], refs[6], refs[7:]
    slab_ref, refs = refs[0], refs[1:]
    owner_ref, counts_ref, owner_sem, counts_sem, refs = refs[:4] + (refs[4:],)
    owner_load = pltpu.make_async_copy(owner_hbm, owner_ref, owner_sem)
    owner_load.start()
    counts_load = pltpu.make_async_copy(counts_hbm, counts_ref, counts_sem)
    counts_load.start()
    grad_ref, packed_ref, part_ref, refs = refs[:3] + (refs[3:],)
    arrived, weights, shard_parts, mid_part, tensor_parts, held, landed, refs = refs[:7] + (refs[7:],)
    (grad_sem, table_sem, state_sem, own_sem, back_sem, small_send, small_recv, tens_send, tens_recv,
     grad_send, grad_recv, weight_send, weight_recv, gather_send, gather_recv,
     scatter_send, scatter_recv) = refs
    count = lax.axis_size("shard")
    columns = lax.axis_size("tensor")
    me = lax.axis_index("shard")
    col = lax.axis_index("tensor")
    capacity, width, slab_rows = states[0].shape
    part_rows = slab_rows // count
    groups = capacity // GROUP
    group_rows = TILES * part_rows
    spare_rows = spare_out.shape[0]
    slab_count = grad_ref.shape[0]
    emb = counts_ref.shape[0]
    layer_slabs = slab_count - emb
    rest = width - LANES
    share = rest // 3
    direct_rows = packed_ref.shape[1] - spare_rows
    last_rows = direct_rows - (groups - 1) * group_rows
    direct = pl.ds(0, direct_rows)
    beyond = pl.ds(direct_rows, spare_rows)
    last = groups - 1
    grad_parts = batches(groups, GRAD_CUTS)
    weight_parts = batches(groups, WEIGHT_CUTS)
    order = [g for batch in grad_parts[:-1] for g in batch] + grad_parts[-1]

    def each(total, body):
        def step(k, carry):
            body(k)
            return carry
        lax.fori_loop(0, total, step, 0)

    def shard_peer(k):
        return lax.rem(me + peer_of(k, count), count)

    def tensor_peer(k):
        return lax.rem(col + k + 1, columns)

    fetch = pltpu.make_async_copy(grad_hbm, grad_ref, grad_sem)
    fetch.start()
    barrier = pltpu.get_barrier_semaphore()
    each(count - 1, lambda k: pl.semaphore_signal(
        barrier, inc=1, device_id=(shard_peer(k), col), device_id_type=MESH))
    each(columns - 1, lambda k: pl.semaphore_signal(
        barrier, inc=1, device_id=(me, tensor_peer(k)), device_id_type=MESH))
    owner_load.wait()
    table_ref[...] = slot_table(owner_ref[...], count)
    tabled = pltpu.make_async_copy(table_ref, slab_ref, table_sem)
    tabled.start()
    counts_load.wait()
    tabled.wait()
    fetch.wait()

    def pack(target, unit, holder, group, tiles, first):
        for j in range(GROUP):
            slab = jnp.clip(slab_ref[holder, group * GROUP + j], 0, slab_count - 1)

            def rows_of(index):
                start = (PLACES[index] - first) * part_rows
                if first == 0:
                    start = group * group_rows + start
                return pl.ds(start, part_rows)
            if PLACES[j] in tiles:
                target[unit, rows_of(j), :] = grad_ref[slab, :, 0:LANES]
            if j < 3:
                if PLACES[4 + j] in tiles:
                    target[unit, rows_of(4 + j), 0:rest] = grad_ref[slab, :, LANES:width]
            else:
                for k in range(3):
                    if PLACES[4 + k] in tiles:
                        begin = LANES + k * share
                        target[unit, rows_of(4 + k), rest:LANES] = (
                            grad_ref[slab, :, begin:begin + share]
                        )

    def tiles_of(group):
        return range(TILES) if group < last else range(last_rows // part_rows)

    def pack_group(group):
        each(count, lambda p: pack(packed_ref, p, p, group, tiles_of(group), 0))

    def small(k, sender):
        peer = shard_peer(k)
        slot = me if sender else peer
        return pltpu.make_async_remote_copy(
            part_ref, shard_parts.at[slot], small_send.at[peer], small_recv.at[slot],
            device_id=(peer, col), device_id_type=MESH)

    def tens(k, sender):
        peer = tensor_peer(k)
        slot = col if sender else peer
        return pltpu.make_async_remote_copy(
            mid_part, tensor_parts.at[slot], tens_send.at[peer], tens_recv.at[slot],
            device_id=(me, peer), device_id_type=MESH)

    def block(parts, source, target, send, recv, k, number, sender):
        peer = shard_peer(k)
        slot = me if sender else peer
        first = parts[number][0] * group_rows
        end = direct_rows if number + 1 == len(parts) else parts[number + 1][0] * group_rows
        window = pl.ds(first, end - first)
        return pltpu.make_async_remote_copy(
            source.at[peer, window], target.at[slot, window],
            send.at[number, peer], recv.at[number, slot],
            device_id=(peer, col), device_id_type=MESH)

    def grad_block(k, number, sender):
        return block(grad_parts, packed_ref, arrived, grad_send, grad_recv, k, number, sender)

    def weight_block(k, number, sender):
        return block(
            weight_parts, weights, returned, weight_send, weight_recv, k, number, sender
        )

    distances = []
    while 2 ** len(distances) < count:
        distances.append(2 ** len(distances))

    def numbered(pairs):
        found, number = [], 0
        for d, chosen in pairs:
            found.append([(number + i, c, d) for i, c in enumerate(chosen)])
            number += len(chosen)
        return found
    gather_steps = numbered([
        (distances[-1 - at], subsets(distances[len(distances) - at:]))
        for at in range(len(distances))
    ])
    scatter_steps = numbered([
        (d, subsets(distances[at + 1:])) for at, d in enumerate(distances)
    ])

    def gather(number, chosen, d, sender):
        unit = flipped(me, chosen if sender else chosen + (d,))
        return pltpu.make_async_remote_copy(
            arrived.at[unit, beyond], arrived.at[unit, beyond], gather_send.at[number], gather_recv.at[number],
            device_id=(flipped(me, (d,)), col), device_id_type=MESH)

    def scatter(number, chosen, d):
        return pltpu.make_async_remote_copy(
            held.at[flipped(me, chosen + (d,))], landed.at[number],
            scatter_send.at[number], scatter_recv.at[number],
            device_id=(flipped(me, (d,)), col), device_id_type=MESH)

    def gather_start(at):
        for one in gather_steps[at]:
            gather(*one, True).start()

    def gather_finish(at):
        for one in gather_steps[at]:
            gather(*one, True).wait_send()
            gather(*one, False).wait_recv()

    def scatter_start(at):
        for one in scatter_steps[at]:
            scatter(*one).start()

    def scatter_finish(at):
        for one in scatter_steps[at]:
            scatter(*one).wait()
            mine = flipped(me, one[1])
            added = held[mine].astype(jnp.float32) + landed[one[0]].astype(jnp.float32)
            held[mine] = added.astype(held.dtype)

    pl.semaphore_wait(barrier, count + columns - 2)

    def pack_first(k):
        peer = shard_peer(k)
        for g in grad_parts[0]:
            pack(packed_ref, peer, peer, g, tiles_of(g), 0)
        grad_block(k, 0, True).start()
    each(count - 1, pack_first)
    for g in grad_parts[0]:
        pack(packed_ref, me, me, g, tiles_of(g), 0)

    loads = [pltpu.make_async_copy(old, new, state_sem.at[i])
             for i, (old, new) in enumerate(zip(old_hbm, states))]
    for load in loads:
        load.start()

    fullest = 0
    for o in range(1, count):
        fullest = jnp.where(slab_ref[o, capacity - SPARE_SLOTS] >= 0, o, fullest)
    spare_tiles = range(last_rows // part_rows, TILES)
    pack(held, 0, fullest, last, spare_tiles, last_rows // part_rows)
    arrived[me, beyond, :] = held[0]
    gather_start(0)

    def squares(i, carry):
        values = grad_ref[i].astype(jnp.float32)
        return carry + values * values
    acc = lax.fori_loop(
        0, layer_slabs, squares, jnp.zeros((part_rows, width), jnp.float32), unroll=10
    )
    row = lax.broadcasted_iota(jnp.int32, (part_rows, width), 0) + me * part_rows
    for e in range(emb):
        values = grad_ref[layer_slabs + e].astype(jnp.float32)
        acc += jnp.where(row < counts_ref[e], values * values, 0.0)
    part_ref[...] = jnp.broadcast_to(jnp.sum(acc, keepdims=True), part_ref.shape)
    each(count - 1, lambda k: small(k, True).start())

    for number in range(1, len(grad_parts)):
        for g in grad_parts[number]:
            pack_group(g)
        each(count - 1, lambda k, number=number: grad_block(k, number, True).start())
    own = pltpu.make_async_copy(packed_ref.at[me, direct], arrived.at[me, direct], own_sem)
    own.start()

    def add_shard(k):
        small(k, False).wait()
        mid_part[...] += shard_parts[shard_peer(k)]

    mid_part[...] = part_ref[...]
    each(count - 1, add_shard)
    each(columns - 1, lambda k: tens(k, True).start())
    gather_finish(0)
    gather_start(1)
    own.wait()
    for load in loads:
        load.wait()
    total = mid_part[0:1, :]
    each(columns - 1, lambda k: tens(k, False).wait())
    for k in range(columns - 1):
        total = total + tensor_parts[tensor_peer(k), 0:1, :]
    clip_scale = jnp.minimum(1.0, max_norm / (jnp.sqrt(total) + 1e-06))
    gather_finish(1)
    gather_start(2)

    eye = picker(slab_rows, slab_rows)

    def compute(group):
        base = group * group_rows

        def rows_of(index):
            return pl.ds(pl.multiple_of(base + PLACES[index] * part_rows, part_rows), part_rows)

        def advance(slot, window, gradient):
            place = group * GROUP + slot
            slab = slab_ref[me, place]
            live = counts_ref[jnp.clip(slab - layer_slabs, 0, emb - 1)]
            limit = jnp.where(slab < 0, -1, jnp.where(slab < layer_slabs, slab_rows, live))
            results = adam_update(
                gradient, clip_scale, limit, *[ref[place, window, :] for ref in states]
            )
            for ref, value in zip(states, results):
                ref[place, window, :] = value
            return results[0].astype(jnp.bfloat16)

        def packed(index):
            return arrived[:, rows_of(index), :].reshape(slab_rows, LANES)

        def send(index, weight):
            done = turned(eye, weight).astype(jnp.bfloat16)
            weights[:, rows_of(index), :] = done.reshape(count, part_rows, LANES)

        rest_pick = picker(rest, LANES)
        share_pick = picker(share, LANES, rest)
        rests = []
        for slot in range(GROUP):
            send(slot, advance(slot, pl.ds(0, LANES), turned(eye, packed(slot))))
            if slot < 3:
                gradient = turned(rest_pick, packed(4 + slot))
            else:
                gradient = jnp.concatenate(
                    [turned(share_pick, packed(4 + k)) for k in range(3)], axis=0
                )
            rests.append(advance(slot, pl.ds(LANES, rest), gradient))
        for k in range(3):
            piece = rests[3][k * share:(k + 1) * share]
            send(4 + k, jnp.concatenate([rests[k], piece], axis=0))

    back = pltpu.make_async_copy(weights.at[me, direct], returned.at[me, direct], back_sem)

    def turn(t, carry):
        group = 0
        for at, g in enumerate(order):
            group = jnp.where(t == at, g, group)
        for number, batch in enumerate(grad_parts):
            @pl.when(t == batch[0])
            def _():
                each(count - 1, lambda k: grad_block(k, number, False).wait())

        @pl.when(group == last)
        def _():
            gather_finish(2)

        compute(group)

        @pl.when(group == last)
        def _():
            held[...] = weights[:, beyond, :]
            scatter_start(0)
        for number, batch in enumerate(weight_parts):
            @pl.when(t == max(order.index(g) for g in batch))
            def _():
                each(count - 1, lambda k: weight_block(k, number, True).start())
        return carry

    lax.fori_loop(0, groups, turn, 0)
    back.start()
    for at in range(len(distances)):
        scatter_finish(at)
        if at + 1 < len(distances):
            scatter_start(at + 1)
    spare_out[...] = held[me]
    for number in range(len(weight_parts)):
        each(count - 1, lambda k, number=number: weight_block(k, number, False).wait())
    back.wait()


def step(owner, counts, grad, states, max_norm, mesh_sizes):
    count, columns = mesh_sizes
    capacity, width, slab_rows = states[0].shape
    part_rows = grad.shape[1]
    groups = capacity // GROUP
    grads = (len(batches(groups, GRAD_CUTS)), count)
    sends = (len(batches(groups, WEIGHT_CUTS)), count)
    packed = (count, groups * TILES * part_rows, LANES)
    spare = (SPARE_BLOCKS * part_rows, LANES)
    vmem = pl.BlockSpec(memory_space=pltpu.VMEM)
    hbm = pl.BlockSpec(memory_space=pltpu.HBM)
    dma = pltpu.SemaphoreType.DMA
    return pl.pallas_call(
        functools.partial(step_kernel, max_norm),
        in_specs=[hbm] * 7,
        out_specs=[vmem] * 7,
        out_shape=[pltpu.VMEM(packed, grad.dtype), pltpu.VMEM(spare, grad.dtype)]
        + [pltpu.VMEM(s.shape, s.dtype) for s in states]
        + [pltpu.VMEM((count, LANES), jnp.int32)],
        scratch_shapes=[
            pltpu.SMEM((count, LANES), jnp.int32),
            pltpu.VMEM(owner.shape, owner.dtype),
            pltpu.SMEM(counts.shape, counts.dtype),
            dma(()), dma(()),
            pltpu.VMEM(grad.shape, grad.dtype),
            pltpu.VMEM(packed, grad.dtype),
            pltpu.VMEM((8, LANES), jnp.float32),
            pltpu.VMEM(packed, grad.dtype),
            pltpu.VMEM(packed, grad.dtype),
            pltpu.VMEM((count, 8, LANES), jnp.float32),
            pltpu.VMEM((8, LANES), jnp.float32),
            pltpu.VMEM((columns, 8, LANES), jnp.float32),
            pltpu.VMEM((count,) + spare, grad.dtype),
            pltpu.VMEM((count,) + spare, grad.dtype),
            dma(()), dma(()), dma((4,)), dma(()), dma(()),
            dma((count,)), dma((count,)), dma((columns,)), dma((columns,)),
            dma(grads), dma(grads), dma(sends), dma(sends),
            dma((count,)), dma((count,)), dma((count,)), dma((count,)),
        ],
        compiler_params=pltpu.CompilerParams(
            collective_id=2, has_side_effects=True, vmem_limit_bytes=40 << 20
        ),
    )(owner, counts, grad, *states)


def unpack_kernel(capacity, table_ref, packed_ref, spare_ref, *refs):
    fresh, weight_hbm, kept, weight_ref, weight_sem, kept_sem, source_ref, source_sem = (
        refs[:4], refs[4], refs[5:9], refs[9], refs[10], refs[11], refs[12], refs[13]
    )
    load = pltpu.make_async_copy(table_ref, source_ref, source_sem)
    load.start()
    stores = [pltpu.make_async_copy(new, out, kept_sem.at[i])
              for i, (new, out) in enumerate(zip(fresh, kept))]
    for store in stores:
        store.start()
    load.wait()
    slab_count, part_rows, columns = weight_hbm.shape
    rest = columns - LANES
    share = rest // 3
    groups = capacity // 4

    def unpack(t, carry):
        p = t // groups
        g = t % groups
        base = g * (7 * part_rows)

        def piece(index):
            rows = pl.ds(pl.multiple_of(base + PLACES[index] * part_rows, part_rows), part_rows)
            return packed_ref[p, rows, :]
        blocks = [piece(index) for index in range(7)]
        for j in range(4):
            slab = source_ref[p, g * 4 + j]
            slab = jnp.where(slab < 0, slab_count, slab)
            weight_ref[slab, :, 0:LANES] = blocks[j]
            if j < 3:
                weight_ref[slab, :, LANES:columns] = blocks[4 + j][:, 0:rest]
            else:
                weight_ref[slab, :, LANES:columns] = jnp.concatenate(
                    [blocks[4 + k][:, rest:LANES] for k in range(3)], axis=1
                )
        return carry
    lax.fori_loop(0, packed_ref.shape[0] * groups, unpack, 0, unroll=2)
    fullest = 0
    for p in range(1, packed_ref.shape[0]):
        first_spare = source_ref[p, capacity - SPARE_SLOTS]
        fullest = jnp.where(first_spare >= 0, p, fullest)
    last = (groups - 1) * (7 * part_rows)
    spare = [None, None] + [
        spare_ref[pl.ds(k * part_rows, part_rows), :] for k in range(SPARE_BLOCKS)
    ]
    spare[1] = packed_ref[fullest, pl.ds(last + part_rows, part_rows), :]
    for j in range(1, 4):
        slab = source_ref[fullest, capacity - 4 + j]
        slab = jnp.where(slab < 0, slab_count, slab)
        weight_ref[slab, :, 0:LANES] = spare[PLACES[j]]
        if j < 3:
            weight_ref[slab, :, LANES:columns] = spare[PLACES[4 + j]][:, 0:rest]
        else:
            weight_ref[slab, :, LANES:columns] = jnp.concatenate(
                [spare[PLACES[4 + k]][:, rest:LANES] for k in range(3)], axis=1
            )
    store = pltpu.make_async_copy(weight_ref.at[pl.ds(0, slab_count)], weight_hbm, weight_sem)
    store.start()
    store.wait()
    for store in stores:
        store.wait()


def unpack(source, packed, spare, states, weight_shape, capacity):
    slab_count, part_rows, columns = weight_shape
    vmem = pl.BlockSpec(memory_space=pltpu.VMEM)
    hbm = pl.BlockSpec(memory_space=pltpu.HBM)
    return pl.pallas_call(
        functools.partial(unpack_kernel, capacity),
        in_specs=[vmem] * 7,
        out_specs=[hbm] * 5,
        out_shape=[jax.ShapeDtypeStruct(weight_shape, packed.dtype)]
        + [jax.ShapeDtypeStruct(s.shape, s.dtype) for s in states],
        scratch_shapes=[
            pltpu.VMEM((slab_count + 1, part_rows, columns), packed.dtype),
            pltpu.SemaphoreType.DMA(()),
            pltpu.SemaphoreType.DMA((4,)),
            pltpu.SMEM(source.shape, source.dtype),
            pltpu.SemaphoreType.DMA(()),
        ],
        compiler_params=pltpu.CompilerParams(vmem_limit_bytes=40 << 20),
    )(source, packed, spare, *states)


def per_device(mesh_sizes, grad, owner, counts, master, moment1, moment2, average):
    owner_count = mesh_sizes[0]
    slab_count, part_rows, columns = grad.shape
    capacity = master.shape[0]
    slab_rows = part_rows * owner_count
    max_norm = 0.5 * math.sqrt(slab_count * slab_rows * D)
    layer_slabs = slab_count - counts.shape[0]
    self_index = lax.axis_index("shard")
    states = (master, moment1, moment2, average)

    if part_rows % 16 == 0 and capacity % 4 == 0 and (columns - LANES) * 4 == 3 * LANES and (
        owner_count & (owner_count - 1) == 0 and slab_count <= 256 and capacity <= LANES
    ):
        inputs = (owner.reshape(1, -1), counts, grad) + states
        owner, counts, grad, *states = [
            pltpu.with_memory_space_constraint(x, pltpu.HBM) for x in inputs
        ]
        returned, spare, *states, source = step(
            owner, counts, grad, states, max_norm, mesh_sizes
        )
        return tuple(unpack(source, returned, spare, states, grad.shape, capacity))

    full_counts = jnp.concatenate([jnp.full((layer_slabs,), slab_rows, jnp.int32), counts])
    row_index = self_index * part_rows + jnp.arange(part_rows, dtype=jnp.int32)
    train_live = row_index[None, :] < full_counts[:, None]
    values = grad.astype(jnp.float32)
    part = jnp.sum(jnp.where(train_live[:, :, None], values * values, 0.0))
    part = jnp.broadcast_to(part, (8, LANES))

    place, marked = slot_tables(owner, owner_count, capacity)
    source = jnp.maximum(marked - 1, 0)
    own_marked = lax.dynamic_slice_in_dim(marked, self_index * capacity, capacity)
    own_live = jnp.take(full_counts, jnp.maximum(own_marked - 1, 0), mode="clip")
    limits = jnp.where(own_marked > 0, own_live, -1)

    outgoing = jnp.take(grad, source, axis=0, mode="clip")
    outgoing = outgoing.reshape(owner_count, capacity * part_rows, columns)
    arrived, total = exchange(outgoing, part, 0, mesh_sizes)
    arrived = arrived.reshape(owner_count, capacity, part_rows, columns)
    arrived = arrived.transpose(1, 0, 2, 3).reshape(capacity, slab_rows, columns)
    weights, *new_states = adam(limits, total, arrived, *states, max_norm, None)
    weights = weights.reshape(capacity, owner_count, part_rows, columns)
    weights = weights.transpose(1, 0, 2, 3)
    weights = weights.reshape(owner_count, capacity * part_rows, columns)
    (returned,) = exchange(weights, None, 1, mesh_sizes)
    returned = returned.reshape(owner_count * capacity, part_rows, columns)
    new_weight = jnp.take(returned, place, axis=0, mode="clip")
    return (new_weight, *new_states)


def solution(mesh):
    sizes = (mesh.shape["shard"], mesh.shape["tensor"])
    return jax.shard_map(
        functools.partial(per_device, sizes),
        mesh=mesh,
        in_specs=(
            P(None, "shard", "tensor"),
            P(),
            P(),
            P("shard", "tensor", None),
            P("shard", "tensor", None),
            P("shard", "tensor", None),
            P("shard", "tensor", None),
        ),
        out_specs=(
            P(None, "shard", "tensor"),
            P("shard", "tensor", None),
            P("shard", "tensor", None),
            P("shard", "tensor", None),
            P("shard", "tensor", None),
        ),
        check_vma=False,
    )
```

```python
import functools
import math

import jax
import jax.numpy as jnp
from jax import lax
from jax.experimental import pallas as pl
from jax.experimental.pallas import tpu as pltpu
from jax.sharding import PartitionSpec as P

D = 896
STEP = 20


BETA_ONE = 0.9
BETA_TWO = 0.95
ADAM_EPS = 1e-08
LEARN_RATE = 0.02
WEIGHT_DECAY = 0.1
AVERAGE_DECAY = 0.99

LANES = 128
PLACES = (0, 2, 3, 4, 1, 5, 6)
SPARE_SLOTS = 3
SPARE_BLOCKS = 5
MESH = pl.DeviceIdType.MESH


def slot_tables(owner, owner_count, capacity):
    slab_count = owner.shape[0]
    owner_ids = jnp.arange(owner_count, dtype=jnp.int32)
    slabs = jnp.arange(slab_count, dtype=jnp.int32)
    before = (owner[:, None] == owner[None, :]) & (slabs[None, :] < slabs[:, None])
    slot_rank = jnp.sum(before.astype(jnp.int32), axis=1)
    place = owner * capacity + slot_rank
    slot_ids = jnp.arange(owner_count * capacity, dtype=jnp.int32)
    matched = place[None, :] == slot_ids[:, None]
    marked = jnp.sum(jnp.where(matched, slabs[None, :] + 1, 0), axis=1)
    return (place, marked)


def peer_of(step, count):
    half = count // 2
    away = (step + 1) // 2
    return jnp.where(step % 2 == 1, half - away, half + away)


def subsets(distances):
    found = [()]
    for d in distances:
        found = found + [c + (d,) for c in found]
    return found


def flipped(index, distances):
    for d in distances:
        index = index + d * (1 - 2 * lax.rem(index // d, 2))
    return index


def exchange_kernel(with_sum, with_spare, *refs):
    refs = list(refs)
    out_ref = refs.pop(0)
    spare_in = refs.pop(0) if with_spare and with_sum else None
    part_ref = refs.pop(0) if with_sum else None
    in_ref = refs.pop(0)
    spare_out = refs.pop(0) if with_spare and not with_sum else None
    total_ref = refs.pop(0) if with_sum else None
    if with_sum:
        shard_parts, mid_part, tensor_parts = refs[:3]
        refs = refs[3:]
    local_sem, send_sem, recv_sem = refs[:3]
    refs = refs[3:]
    if with_sum:
        small_send, small_recv, tens_send, tens_recv = refs[:4]
        refs = refs[4:]
    if with_spare:
        spare_local, spare_send, spare_recv = refs[:3]
        refs = refs[3:]
        if not with_sum:
            held, landed = refs
    count = lax.axis_size("shard")
    columns = lax.axis_size("tensor")
    me = lax.axis_index("shard")
    col = lax.axis_index("tensor")

    def each(total, body):
        def step(k, carry):
            body(k)
            return carry
        lax.fori_loop(0, total, step, 0)

    def shard_peer(k):
        return lax.rem(me + peer_of(k, count), count)

    def tensor_peer(k):
        return lax.rem(col + k + 1, columns)

    rows = out_ref.shape[1]
    spare_rows = with_spare
    direct = pl.ds(0, rows - spare_rows)
    beyond = pl.ds(rows - spare_rows, spare_rows)
    distances = []
    while with_spare and 2 ** len(distances) < count:
        distances.append(2 ** len(distances))
    if spare_in is not None:
        keep_own = pltpu.make_async_copy(spare_in, in_ref.at[me, beyond], spare_local)
        keep_own.start()
    if spare_out is not None:
        keep_own = pltpu.make_async_copy(out_ref.at[:, beyond], held, spare_local)
        keep_own.start()
    own = pltpu.make_async_copy(
        out_ref.at[me, direct], in_ref.at[me, direct], local_sem
    )
    own.start()
    barrier = pltpu.get_barrier_semaphore()
    each(count - 1, lambda k: pl.semaphore_signal(
        barrier, inc=1, device_id=(shard_peer(k), col), device_id_type=MESH))
    greeted = count - 1
    if with_sum:
        each(columns - 1, lambda k: pl.semaphore_signal(
            barrier, inc=1, device_id=(me, tensor_peer(k)), device_id_type=MESH))
        greeted += columns - 1
    pl.semaphore_wait(barrier, greeted)

    def small(k):
        peer = shard_peer(k)
        return pltpu.make_async_remote_copy(
            part_ref, shard_parts.at[me], small_send.at[peer], small_recv.at[me],
            device_id=(peer, col), device_id_type=MESH)

    def small_in(k):
        peer = shard_peer(k)
        return pltpu.make_async_remote_copy(
            part_ref, shard_parts.at[peer], small_send.at[peer], small_recv.at[peer],
            device_id=(peer, col), device_id_type=MESH)

    def tens(k):
        peer = tensor_peer(k)
        return pltpu.make_async_remote_copy(
            mid_part, tensor_parts.at[col], tens_send.at[peer], tens_recv.at[col],
            device_id=(me, peer), device_id_type=MESH)

    def tens_in(k):
        peer = tensor_peer(k)
        return pltpu.make_async_remote_copy(
            mid_part, tensor_parts.at[peer], tens_send.at[peer], tens_recv.at[peer],
            device_id=(me, peer), device_id_type=MESH)

    def big(k):
        peer = shard_peer(k)
        return pltpu.make_async_remote_copy(
            out_ref.at[peer, direct], in_ref.at[me, direct], send_sem.at[peer], recv_sem.at[me],
            device_id=(peer, col), device_id_type=MESH)

    def big_in(k):
        peer = shard_peer(k)
        return pltpu.make_async_remote_copy(
            out_ref.at[peer, direct], in_ref.at[peer, direct], send_sem.at[peer], recv_sem.at[peer],
            device_id=(peer, col), device_id_type=MESH)

    def gather(number, chosen, d):
        unit = flipped(me, chosen)
        source = in_ref.at[unit, beyond] if chosen else spare_in
        return pltpu.make_async_remote_copy(
            source, in_ref.at[unit, beyond], spare_send.at[number], spare_recv.at[number],
            device_id=(flipped(me, (d,)), col), device_id_type=MESH)

    def gather_in(number, chosen, d):
        unit = flipped(me, chosen + (d,))
        return pltpu.make_async_remote_copy(
            spare_in, in_ref.at[unit, beyond], spare_send.at[number], spare_recv.at[number],
            device_id=(flipped(me, (d,)), col), device_id_type=MESH)

    def scatter(number, chosen, d):
        return pltpu.make_async_remote_copy(
            held.at[flipped(me, chosen + (d,))], landed.at[number],
            spare_send.at[number], spare_recv.at[number],
            device_id=(flipped(me, (d,)), col), device_id_type=MESH)

    steps = []
    if spare_in is not None:
        for at in range(len(distances)):
            d = distances[-1 - at]
            steps.append((d, subsets(distances[len(distances) - at:])))
    if spare_out is not None:
        for at, d in enumerate(distances):
            steps.append((d, subsets(distances[at + 1:])))
    number = 0
    numbered = []
    for d, chosen in steps:
        numbered.append([(number + i, c, d) for i, c in enumerate(chosen)])
        number += len(chosen)

    def spare_start(step):
        for one in step:
            (gather if spare_in is not None else scatter)(*one).start()

    def spare_finish(step):
        for one in step:
            if spare_in is not None:
                gather_in(*one).wait()
            else:
                scatter(*one).wait()
                mine = flipped(me, one[1])
                added = held[mine].astype(jnp.float32) + landed[one[0]].astype(jnp.float32)
                held[mine] = added.astype(held.dtype)

    if with_sum:
        each(count - 1, lambda k: small(k).start())
    if with_spare:
        if not with_sum:
            keep_own.wait()
        spare_start(numbered[0])
    def sum_shard():
        each(count - 1, lambda k: small_in(k).wait())
        mid_part[...] = part_ref[...]

        def add_shard(k):
            mid_part[...] += shard_parts[shard_peer(k)]
        each(count - 1, add_shard)
        each(columns - 1, lambda k: tens(k).start())

    stages = max(len(numbered), 1)
    share = (count - 1) // stages
    each(share, lambda k: big(k).start())
    for at in range(1, stages):
        spare_finish(numbered[at - 1])
        spare_start(numbered[at])
        if with_sum and at == 1:
            sum_shard()
        more = share if at + 1 < stages else count - 1 - at * share
        each(more, lambda k, at=at: big(k + at * share).start())
    if with_spare:
        spare_finish(numbered[-1])
        if with_sum:
            keep_own.wait()
        else:
            spare_out[...] = held[me]
    if with_sum:
        if stages == 1:
            sum_shard()
        each(columns - 1, lambda k: tens_in(k).wait())
        total_ref[...] = mid_part[...]

        def add_tensor(k):
            total_ref[...] += tensor_parts[tensor_peer(k)]
        each(columns - 1, add_tensor)
    each(count - 1, lambda k: big_in(k).wait())
    own.wait()


def exchange(blocks, part, collective_id, mesh_sizes, spare=None):
    count, columns = mesh_sizes
    with_sum = part is not None
    any_spec = pl.BlockSpec(memory_space=pl.ANY)
    vmem_spec = pl.BlockSpec(memory_space=pltpu.VMEM)
    out_shape = [jax.ShapeDtypeStruct(blocks.shape, blocks.dtype)]
    scratch = [
        pltpu.SemaphoreType.DMA(()),
        pltpu.SemaphoreType.DMA((count,)),
        pltpu.SemaphoreType.DMA((count,)),
    ]
    operands = [blocks]
    in_specs = [any_spec]
    out_specs = [any_spec]
    if spare is not None and with_sum:
        operands.append(spare)
        in_specs.append(any_spec)
    if spare is not None and not with_sum:
        out_shape.append(jax.ShapeDtypeStruct(spare.shape, spare.dtype))
        out_specs.append(vmem_spec)
    if with_sum:
        out_shape.append(jax.ShapeDtypeStruct(part.shape, part.dtype))
        out_specs.append(vmem_spec)
        in_specs.append(vmem_spec)
        operands.append(part)
        scratch = [
            pltpu.VMEM((count,) + part.shape, part.dtype),
            pltpu.VMEM(part.shape, part.dtype),
            pltpu.VMEM((columns,) + part.shape, part.dtype),
        ] + scratch + [
            pltpu.SemaphoreType.DMA((count,)),
            pltpu.SemaphoreType.DMA((count,)),
            pltpu.SemaphoreType.DMA((columns,)),
            pltpu.SemaphoreType.DMA((columns,)),
        ]
    if spare is not None:
        scratch = scratch + [
            pltpu.SemaphoreType.DMA(()),
            pltpu.SemaphoreType.DMA((count,)),
            pltpu.SemaphoreType.DMA((count,)),
        ]
        if not with_sum:
            scratch = scratch + [
                pltpu.VMEM((count,) + spare.shape, spare.dtype),
                pltpu.VMEM((count,) + spare.shape, spare.dtype),
            ]
    spare_rows = 0 if spare is None else spare.shape[0]
    return pl.pallas_call(
        functools.partial(exchange_kernel, with_sum, spare_rows),
        out_shape=out_shape,
        in_specs=in_specs,
        out_specs=out_specs,
        scratch_shapes=scratch,
        compiler_params=pltpu.CompilerParams(
            collective_id=collective_id, has_side_effects=True
        ),
    )(*operands)


def adam_update(gradient, clip_scale, limit, weight_old, first_old, second_old, average_old):
    lane = lax.broadcasted_iota(jnp.int32, gradient.shape, 1)
    live = lane < limit
    keep = lane >= jnp.where(limit < 0, gradient.shape[1], 0)
    clipped = gradient * clip_scale
    first_new = BETA_ONE * first_old + (1.0 - BETA_ONE) * clipped
    second_new = BETA_TWO * second_old + (1.0 - BETA_TWO) * clipped * clipped
    update = (first_new * (1.0 / (1.0 - BETA_ONE**STEP))) / (
        jnp.sqrt(second_new * (1.0 / (1.0 - BETA_TWO**STEP))) + ADAM_EPS
    )
    weight_new = weight_old - LEARN_RATE * (update + WEIGHT_DECAY * weight_old)
    average_new = AVERAGE_DECAY * average_old + (1.0 - AVERAGE_DECAY) * weight_new
    pairs = ((weight_new, weight_old), (first_new, first_old), (second_new, second_old),
             (average_new, average_old))
    return [jnp.where(keep, jnp.where(live, new, old), 0.0) for new, old in pairs]


def picker(rows, columns, shift=0):
    row = lax.broadcasted_iota(jnp.int32, (rows, columns), 0)
    column = lax.broadcasted_iota(jnp.int32, (rows, columns), 1)
    return (row + shift == column).astype(jnp.bfloat16)


def turned(pick, block):
    return lax.dot_general(
        pick, block, (((1,), (1,)), ((), ())), preferred_element_type=jnp.float32
    )


def adam_kernel(max_norm, part_rows, limit_ref, total_ref, grad_ref, *refs):
    old_refs, weight_out, new_refs = refs[:4], refs[4], refs[5:]
    per_step, columns, slab_rows = new_refs[0].shape
    total = total_ref[0:1, :]
    clip_scale = jnp.minimum(1.0, max_norm / (jnp.sqrt(total) + 1e-06))

    def advance(slot, window, gradient):
        limit = limit_ref[pl.program_id(0) * per_step + slot]
        results = adam_update(
            gradient, clip_scale, limit, *[ref[slot, window, :] for ref in old_refs]
        )
        for ref, value in zip(new_refs, results):
            ref[slot, window, :] = value
        return results[0].astype(jnp.bfloat16)

    eye = picker(slab_rows, slab_rows)
    if part_rows is None:
        for slot in range(per_step):
            weight = advance(slot, pl.ds(0, columns),
                             turned(picker(columns, columns), grad_ref[slot]))
            weight_out[slot] = turned(eye, weight).astype(jnp.bfloat16)
        return

    rest = columns - LANES
    share = rest // 3

    def packed(index):
        rows = pl.ds(PLACES[index] * part_rows, part_rows)
        return grad_ref[:, rows, :].reshape(slab_rows, LANES)

    def send(index, weight):
        rows = pl.ds(PLACES[index] * part_rows, part_rows)
        block = turned(eye, weight).astype(jnp.bfloat16)
        weight_out[:, rows, :] = block.reshape(-1, part_rows, LANES)

    main_pick = picker(LANES, LANES)
    rest_pick = picker(rest, LANES)
    share_pick = picker(share, LANES, rest)
    rests = []
    for slot in range(4):
        send(slot, advance(slot, pl.ds(0, LANES), turned(main_pick, packed(slot))))
        if slot < 3:
            gradient = turned(rest_pick, packed(4 + slot))
        else:
            gradient = jnp.concatenate(
                [turned(share_pick, packed(4 + k)) for k in range(3)], axis=0
            )
        rests.append(advance(slot, pl.ds(LANES, rest), gradient))
    for k in range(3):
        piece = rests[3][k * share:(k + 1) * share]
        send(4 + k, jnp.concatenate([rests[k], piece], axis=0))


def adam(limits, total, arrived, master, moment1, moment2, average, max_norm, part_rows):
    capacity, columns, slab_rows = master.shape
    per_step = 1 if part_rows is None else 4
    state = pl.BlockSpec((per_step, columns, slab_rows), lambda s, _: (s, 0, 0))
    if part_rows is None:
        rows = pl.BlockSpec((per_step, slab_rows, columns), lambda s, _: (s, 0, 0))
    else:
        rows = pl.BlockSpec(
            (slab_rows // part_rows, 7 * part_rows, LANES), lambda s, _: (0, s, 0)
        )
    whole = pl.BlockSpec(total.shape, lambda s, _: (0, 0))
    return pl.pallas_call(
        functools.partial(adam_kernel, max_norm, part_rows),
        grid_spec=pltpu.PrefetchScalarGridSpec(
            num_scalar_prefetch=1,
            grid=(capacity // per_step,),
            in_specs=[whole, rows, state, state, state, state],
            out_specs=[rows, state, state, state, state],
        ),
        out_shape=[jax.ShapeDtypeStruct(arrived.shape, jnp.bfloat16)]
        + [jax.ShapeDtypeStruct(master.shape, jnp.float32)] * 4,
        compiler_params=pltpu.CompilerParams(vmem_limit_bytes=60 << 20),
    )(limits, total, arrived, master, moment1, moment2, average)


GROUP = 4
GRAD_CUTS = (1, 3)
EARLY = 1
WEIGHT_CUTS = (1, 3)
LATE = 1
TILES = 7


def batches(groups, cuts):
    cuts = sorted({0, groups, *[min(c, groups) for c in cuts]})
    return [list(range(a, b)) for a, b in zip(cuts, cuts[1:])]


def grad_batches(groups):
    first, *later = batches(groups - 1, GRAD_CUTS)
    return [first, [groups - 1], *later]


def work_order(groups):
    order = list(range(groups - 1))
    order.insert(min(EARLY, groups - 1), groups - 1)
    return order


def slot_table(owner, owner_count):
    slab_count = owner.shape[1]
    wide = (owner_count, slab_count)
    hit = owner == lax.broadcasted_iota(jnp.int32, wide, 0)
    earlier = lax.broadcasted_iota(jnp.int32, (slab_count, slab_count), 0) < (
        lax.broadcasted_iota(jnp.int32, (slab_count, slab_count), 1)
    )
    ranks = jnp.dot(
        hit.astype(jnp.bfloat16), earlier.astype(jnp.bfloat16), preferred_element_type=jnp.float32
    )
    rank = jnp.sum(jnp.where(hit, ranks, 0.0), axis=0, keepdims=True).astype(jnp.int32)
    at_slot = rank == lax.broadcasted_iota(jnp.int32, (LANES, slab_count), 0)
    number = lax.broadcasted_iota(jnp.int32, wide, 1) + 1
    marked = lax.dot_general(
        jnp.where(hit, number, 0).astype(jnp.float32).astype(jnp.bfloat16),
        at_slot.astype(jnp.bfloat16),
        (((1,), (1,)), ((), ())), preferred_element_type=jnp.float32,
    )
    return marked.astype(jnp.int32) - 1


def step_kernel(max_norm, owner_hbm, counts_hbm, grad_hbm, *refs):
    old_hbm, refs = refs[:4], refs[4:]
    returned, spare_out, states, table_ref, refs = refs[0], refs[1], refs[2:6], refs[6], refs[7:]
    slab_ref, refs = refs[0], refs[1:]
    owner_ref, counts_ref, owner_sem, counts_sem, refs = refs[:4] + (refs[4:],)
    owner_load = pltpu.make_async_copy(owner_hbm, owner_ref, owner_sem)
    owner_load.start()
    counts_load = pltpu.make_async_copy(counts_hbm, counts_ref, counts_sem)
    counts_load.start()
    grad_ref, packed_ref, part_ref, refs = refs[:3] + (refs[3:],)
    arrived, weights, shard_parts, mid_part, tensor_parts, held, landed, refs = refs[:7] + (refs[7:],)
    (grad_sem, table_sem, state_sem, own_sem, back_sem, small_send, small_recv, tens_send, tens_recv,
     grad_send, grad_recv, weight_send, weight_recv, gather_send, gather_recv,
     scatter_send, scatter_recv) = refs
    count = lax.axis_size("shard")
    columns = lax.axis_size("tensor")
    me = lax.axis_index("shard")
    col = lax.axis_index("tensor")
    capacity, width, slab_rows = states[0].shape
    part_rows = slab_rows // count
    groups = capacity // GROUP
    group_rows = TILES * part_rows
    spare_rows = spare_out.shape[0]
    slab_count = grad_ref.shape[0]
    emb = counts_ref.shape[0]
    layer_slabs = slab_count - emb
    rest = width - LANES
    share = rest // 3
    direct_rows = packed_ref.shape[1] - spare_rows
    last_rows = direct_rows - (groups - 1) * group_rows
    direct = pl.ds(0, direct_rows)
    beyond = pl.ds(direct_rows, spare_rows)
    last = groups - 1
    weight_parts = batches(groups, WEIGHT_CUTS)
    grad_parts = grad_batches(groups)
    order = work_order(groups)

    def each(total, body):
        def step(k, carry):
            body(k)
            return carry
        lax.fori_loop(0, total, step, 0)

    def shard_peer(k):
        return lax.rem(me + peer_of(k, count), count)

    def tensor_peer(k):
        return lax.rem(col + k + 1, columns)

    def late_peer(k):
        half, front = count // 2, count // 4
        own = jnp.where(me >= half, me, jnp.where(me < front, me, me + half))
        at = jnp.where(k >= own, k + 1, k)
        near = jnp.where(at < front, at, jnp.where(at < front + half, at - front + half, at - half))
        return jnp.where(me >= half, at, near)

    fetch = pltpu.make_async_copy(grad_hbm, grad_ref, grad_sem)
    fetch.start()
    barrier = pltpu.get_barrier_semaphore()
    each(count - 1, lambda k: pl.semaphore_signal(
        barrier, inc=1, device_id=(shard_peer(k), col), device_id_type=MESH))
    each(columns - 1, lambda k: pl.semaphore_signal(
        barrier, inc=1, device_id=(me, tensor_peer(k)), device_id_type=MESH))
    owner_load.wait()
    table_ref[...] = slot_table(owner_ref[...], count)
    tabled = pltpu.make_async_copy(table_ref, slab_ref, table_sem)
    tabled.start()
    counts_load.wait()
    tabled.wait()
    fetch.wait()

    def pack(target, unit, holder, group, tiles, first):
        for j in range(GROUP):
            slab = jnp.clip(slab_ref[holder, group * GROUP + j], 0, slab_count - 1)

            def rows_of(index):
                start = (PLACES[index] - first) * part_rows
                if first == 0:
                    start = group * group_rows + start
                return pl.ds(start, part_rows)
            if PLACES[j] in tiles:
                target[unit, rows_of(j), :] = grad_ref[slab, :, 0:LANES]
            if j < 3:
                if PLACES[4 + j] in tiles:
                    target[unit, rows_of(4 + j), 0:rest] = grad_ref[slab, :, LANES:width]
            else:
                for k in range(3):
                    if PLACES[4 + k] in tiles:
                        begin = LANES + k * share
                        target[unit, rows_of(4 + k), rest:LANES] = (
                            grad_ref[slab, :, begin:begin + share]
                        )

    def tiles_of(group):
        return range(TILES) if group < last else range(last_rows // part_rows)

    def pack_group(group):
        each(count, lambda p: pack(packed_ref, p, p, group, tiles_of(group), 0))

    def small(k, sender):
        peer = shard_peer(k)
        slot = me if sender else peer
        return pltpu.make_async_remote_copy(
            part_ref, shard_parts.at[slot], small_send.at[peer], small_recv.at[slot],
            device_id=(peer, col), device_id_type=MESH)

    def tens(k, sender):
        peer = tensor_peer(k)
        slot = col if sender else peer
        return pltpu.make_async_remote_copy(
            mid_part, tensor_parts.at[slot], tens_send.at[peer], tens_recv.at[slot],
            device_id=(me, peer), device_id_type=MESH)

    def block(parts, source, target, send, recv, peer, number, sender):
        slot = me if sender else peer
        first = parts[number][0] * group_rows
        end = direct_rows if parts[number][-1] == last else (parts[number][-1] + 1) * group_rows
        window = pl.ds(first, end - first)
        return pltpu.make_async_remote_copy(
            source.at[peer, window], target.at[slot, window],
            send.at[number, peer], recv.at[number, slot],
            device_id=(peer, col), device_id_type=MESH)

    def grad_block(k, number, sender):
        return block(
            grad_parts, packed_ref, arrived, grad_send, grad_recv, shard_peer(k), number, sender
        )

    def weight_block(k, number, sender):
        peer = late_peer(k) if number >= LATE else shard_peer(k)
        return block(
            weight_parts, weights, returned, weight_send, weight_recv, peer, number, sender
        )

    distances = []
    while 2 ** len(distances) < count:
        distances.append(2 ** len(distances))

    def numbered(pairs):
        found, number = [], 0
        for d, chosen in pairs:
            found.append([(number + i, c, d) for i, c in enumerate(chosen)])
            number += len(chosen)
        return found
    gather_steps = numbered([
        (distances[-1 - at], subsets(distances[len(distances) - at:]))
        for at in range(len(distances))
    ])
    scatter_steps = numbered([
        (d, subsets(distances[at + 1:])) for at, d in enumerate(distances)
    ])

    def gather(number, chosen, d, sender):
        unit = flipped(me, chosen if sender else chosen + (d,))
        return pltpu.make_async_remote_copy(
            arrived.at[unit, beyond], arrived.at[unit, beyond], gather_send.at[number], gather_recv.at[number],
            device_id=(flipped(me, (d,)), col), device_id_type=MESH)

    def scatter(number, chosen, d):
        return pltpu.make_async_remote_copy(
            held.at[flipped(me, chosen + (d,))], landed.at[number],
            scatter_send.at[number], scatter_recv.at[number],
            device_id=(flipped(me, (d,)), col), device_id_type=MESH)

    def gather_start(at):
        for one in gather_steps[at]:
            gather(*one, True).start()

    def gather_finish(at):
        for one in gather_steps[at]:
            gather(*one, True).wait_send()
            gather(*one, False).wait_recv()

    def scatter_start(at):
        for one in scatter_steps[at]:
            scatter(*one).start()

    def scatter_finish(at):
        for one in scatter_steps[at]:
            scatter(*one).wait()
            mine = flipped(me, one[1])
            added = held[mine].astype(jnp.float32) + landed[one[0]].astype(jnp.float32)
            held[mine] = added.astype(held.dtype)

    pl.semaphore_wait(barrier, count + columns - 2)

    def pack_first(k):
        peer = shard_peer(k)
        for g in grad_parts[0]:
            pack(packed_ref, peer, peer, g, tiles_of(g), 0)
        grad_block(k, 0, True).start()
    each(count - 1, pack_first)
    for g in grad_parts[0]:
        pack(packed_ref, me, me, g, tiles_of(g), 0)

    loads = [pltpu.make_async_copy(old, new, state_sem.at[i])
             for i, (old, new) in enumerate(zip(old_hbm, states))]
    for load in loads:
        load.start()

    fullest = 0
    for o in range(1, count):
        fullest = jnp.where(slab_ref[o, capacity - SPARE_SLOTS] >= 0, o, fullest)
    spare_tiles = range(last_rows // part_rows, TILES)
    pack(held, 0, fullest, last, spare_tiles, last_rows // part_rows)
    arrived[me, beyond, :] = held[0]
    gather_start(0)

    def squares(i, carry):
        values = grad_ref[i].astype(jnp.float32)
        return carry + values * values
    acc = lax.fori_loop(
        0, layer_slabs, squares, jnp.zeros((part_rows, width), jnp.float32), unroll=10
    )
    row = lax.broadcasted_iota(jnp.int32, (part_rows, width), 0) + me * part_rows
    for e in range(emb):
        values = grad_ref[layer_slabs + e].astype(jnp.float32)
        acc += jnp.where(row < counts_ref[e], values * values, 0.0)
    part_ref[...] = jnp.broadcast_to(jnp.sum(acc, keepdims=True), part_ref.shape)
    each(count - 1, lambda k: small(k, True).start())

    for number in range(1, len(grad_parts)):
        for g in grad_parts[number]:
            pack_group(g)
        each(count - 1, lambda k, number=number: grad_block(k, number, True).start())
    own = pltpu.make_async_copy(packed_ref.at[me, direct], arrived.at[me, direct], own_sem)
    own.start()

    def add_shard(k):
        small(k, False).wait()
        mid_part[...] += shard_parts[shard_peer(k)]

    mid_part[...] = part_ref[...]
    each(count - 1, add_shard)
    each(columns - 1, lambda k: tens(k, True).start())
    gather_finish(0)
    gather_start(1)
    own.wait()
    for load in loads:
        load.wait()
    total = mid_part[0:1, :]
    each(columns - 1, lambda k: tens(k, False).wait())
    for k in range(columns - 1):
        total = total + tensor_parts[tensor_peer(k), 0:1, :]
    clip_scale = jnp.minimum(1.0, max_norm / (jnp.sqrt(total) + 1e-06))
    gather_finish(1)
    gather_start(2)

    eye = picker(slab_rows, slab_rows)

    def compute(group):
        base = group * group_rows

        def rows_of(index):
            return pl.ds(pl.multiple_of(base + PLACES[index] * part_rows, part_rows), part_rows)

        def advance(slot, window, gradient):
            place = group * GROUP + slot
            slab = slab_ref[me, place]
            live = counts_ref[jnp.clip(slab - layer_slabs, 0, emb - 1)]
            limit = jnp.where(slab < 0, -1, jnp.where(slab < layer_slabs, slab_rows, live))
            results = adam_update(
                gradient, clip_scale, limit, *[ref[place, window, :] for ref in states]
            )
            for ref, value in zip(states, results):
                ref[place, window, :] = value
            return results[0].astype(jnp.bfloat16)

        def packed(index):
            return arrived[:, rows_of(index), :].reshape(slab_rows, LANES)

        def send(index, weight):
            done = turned(eye, weight).astype(jnp.bfloat16)
            weights[:, rows_of(index), :] = done.reshape(count, part_rows, LANES)

        rest_pick = picker(rest, LANES)
        share_pick = picker(share, LANES, rest)
        rests = []
        for slot in range(GROUP):
            send(slot, advance(slot, pl.ds(0, LANES), turned(eye, packed(slot))))
            if slot < 3:
                gradient = turned(rest_pick, packed(4 + slot))
            else:
                gradient = jnp.concatenate(
                    [turned(share_pick, packed(4 + k)) for k in range(3)], axis=0
                )
            rests.append(advance(slot, pl.ds(LANES, rest), gradient))
        for k in range(3):
            piece = rests[3][k * share:(k + 1) * share]
            send(4 + k, jnp.concatenate([rests[k], piece], axis=0))

    back = pltpu.make_async_copy(weights.at[me, direct], returned.at[me, direct], back_sem)

    def turn(t, carry):
        group = 0
        for at, g in enumerate(order):
            group = jnp.where(t == at, g, group)
        for number, batch in enumerate(grad_parts):
            @pl.when(t == min(order.index(g) for g in batch))
            def _():
                each(count - 1, lambda k: grad_block(k, number, False).wait())

        @pl.when(group == last)
        def _():
            gather_finish(2)

        compute(group)

        @pl.when(group == last)
        def _():
            held[...] = weights[:, beyond, :]
            scatter_start(0)
        for number, batch in enumerate(weight_parts):
            @pl.when(t == max(order.index(g) for g in batch))
            def _():
                if number + 1 < len(weight_parts):
                    each(count - 1, lambda k: weight_block(k, number, True).start())
                else:
                    each(1, lambda k: weight_block(k, number, True).start())
        for at in range(1, len(distances)):
            @pl.when(t == groups - len(distances) + at)
            def _():
                scatter_finish(at - 1)
                scatter_start(at)
        return carry

    lax.fori_loop(0, groups, turn, 0)
    last_part = len(weight_parts) - 1
    each(1, lambda k: weight_block(k, last_part, True).wait_send())
    each(count - 1 - 1, lambda k: weight_block(k + 1, last_part, True).start())
    back.start()
    scatter_finish(len(distances) - 1)
    spare_out[...] = held[me]
    for number in range(len(weight_parts) - 1):
        each(count - 1, lambda k, number=number: weight_block(k, number, False).wait())
    final = len(weight_parts) - 1
    each(count - 1, lambda k: weight_block(k, final, False).wait_recv())
    each(count - 1 - 1, lambda k: weight_block(k + 1, final, False).wait_send())
    back.wait()


def step(owner, counts, grad, states, max_norm, mesh_sizes):
    count, columns = mesh_sizes
    capacity, width, slab_rows = states[0].shape
    part_rows = grad.shape[1]
    groups = capacity // GROUP
    grads = (len(grad_batches(groups)), count)
    sends = (len(batches(groups, WEIGHT_CUTS)), count)
    packed = (count, groups * TILES * part_rows, LANES)
    spare = (SPARE_BLOCKS * part_rows, LANES)
    vmem = pl.BlockSpec(memory_space=pltpu.VMEM)
    hbm = pl.BlockSpec(memory_space=pltpu.HBM)
    dma = pltpu.SemaphoreType.DMA
    return pl.pallas_call(
        functools.partial(step_kernel, max_norm),
        in_specs=[hbm] * 7,
        out_specs=[vmem] * 7,
        out_shape=[pltpu.VMEM(packed, grad.dtype), pltpu.VMEM(spare, grad.dtype)]
        + [pltpu.VMEM(s.shape, s.dtype) for s in states]
        + [pltpu.VMEM((count, LANES), jnp.int32)],
        scratch_shapes=[
            pltpu.SMEM((count, LANES), jnp.int32),
            pltpu.VMEM(owner.shape, owner.dtype),
            pltpu.SMEM(counts.shape, counts.dtype),
            dma(()), dma(()),
            pltpu.VMEM(grad.shape, grad.dtype),
            pltpu.VMEM(packed, grad.dtype),
            pltpu.VMEM((8, LANES), jnp.float32),
            pltpu.VMEM(packed, grad.dtype),
            pltpu.VMEM(packed, grad.dtype),
            pltpu.VMEM((count, 8, LANES), jnp.float32),
            pltpu.VMEM((8, LANES), jnp.float32),
            pltpu.VMEM((columns, 8, LANES), jnp.float32),
            pltpu.VMEM((count,) + spare, grad.dtype),
            pltpu.VMEM((count,) + spare, grad.dtype),
            dma(()), dma(()), dma((4,)), dma(()), dma(()),
            dma((count,)), dma((count,)), dma((columns,)), dma((columns,)),
            dma(grads), dma(grads), dma(sends), dma(sends),
            dma((count,)), dma((count,)), dma((count,)), dma((count,)),
        ],
        compiler_params=pltpu.CompilerParams(
            collective_id=2, has_side_effects=True, vmem_limit_bytes=40 << 20
        ),
    )(owner, counts, grad, *states)


def unpack_kernel(capacity, table_ref, packed_ref, spare_ref, *refs):
    fresh, weight_hbm, kept, weight_ref, weight_sem, kept_sem, source_ref, source_sem = (
        refs[:4], refs[4], refs[5:9], refs[9], refs[10], refs[11], refs[12], refs[13]
    )
    load = pltpu.make_async_copy(table_ref, source_ref, source_sem)
    load.start()
    stores = [pltpu.make_async_copy(new, out, kept_sem.at[i])
              for i, (new, out) in enumerate(zip(fresh, kept))]
    for store in stores:
        store.start()
    load.wait()
    slab_count, part_rows, columns = weight_hbm.shape
    rest = columns - LANES
    share = rest // 3
    groups = capacity // 4

    def unpack(t, carry):
        p = t // groups
        g = t % groups
        base = g * (7 * part_rows)

        def piece(index):
            rows = pl.ds(pl.multiple_of(base + PLACES[index] * part_rows, part_rows), part_rows)
            return packed_ref[p, rows, :]
        blocks = [piece(index) for index in range(7)]
        for j in range(4):
            slab = source_ref[p, g * 4 + j]
            slab = jnp.where(slab < 0, slab_count, slab)
            weight_ref[slab, :, 0:LANES] = blocks[j]
            if j < 3:
                weight_ref[slab, :, LANES:columns] = blocks[4 + j][:, 0:rest]
            else:
                weight_ref[slab, :, LANES:columns] = jnp.concatenate(
                    [blocks[4 + k][:, rest:LANES] for k in range(3)], axis=1
                )
        return carry
    lax.fori_loop(0, packed_ref.shape[0] * groups, unpack, 0, unroll=2)
    fullest = 0
    for p in range(1, packed_ref.shape[0]):
        first_spare = source_ref[p, capacity - SPARE_SLOTS]
        fullest = jnp.where(first_spare >= 0, p, fullest)
    last = (groups - 1) * (7 * part_rows)
    spare = [None, None] + [
        spare_ref[pl.ds(k * part_rows, part_rows), :] for k in range(SPARE_BLOCKS)
    ]
    spare[1] = packed_ref[fullest, pl.ds(last + part_rows, part_rows), :]
    for j in range(1, 4):
        slab = source_ref[fullest, capacity - 4 + j]
        slab = jnp.where(slab < 0, slab_count, slab)
        weight_ref[slab, :, 0:LANES] = spare[PLACES[j]]
        if j < 3:
            weight_ref[slab, :, LANES:columns] = spare[PLACES[4 + j]][:, 0:rest]
        else:
            weight_ref[slab, :, LANES:columns] = jnp.concatenate(
                [spare[PLACES[4 + k]][:, rest:LANES] for k in range(3)], axis=1
            )
    store = pltpu.make_async_copy(weight_ref.at[pl.ds(0, slab_count)], weight_hbm, weight_sem)
    store.start()
    store.wait()
    for store in stores:
        store.wait()


def unpack(source, packed, spare, states, weight_shape, capacity):
    slab_count, part_rows, columns = weight_shape
    vmem = pl.BlockSpec(memory_space=pltpu.VMEM)
    hbm = pl.BlockSpec(memory_space=pltpu.HBM)
    return pl.pallas_call(
        functools.partial(unpack_kernel, capacity),
        in_specs=[vmem] * 7,
        out_specs=[hbm] * 5,
        out_shape=[jax.ShapeDtypeStruct(weight_shape, packed.dtype)]
        + [jax.ShapeDtypeStruct(s.shape, s.dtype) for s in states],
        scratch_shapes=[
            pltpu.VMEM((slab_count + 1, part_rows, columns), packed.dtype),
            pltpu.SemaphoreType.DMA(()),
            pltpu.SemaphoreType.DMA((4,)),
            pltpu.SMEM(source.shape, source.dtype),
            pltpu.SemaphoreType.DMA(()),
        ],
        compiler_params=pltpu.CompilerParams(vmem_limit_bytes=40 << 20),
    )(source, packed, spare, *states)


def per_device(mesh_sizes, grad, owner, counts, master, moment1, moment2, average):
    owner_count = mesh_sizes[0]
    slab_count, part_rows, columns = grad.shape
    capacity = master.shape[0]
    slab_rows = part_rows * owner_count
    max_norm = 0.5 * math.sqrt(slab_count * slab_rows * D)
    layer_slabs = slab_count - counts.shape[0]
    self_index = lax.axis_index("shard")
    states = (master, moment1, moment2, average)

    if part_rows % 16 == 0 and capacity % 4 == 0 and (columns - LANES) * 4 == 3 * LANES and (
        owner_count & (owner_count - 1) == 0 and slab_count <= 256 and capacity <= LANES
    ):
        inputs = (owner.reshape(1, -1), counts, grad) + states
        owner, counts, grad, *states = [
            pltpu.with_memory_space_constraint(x, pltpu.HBM) for x in inputs
        ]
        returned, spare, *states, source = step(
            owner, counts, grad, states, max_norm, mesh_sizes
        )
        return tuple(unpack(source, returned, spare, states, grad.shape, capacity))

    full_counts = jnp.concatenate([jnp.full((layer_slabs,), slab_rows, jnp.int32), counts])
    row_index = self_index * part_rows + jnp.arange(part_rows, dtype=jnp.int32)
    train_live = row_index[None, :] < full_counts[:, None]
    values = grad.astype(jnp.float32)
    part = jnp.sum(jnp.where(train_live[:, :, None], values * values, 0.0))
    part = jnp.broadcast_to(part, (8, LANES))

    place, marked = slot_tables(owner, owner_count, capacity)
    source = jnp.maximum(marked - 1, 0)
    own_marked = lax.dynamic_slice_in_dim(marked, self_index * capacity, capacity)
    own_live = jnp.take(full_counts, jnp.maximum(own_marked - 1, 0), mode="clip")
    limits = jnp.where(own_marked > 0, own_live, -1)

    outgoing = jnp.take(grad, source, axis=0, mode="clip")
    outgoing = outgoing.reshape(owner_count, capacity * part_rows, columns)
    arrived, total = exchange(outgoing, part, 0, mesh_sizes)
    arrived = arrived.reshape(owner_count, capacity, part_rows, columns)
    arrived = arrived.transpose(1, 0, 2, 3).reshape(capacity, slab_rows, columns)
    weights, *new_states = adam(limits, total, arrived, *states, max_norm, None)
    weights = weights.reshape(capacity, owner_count, part_rows, columns)
    weights = weights.transpose(1, 0, 2, 3)
    weights = weights.reshape(owner_count, capacity * part_rows, columns)
    (returned,) = exchange(weights, None, 1, mesh_sizes)
    returned = returned.reshape(owner_count * capacity, part_rows, columns)
    new_weight = jnp.take(returned, place, axis=0, mode="clip")
    return (new_weight, *new_states)


def solution(mesh):
    sizes = (mesh.shape["shard"], mesh.shape["tensor"])
    return jax.shard_map(
        functools.partial(per_device, sizes),
        mesh=mesh,
        in_specs=(
            P(None, "shard", "tensor"),
            P(),
            P(),
            P("shard", "tensor", None),
            P("shard", "tensor", None),
            P("shard", "tensor", None),
            P("shard", "tensor", None),
        ),
        out_specs=(
            P(None, "shard", "tensor"),
            P("shard", "tensor", None),
            P("shard", "tensor", None),
            P("shard", "tensor", None),
            P("shard", "tensor", None),
        ),
        check_vma=False,
    )
```

```python
import functools
import math

import jax
import jax.numpy as jnp
from jax import lax
from jax.experimental import pallas as pl
from jax.experimental.pallas import tpu as pltpu
from jax.sharding import PartitionSpec as P

D = 896
STEP = 20


BETA_ONE = 0.9
BETA_TWO = 0.95
ADAM_EPS = 1e-08
LEARN_RATE = 0.02
WEIGHT_DECAY = 0.1
AVERAGE_DECAY = 0.99

LANES = 128
PLACES = (0, 2, 3, 4, 1, 5, 6)
SPARE_SLOTS = 3
SPARE_BLOCKS = 5
MESH = pl.DeviceIdType.MESH


def slot_tables(owner, owner_count, capacity):
    slab_count = owner.shape[0]
    owner_ids = jnp.arange(owner_count, dtype=jnp.int32)
    slabs = jnp.arange(slab_count, dtype=jnp.int32)
    before = (owner[:, None] == owner[None, :]) & (slabs[None, :] < slabs[:, None])
    slot_rank = jnp.sum(before.astype(jnp.int32), axis=1)
    place = owner * capacity + slot_rank
    slot_ids = jnp.arange(owner_count * capacity, dtype=jnp.int32)
    matched = place[None, :] == slot_ids[:, None]
    marked = jnp.sum(jnp.where(matched, slabs[None, :] + 1, 0), axis=1)
    return (place, marked)


def peer_of(step, count):
    half = count // 2
    away = (step + 1) // 2
    return jnp.where(step % 2 == 1, half - away, half + away)


def subsets(distances):
    found = [()]
    for d in distances:
        found = found + [c + (d,) for c in found]
    return found


def flipped(index, distances):
    for d in distances:
        index = index + d * (1 - 2 * lax.rem(index // d, 2))
    return index


def exchange_kernel(with_sum, with_spare, *refs):
    refs = list(refs)
    out_ref = refs.pop(0)
    spare_in = refs.pop(0) if with_spare and with_sum else None
    part_ref = refs.pop(0) if with_sum else None
    in_ref = refs.pop(0)
    spare_out = refs.pop(0) if with_spare and not with_sum else None
    total_ref = refs.pop(0) if with_sum else None
    if with_sum:
        shard_parts, mid_part, tensor_parts = refs[:3]
        refs = refs[3:]
    local_sem, send_sem, recv_sem = refs[:3]
    refs = refs[3:]
    if with_sum:
        small_send, small_recv, tens_send, tens_recv = refs[:4]
        refs = refs[4:]
    if with_spare:
        spare_local, spare_send, spare_recv = refs[:3]
        refs = refs[3:]
        if not with_sum:
            held, landed = refs
    count = lax.axis_size("shard")
    columns = lax.axis_size("tensor")
    me = lax.axis_index("shard")
    col = lax.axis_index("tensor")

    def each(total, body):
        def step(k, carry):
            body(k)
            return carry
        lax.fori_loop(0, total, step, 0)

    def shard_peer(k):
        return lax.rem(me + peer_of(k, count), count)

    def tensor_peer(k):
        return lax.rem(col + k + 1, columns)

    rows = out_ref.shape[1]
    spare_rows = with_spare
    direct = pl.ds(0, rows - spare_rows)
    beyond = pl.ds(rows - spare_rows, spare_rows)
    distances = []
    while with_spare and 2 ** len(distances) < count:
        distances.append(2 ** len(distances))
    if spare_in is not None:
        keep_own = pltpu.make_async_copy(spare_in, in_ref.at[me, beyond], spare_local)
        keep_own.start()
    if spare_out is not None:
        keep_own = pltpu.make_async_copy(out_ref.at[:, beyond], held, spare_local)
        keep_own.start()
    own = pltpu.make_async_copy(
        out_ref.at[me, direct], in_ref.at[me, direct], local_sem
    )
    own.start()
    barrier = pltpu.get_barrier_semaphore()
    each(count - 1, lambda k: pl.semaphore_signal(
        barrier, inc=1, device_id=(shard_peer(k), col), device_id_type=MESH))
    greeted = count - 1
    if with_sum:
        each(columns - 1, lambda k: pl.semaphore_signal(
            barrier, inc=1, device_id=(me, tensor_peer(k)), device_id_type=MESH))
        greeted += columns - 1
    pl.semaphore_wait(barrier, greeted)

    def small(k):
        peer = shard_peer(k)
        return pltpu.make_async_remote_copy(
            part_ref, shard_parts.at[me], small_send.at[peer], small_recv.at[me],
            device_id=(peer, col), device_id_type=MESH)

    def small_in(k):
        peer = shard_peer(k)
        return pltpu.make_async_remote_copy(
            part_ref, shard_parts.at[peer], small_send.at[peer], small_recv.at[peer],
            device_id=(peer, col), device_id_type=MESH)

    def tens(k):
        peer = tensor_peer(k)
        return pltpu.make_async_remote_copy(
            mid_part, tensor_parts.at[col], tens_send.at[peer], tens_recv.at[col],
            device_id=(me, peer), device_id_type=MESH)

    def tens_in(k):
        peer = tensor_peer(k)
        return pltpu.make_async_remote_copy(
            mid_part, tensor_parts.at[peer], tens_send.at[peer], tens_recv.at[peer],
            device_id=(me, peer), device_id_type=MESH)

    def big(k):
        peer = shard_peer(k)
        return pltpu.make_async_remote_copy(
            out_ref.at[peer, direct], in_ref.at[me, direct], send_sem.at[peer], recv_sem.at[me],
            device_id=(peer, col), device_id_type=MESH)

    def big_in(k):
        peer = shard_peer(k)
        return pltpu.make_async_remote_copy(
            out_ref.at[peer, direct], in_ref.at[peer, direct], send_sem.at[peer], recv_sem.at[peer],
            device_id=(peer, col), device_id_type=MESH)

    def gather(number, chosen, d):
        unit = flipped(me, chosen)
        source = in_ref.at[unit, beyond] if chosen else spare_in
        return pltpu.make_async_remote_copy(
            source, in_ref.at[unit, beyond], spare_send.at[number], spare_recv.at[number],
            device_id=(flipped(me, (d,)), col), device_id_type=MESH)

    def gather_in(number, chosen, d):
        unit = flipped(me, chosen + (d,))
        return pltpu.make_async_remote_copy(
            spare_in, in_ref.at[unit, beyond], spare_send.at[number], spare_recv.at[number],
            device_id=(flipped(me, (d,)), col), device_id_type=MESH)

    def scatter(number, chosen, d):
        return pltpu.make_async_remote_copy(
            held.at[flipped(me, chosen + (d,))], landed.at[number],
            spare_send.at[number], spare_recv.at[number],
            device_id=(flipped(me, (d,)), col), device_id_type=MESH)

    steps = []
    if spare_in is not None:
        for at in range(len(distances)):
            d = distances[-1 - at]
            steps.append((d, subsets(distances[len(distances) - at:])))
    if spare_out is not None:
        for at, d in enumerate(distances):
            steps.append((d, subsets(distances[at + 1:])))
    number = 0
    numbered = []
    for d, chosen in steps:
        numbered.append([(number + i, c, d) for i, c in enumerate(chosen)])
        number += len(chosen)

    def spare_start(step):
        for one in step:
            (gather if spare_in is not None else scatter)(*one).start()

    def spare_finish(step):
        for one in step:
            if spare_in is not None:
                gather_in(*one).wait()
            else:
                scatter(*one).wait()
                mine = flipped(me, one[1])
                added = held[mine].astype(jnp.float32) + landed[one[0]].astype(jnp.float32)
                held[mine] = added.astype(held.dtype)

    if with_sum:
        each(count - 1, lambda k: small(k).start())
    if with_spare:
        if not with_sum:
            keep_own.wait()
        spare_start(numbered[0])
    def sum_shard():
        each(count - 1, lambda k: small_in(k).wait())
        mid_part[...] = part_ref[...]

        def add_shard(k):
            mid_part[...] += shard_parts[shard_peer(k)]
        each(count - 1, add_shard)
        each(columns - 1, lambda k: tens(k).start())

    stages = max(len(numbered), 1)
    share = (count - 1) // stages
    each(share, lambda k: big(k).start())
    for at in range(1, stages):
        spare_finish(numbered[at - 1])
        spare_start(numbered[at])
        if with_sum and at == 1:
            sum_shard()
        more = share if at + 1 < stages else count - 1 - at * share
        each(more, lambda k, at=at: big(k + at * share).start())
    if with_spare:
        spare_finish(numbered[-1])
        if with_sum:
            keep_own.wait()
        else:
            spare_out[...] = held[me]
    if with_sum:
        if stages == 1:
            sum_shard()
        each(columns - 1, lambda k: tens_in(k).wait())
        total_ref[...] = mid_part[...]

        def add_tensor(k):
            total_ref[...] += tensor_parts[tensor_peer(k)]
        each(columns - 1, add_tensor)
    each(count - 1, lambda k: big_in(k).wait())
    own.wait()


def exchange(blocks, part, collective_id, mesh_sizes, spare=None):
    count, columns = mesh_sizes
    with_sum = part is not None
    any_spec = pl.BlockSpec(memory_space=pl.ANY)
    vmem_spec = pl.BlockSpec(memory_space=pltpu.VMEM)
    out_shape = [jax.ShapeDtypeStruct(blocks.shape, blocks.dtype)]
    scratch = [
        pltpu.SemaphoreType.DMA(()),
        pltpu.SemaphoreType.DMA((count,)),
        pltpu.SemaphoreType.DMA((count,)),
    ]
    operands = [blocks]
    in_specs = [any_spec]
    out_specs = [any_spec]
    if spare is not None and with_sum:
        operands.append(spare)
        in_specs.append(any_spec)
    if spare is not None and not with_sum:
        out_shape.append(jax.ShapeDtypeStruct(spare.shape, spare.dtype))
        out_specs.append(vmem_spec)
    if with_sum:
        out_shape.append(jax.ShapeDtypeStruct(part.shape, part.dtype))
        out_specs.append(vmem_spec)
        in_specs.append(vmem_spec)
        operands.append(part)
        scratch = [
            pltpu.VMEM((count,) + part.shape, part.dtype),
            pltpu.VMEM(part.shape, part.dtype),
            pltpu.VMEM((columns,) + part.shape, part.dtype),
        ] + scratch + [
            pltpu.SemaphoreType.DMA((count,)),
            pltpu.SemaphoreType.DMA((count,)),
            pltpu.SemaphoreType.DMA((columns,)),
            pltpu.SemaphoreType.DMA((columns,)),
        ]
    if spare is not None:
        scratch = scratch + [
            pltpu.SemaphoreType.DMA(()),
            pltpu.SemaphoreType.DMA((count,)),
            pltpu.SemaphoreType.DMA((count,)),
        ]
        if not with_sum:
            scratch = scratch + [
                pltpu.VMEM((count,) + spare.shape, spare.dtype),
                pltpu.VMEM((count,) + spare.shape, spare.dtype),
            ]
    spare_rows = 0 if spare is None else spare.shape[0]
    return pl.pallas_call(
        functools.partial(exchange_kernel, with_sum, spare_rows),
        out_shape=out_shape,
        in_specs=in_specs,
        out_specs=out_specs,
        scratch_shapes=scratch,
        compiler_params=pltpu.CompilerParams(
            collective_id=collective_id, has_side_effects=True
        ),
    )(*operands)


def adam_update(gradient, clip_scale, limit, weight_old, first_old, second_old, average_old):
    lane = lax.broadcasted_iota(jnp.int32, gradient.shape, 1)
    live = lane < limit
    keep = lane >= jnp.where(limit < 0, gradient.shape[1], 0)
    clipped = gradient * clip_scale
    first_new = BETA_ONE * first_old + (1.0 - BETA_ONE) * clipped
    second_new = BETA_TWO * second_old + (1.0 - BETA_TWO) * clipped * clipped
    update = (first_new * (1.0 / (1.0 - BETA_ONE**STEP))) / (
        jnp.sqrt(second_new * (1.0 / (1.0 - BETA_TWO**STEP))) + ADAM_EPS
    )
    weight_new = weight_old - LEARN_RATE * (update + WEIGHT_DECAY * weight_old)
    average_new = AVERAGE_DECAY * average_old + (1.0 - AVERAGE_DECAY) * weight_new
    pairs = ((weight_new, weight_old), (first_new, first_old), (second_new, second_old),
             (average_new, average_old))
    return [jnp.where(keep, jnp.where(live, new, old), 0.0) for new, old in pairs]


def picker(rows, columns, shift=0):
    row = lax.broadcasted_iota(jnp.int32, (rows, columns), 0)
    column = lax.broadcasted_iota(jnp.int32, (rows, columns), 1)
    return (row + shift == column).astype(jnp.bfloat16)


def turned(pick, block):
    return lax.dot_general(
        pick, block, (((1,), (1,)), ((), ())), preferred_element_type=jnp.float32
    )


def adam_kernel(max_norm, part_rows, limit_ref, total_ref, grad_ref, *refs):
    old_refs, weight_out, new_refs = refs[:4], refs[4], refs[5:]
    per_step, columns, slab_rows = new_refs[0].shape
    total = total_ref[0:1, :]
    clip_scale = jnp.minimum(1.0, max_norm / (jnp.sqrt(total) + 1e-06))

    def advance(slot, window, gradient):
        limit = limit_ref[pl.program_id(0) * per_step + slot]
        results = adam_update(
            gradient, clip_scale, limit, *[ref[slot, window, :] for ref in old_refs]
        )
        for ref, value in zip(new_refs, results):
            ref[slot, window, :] = value
        return results[0].astype(jnp.bfloat16)

    eye = picker(slab_rows, slab_rows)
    if part_rows is None:
        for slot in range(per_step):
            weight = advance(slot, pl.ds(0, columns),
                             turned(picker(columns, columns), grad_ref[slot]))
            weight_out[slot] = turned(eye, weight).astype(jnp.bfloat16)
        return

    rest = columns - LANES
    share = rest // 3

    def packed(index):
        rows = pl.ds(PLACES[index] * part_rows, part_rows)
        return grad_ref[:, rows, :].reshape(slab_rows, LANES)

    def send(index, weight):
        rows = pl.ds(PLACES[index] * part_rows, part_rows)
        block = turned(eye, weight).astype(jnp.bfloat16)
        weight_out[:, rows, :] = block.reshape(-1, part_rows, LANES)

    main_pick = picker(LANES, LANES)
    rest_pick = picker(rest, LANES)
    share_pick = picker(share, LANES, rest)
    rests = []
    for slot in range(4):
        send(slot, advance(slot, pl.ds(0, LANES), turned(main_pick, packed(slot))))
        if slot < 3:
            gradient = turned(rest_pick, packed(4 + slot))
        else:
            gradient = jnp.concatenate(
                [turned(share_pick, packed(4 + k)) for k in range(3)], axis=0
            )
        rests.append(advance(slot, pl.ds(LANES, rest), gradient))
    for k in range(3):
        piece = rests[3][k * share:(k + 1) * share]
        send(4 + k, jnp.concatenate([rests[k], piece], axis=0))


def adam(limits, total, arrived, master, moment1, moment2, average, max_norm, part_rows):
    capacity, columns, slab_rows = master.shape
    per_step = 1 if part_rows is None else 4
    state = pl.BlockSpec((per_step, columns, slab_rows), lambda s, _: (s, 0, 0))
    if part_rows is None:
        rows = pl.BlockSpec((per_step, slab_rows, columns), lambda s, _: (s, 0, 0))
    else:
        rows = pl.BlockSpec(
            (slab_rows // part_rows, 7 * part_rows, LANES), lambda s, _: (0, s, 0)
        )
    whole = pl.BlockSpec(total.shape, lambda s, _: (0, 0))
    return pl.pallas_call(
        functools.partial(adam_kernel, max_norm, part_rows),
        grid_spec=pltpu.PrefetchScalarGridSpec(
            num_scalar_prefetch=1,
            grid=(capacity // per_step,),
            in_specs=[whole, rows, state, state, state, state],
            out_specs=[rows, state, state, state, state],
        ),
        out_shape=[jax.ShapeDtypeStruct(arrived.shape, jnp.bfloat16)]
        + [jax.ShapeDtypeStruct(master.shape, jnp.float32)] * 4,
        compiler_params=pltpu.CompilerParams(vmem_limit_bytes=60 << 20),
    )(limits, total, arrived, master, moment1, moment2, average)


GROUP = 4
GRAD_CUTS = (1, 3)
EARLY = 1
WEIGHT_CUTS = (1, 3)
LATE = 1
TILES = 7


def batches(groups, cuts):
    cuts = sorted({0, groups, *[min(c, groups) for c in cuts]})
    return [list(range(a, b)) for a, b in zip(cuts, cuts[1:])]


def grad_batches(groups):
    first, *later = batches(groups - 1, GRAD_CUTS)
    return [first, [groups - 1], *later]


def work_order(groups):
    order = list(range(groups - 1))
    order.insert(min(EARLY, groups - 1), groups - 1)
    return order


def slot_table(owner, owner_count):
    slab_count = owner.shape[1]
    wide = (owner_count, slab_count)
    hit = owner == lax.broadcasted_iota(jnp.int32, wide, 0)
    earlier = lax.broadcasted_iota(jnp.int32, (slab_count, slab_count), 0) < (
        lax.broadcasted_iota(jnp.int32, (slab_count, slab_count), 1)
    )
    ranks = jnp.dot(
        hit.astype(jnp.bfloat16), earlier.astype(jnp.bfloat16), preferred_element_type=jnp.float32
    )
    rank = jnp.sum(jnp.where(hit, ranks, 0.0), axis=0, keepdims=True).astype(jnp.int32)
    at_slot = rank == lax.broadcasted_iota(jnp.int32, (LANES, slab_count), 0)
    number = lax.broadcasted_iota(jnp.int32, wide, 1) + 1
    marked = lax.dot_general(
        jnp.where(hit, number, 0).astype(jnp.float32).astype(jnp.bfloat16),
        at_slot.astype(jnp.bfloat16),
        (((1,), (1,)), ((), ())), preferred_element_type=jnp.float32,
    )
    return marked.astype(jnp.int32) - 1


def step_kernel(max_norm, owner_hbm, counts_hbm, grad_hbm, *refs):
    old_hbm, refs = refs[:4], refs[4:]
    returned, spare_out, states, table_ref, refs = refs[0], refs[1], refs[2:6], refs[6], refs[7:]
    slab_ref, refs = refs[0], refs[1:]
    owner_ref, counts_ref, owner_sem, counts_sem, refs = refs[:4] + (refs[4:],)
    owner_load = pltpu.make_async_copy(owner_hbm, owner_ref, owner_sem)
    owner_load.start()
    counts_load = pltpu.make_async_copy(counts_hbm, counts_ref, counts_sem)
    counts_load.start()
    grad_ref, packed_ref, part_ref, refs = refs[:3] + (refs[3:],)
    arrived, weights, shard_parts, mid_part, tensor_parts, held, landed, refs = refs[:7] + (refs[7:],)
    (grad_sem, table_sem, state_sem, own_sem, back_sem, small_send, small_recv, tens_send, tens_recv,
     grad_send, grad_recv, weight_send, weight_recv, gather_send, gather_recv,
     scatter_send, scatter_recv) = refs
    count = lax.axis_size("shard")
    columns = lax.axis_size("tensor")
    me = lax.axis_index("shard")
    col = lax.axis_index("tensor")
    capacity, width, slab_rows = states[0].shape
    part_rows = slab_rows // count
    groups = capacity // GROUP
    group_rows = TILES * part_rows
    spare_rows = spare_out.shape[0]
    slab_count = grad_ref.shape[0]
    emb = counts_ref.shape[0]
    layer_slabs = slab_count - emb
    rest = width - LANES
    share = rest // 3
    direct_rows = packed_ref.shape[1] - spare_rows
    last_rows = direct_rows - (groups - 1) * group_rows
    direct = pl.ds(0, direct_rows)
    beyond = pl.ds(direct_rows, spare_rows)
    last = groups - 1
    weight_parts = batches(groups, WEIGHT_CUTS)
    grad_parts = grad_batches(groups)
    order = work_order(groups)

    def each(total, body):
        def step(k, carry):
            body(k)
            return carry
        lax.fori_loop(0, total, step, 0)

    def shard_peer(k):
        return lax.rem(me + peer_of(k, count), count)

    def tensor_peer(k):
        return lax.rem(col + k + 1, columns)

    def late_peer(k):
        half, front = count // 2, count // 4
        own = jnp.where(me >= half, me, jnp.where(me < front, me, me + half))
        at = jnp.where(k >= own, k + 1, k)
        near = jnp.where(at < front, at, jnp.where(at < front + half, at - front + half, at - half))
        return jnp.where(me >= half, at, near)

    fetch = pltpu.make_async_copy(grad_hbm, grad_ref, grad_sem)
    fetch.start()
    barrier = pltpu.get_barrier_semaphore()
    each(count - 1, lambda k: pl.semaphore_signal(
        barrier, inc=1, device_id=(shard_peer(k), col), device_id_type=MESH))
    each(columns - 1, lambda k: pl.semaphore_signal(
        barrier, inc=1, device_id=(me, tensor_peer(k)), device_id_type=MESH))
    owner_load.wait()
    table_ref[...] = slot_table(owner_ref[...], count)
    tabled = pltpu.make_async_copy(table_ref, slab_ref, table_sem)
    tabled.start()
    counts_load.wait()
    tabled.wait()
    fetch.wait()

    def pack(target, unit, holder, group, tiles, first):
        for j in range(GROUP):
            slab = jnp.clip(slab_ref[holder, group * GROUP + j], 0, slab_count - 1)

            def rows_of(index):
                start = (PLACES[index] - first) * part_rows
                if first == 0:
                    start = group * group_rows + start
                return pl.ds(start, part_rows)
            if PLACES[j] in tiles:
                target[unit, rows_of(j), :] = grad_ref[slab, :, 0:LANES]
            if j < 3:
                if PLACES[4 + j] in tiles:
                    target[unit, rows_of(4 + j), 0:rest] = grad_ref[slab, :, LANES:width]
            else:
                for k in range(3):
                    if PLACES[4 + k] in tiles:
                        begin = LANES + k * share
                        target[unit, rows_of(4 + k), rest:LANES] = (
                            grad_ref[slab, :, begin:begin + share]
                        )

    def tiles_of(group):
        return range(TILES) if group < last else range(last_rows // part_rows)

    def pack_group(group):
        each(count, lambda p: pack(packed_ref, p, p, group, tiles_of(group), 0))

    def small(k, sender):
        peer = shard_peer(k)
        slot = me if sender else peer
        return pltpu.make_async_remote_copy(
            part_ref, shard_parts.at[slot], small_send.at[peer], small_recv.at[slot],
            device_id=(peer, col), device_id_type=MESH)

    def tens(k, sender):
        peer = tensor_peer(k)
        slot = col if sender else peer
        return pltpu.make_async_remote_copy(
            mid_part, tensor_parts.at[slot], tens_send.at[peer], tens_recv.at[slot],
            device_id=(me, peer), device_id_type=MESH)

    def block(parts, source, target, send, recv, peer, number, sender):
        slot = me if sender else peer
        first = parts[number][0] * group_rows
        end = direct_rows if parts[number][-1] == last else (parts[number][-1] + 1) * group_rows
        window = pl.ds(first, end - first)
        return pltpu.make_async_remote_copy(
            source.at[peer, window], target.at[slot, window],
            send.at[number, peer], recv.at[number, slot],
            device_id=(peer, col), device_id_type=MESH)

    def grad_block(k, number, sender):
        return block(
            grad_parts, packed_ref, arrived, grad_send, grad_recv, shard_peer(k), number, sender
        )

    def weight_block(k, number, sender):
        peer = late_peer(k) if number >= LATE else shard_peer(k)
        return block(
            weight_parts, weights, returned, weight_send, weight_recv, peer, number, sender
        )

    distances = []
    while 2 ** len(distances) < count:
        distances.append(2 ** len(distances))

    def numbered(pairs):
        found, number = [], 0
        for d, chosen in pairs:
            found.append([(number + i, c, d) for i, c in enumerate(chosen)])
            number += len(chosen)
        return found
    gather_steps = numbered([
        (distances[-1 - at], subsets(distances[len(distances) - at:]))
        for at in range(len(distances))
    ])
    scatter_steps = numbered([
        (d, subsets(distances[at + 1:])) for at, d in enumerate(distances)
    ])

    def gather(number, chosen, d, sender):
        unit = flipped(me, chosen if sender else chosen + (d,))
        return pltpu.make_async_remote_copy(
            arrived.at[unit, beyond], arrived.at[unit, beyond], gather_send.at[number], gather_recv.at[number],
            device_id=(flipped(me, (d,)), col), device_id_type=MESH)

    def scatter(number, chosen, d):
        return pltpu.make_async_remote_copy(
            held.at[flipped(me, chosen + (d,))], landed.at[number],
            scatter_send.at[number], scatter_recv.at[number],
            device_id=(flipped(me, (d,)), col), device_id_type=MESH)

    def gather_start(at):
        for one in gather_steps[at]:
            gather(*one, True).start()

    def gather_finish(at):
        for one in gather_steps[at]:
            gather(*one, True).wait_send()
            gather(*one, False).wait_recv()

    def scatter_start(at):
        for one in scatter_steps[at]:
            scatter(*one).start()

    def scatter_finish(at):
        for one in scatter_steps[at]:
            scatter(*one).wait()
            mine = flipped(me, one[1])
            added = held[mine].astype(jnp.float32) + landed[one[0]].astype(jnp.float32)
            held[mine] = added.astype(held.dtype)

    pl.semaphore_wait(barrier, count + columns - 2)

    def pack_first(k):
        peer = shard_peer(k)
        for g in grad_parts[0]:
            pack(packed_ref, peer, peer, g, tiles_of(g), 0)
        grad_block(k, 0, True).start()
    each(count - 1, pack_first)
    for g in grad_parts[0]:
        pack(packed_ref, me, me, g, tiles_of(g), 0)

    loads = [pltpu.make_async_copy(old, new, state_sem.at[i])
             for i, (old, new) in enumerate(zip(old_hbm, states))]
    for load in loads:
        load.start()

    fullest = 0
    for o in range(1, count):
        fullest = jnp.where(slab_ref[o, capacity - SPARE_SLOTS] >= 0, o, fullest)
    spare_tiles = range(last_rows // part_rows, TILES)
    pack(held, 0, fullest, last, spare_tiles, last_rows // part_rows)
    arrived[me, beyond, :] = held[0]
    gather_start(0)

    def squares(i, carry):
        values = grad_ref[i].astype(jnp.float32)
        return carry + values * values
    acc = lax.fori_loop(
        0, layer_slabs, squares, jnp.zeros((part_rows, width), jnp.float32), unroll=10
    )
    row = lax.broadcasted_iota(jnp.int32, (part_rows, width), 0) + me * part_rows
    for e in range(emb):
        values = grad_ref[layer_slabs + e].astype(jnp.float32)
        acc += jnp.where(row < counts_ref[e], values * values, 0.0)
    part_ref[...] = jnp.broadcast_to(jnp.sum(acc, keepdims=True), part_ref.shape)
    each(count - 1, lambda k: small(k, True).start())

    for number in range(1, len(grad_parts)):
        for g in grad_parts[number]:
            pack_group(g)
        each(count - 1, lambda k, number=number: grad_block(k, number, True).start())
    own = pltpu.make_async_copy(packed_ref.at[me, direct], arrived.at[me, direct], own_sem)
    own.start()

    def add_shard(k):
        small(k, False).wait()
        mid_part[...] += shard_parts[shard_peer(k)]

    mid_part[...] = part_ref[...]
    each(count - 1, add_shard)
    each(columns - 1, lambda k: tens(k, True).start())
    gather_finish(0)
    gather_start(1)
    own.wait()
    for load in loads:
        load.wait()
    total = mid_part[0:1, :]
    each(columns - 1, lambda k: tens(k, False).wait())
    for k in range(columns - 1):
        total = total + tensor_parts[tensor_peer(k), 0:1, :]
    clip_scale = jnp.minimum(1.0, max_norm / (jnp.sqrt(total) + 1e-06))
    gather_finish(1)
    gather_start(2)

    eye = picker(slab_rows, slab_rows)

    def compute(group):
        base = group * group_rows

        def rows_of(index):
            return pl.ds(pl.multiple_of(base + PLACES[index] * part_rows, part_rows), part_rows)

        def advance(slot, window, gradient):
            place = group * GROUP + slot
            slab = slab_ref[me, place]
            live = counts_ref[jnp.clip(slab - layer_slabs, 0, emb - 1)]
            limit = jnp.where(slab < 0, -1, jnp.where(slab < layer_slabs, slab_rows, live))
            results = adam_update(
                gradient, clip_scale, limit, *[ref[place, window, :] for ref in states]
            )
            for ref, value in zip(states, results):
                ref[place, window, :] = value
            return results[0].astype(jnp.bfloat16)

        def packed(index):
            return arrived[:, rows_of(index), :].reshape(slab_rows, LANES)

        def send(index, weight):
            done = turned(eye, weight).astype(jnp.bfloat16)
            weights[:, rows_of(index), :] = done.reshape(count, part_rows, LANES)

        rest_pick = picker(rest, LANES)
        share_pick = picker(share, LANES, rest)
        rests = []
        for slot in range(GROUP):
            send(slot, advance(slot, pl.ds(0, LANES), turned(eye, packed(slot))))
            if slot < 3:
                gradient = turned(rest_pick, packed(4 + slot))
            else:
                gradient = jnp.concatenate(
                    [turned(share_pick, packed(4 + k)) for k in range(3)], axis=0
                )
            rests.append(advance(slot, pl.ds(LANES, rest), gradient))
        for k in range(3):
            piece = rests[3][k * share:(k + 1) * share]
            send(4 + k, jnp.concatenate([rests[k], piece], axis=0))

    back = pltpu.make_async_copy(weights.at[me, direct], returned.at[me, direct], back_sem)

    def turn(t, carry):
        group = 0
        for at, g in enumerate(order):
            group = jnp.where(t == at, g, group)
        for number, batch in enumerate(grad_parts):
            @pl.when(t == min(order.index(g) for g in batch))
            def _():
                each(count - 1, lambda k: grad_block(k, number, False).wait())

        @pl.when(group == last)
        def _():
            gather_finish(2)

        compute(group)

        @pl.when(group == last)
        def _():
            held[...] = weights[:, beyond, :]
            scatter_start(0)
        for number, batch in enumerate(weight_parts):
            @pl.when(t == max(order.index(g) for g in batch))
            def _():
                if number + 1 < len(weight_parts):
                    each(count - 1, lambda k: weight_block(k, number, True).start())
                else:
                    each(1, lambda k: weight_block(k, number, True).start())
        for at in range(1, len(distances)):
            @pl.when(t == groups - len(distances) + at)
            def _():
                scatter_finish(at - 1)
                scatter_start(at)
        return carry

    lax.fori_loop(0, groups, turn, 0)
    last_part = len(weight_parts) - 1
    each(1, lambda k: weight_block(k, last_part, True).wait_send())
    each(count - 1 - 1, lambda k: weight_block(k + 1, last_part, True).start())
    back.start()
    scatter_finish(len(distances) - 1)
    spare_out[...] = held[me]
    for number in range(len(weight_parts) - 1):
        each(count - 1, lambda k, number=number: weight_block(k, number, False).wait())
    final = len(weight_parts) - 1
    each(count - 1, lambda k: weight_block(k, final, False).wait_recv())
    each(count - 1 - 1, lambda k: weight_block(k + 1, final, False).wait_send())
    back.wait()


def step(owner, counts, grad, states, max_norm, mesh_sizes):
    count, columns = mesh_sizes
    capacity, width, slab_rows = states[0].shape
    part_rows = grad.shape[1]
    groups = capacity // GROUP
    grads = (len(grad_batches(groups)), count)
    sends = (len(batches(groups, WEIGHT_CUTS)), count)
    packed = (count, groups * TILES * part_rows, LANES)
    spare = (SPARE_BLOCKS * part_rows, LANES)
    vmem = pl.BlockSpec(memory_space=pltpu.VMEM)
    hbm = pl.BlockSpec(memory_space=pltpu.HBM)
    dma = pltpu.SemaphoreType.DMA
    return pl.pallas_call(
        functools.partial(step_kernel, max_norm),
        in_specs=[hbm] * 7,
        out_specs=[vmem] * 7,
        out_shape=[pltpu.VMEM(packed, grad.dtype), pltpu.VMEM(spare, grad.dtype)]
        + [pltpu.VMEM(s.shape, s.dtype) for s in states]
        + [pltpu.VMEM((count, LANES), jnp.int32)],
        scratch_shapes=[
            pltpu.SMEM((count, LANES), jnp.int32),
            pltpu.VMEM(owner.shape, owner.dtype),
            pltpu.SMEM(counts.shape, counts.dtype),
            dma(()), dma(()),
            pltpu.VMEM(grad.shape, grad.dtype),
            pltpu.VMEM(packed, grad.dtype),
            pltpu.VMEM((1, LANES), jnp.float32),
            pltpu.VMEM(packed, grad.dtype),
            pltpu.VMEM(packed, grad.dtype),
            pltpu.VMEM((count, 1, LANES), jnp.float32),
            pltpu.VMEM((1, LANES), jnp.float32),
            pltpu.VMEM((columns, 1, LANES), jnp.float32),
            pltpu.VMEM((count,) + spare, grad.dtype),
            pltpu.VMEM((count,) + spare, grad.dtype),
            dma(()), dma(()), dma((4,)), dma(()), dma(()),
            dma((count,)), dma((count,)), dma((columns,)), dma((columns,)),
            dma(grads), dma(grads), dma(sends), dma(sends),
            dma((count,)), dma((count,)), dma((count,)), dma((count,)),
        ],
        compiler_params=pltpu.CompilerParams(
            collective_id=2, has_side_effects=True, vmem_limit_bytes=40 << 20
        ),
    )(owner, counts, grad, *states)


def unpack_kernel(capacity, table_ref, packed_ref, spare_ref, *refs):
    fresh, weight_hbm, kept, weight_ref, weight_sem, kept_sem, source_ref, source_sem = (
        refs[:4], refs[4], refs[5:9], refs[9], refs[10], refs[11], refs[12], refs[13]
    )
    load = pltpu.make_async_copy(table_ref, source_ref, source_sem)
    load.start()
    stores = [pltpu.make_async_copy(new, out, kept_sem.at[i])
              for i, (new, out) in enumerate(zip(fresh, kept))]
    for store in stores:
        store.start()
    load.wait()
    slab_count, part_rows, columns = weight_hbm.shape
    rest = columns - LANES
    share = rest // 3
    groups = capacity // 4

    def unpack(t, carry):
        p = t // groups
        g = t % groups
        base = g * (7 * part_rows)

        def piece(index):
            rows = pl.ds(pl.multiple_of(base + PLACES[index] * part_rows, part_rows), part_rows)
            return packed_ref[p, rows, :]
        blocks = [piece(index) for index in range(7)]
        for j in range(4):
            slab = source_ref[p, g * 4 + j]
            slab = jnp.where(slab < 0, slab_count, slab)
            weight_ref[slab, :, 0:LANES] = blocks[j]
            if j < 3:
                weight_ref[slab, :, LANES:columns] = blocks[4 + j][:, 0:rest]
            else:
                weight_ref[slab, :, LANES:columns] = jnp.concatenate(
                    [blocks[4 + k][:, rest:LANES] for k in range(3)], axis=1
                )
        return carry
    lax.fori_loop(0, packed_ref.shape[0] * groups, unpack, 0, unroll=2)
    fullest = 0
    for p in range(1, packed_ref.shape[0]):
        first_spare = source_ref[p, capacity - SPARE_SLOTS]
        fullest = jnp.where(first_spare >= 0, p, fullest)
    last = (groups - 1) * (7 * part_rows)
    spare = [None, None] + [
        spare_ref[pl.ds(k * part_rows, part_rows), :] for k in range(SPARE_BLOCKS)
    ]
    spare[1] = packed_ref[fullest, pl.ds(last + part_rows, part_rows), :]
    for j in range(1, 4):
        slab = source_ref[fullest, capacity - 4 + j]
        slab = jnp.where(slab < 0, slab_count, slab)
        weight_ref[slab, :, 0:LANES] = spare[PLACES[j]]
        if j < 3:
            weight_ref[slab, :, LANES:columns] = spare[PLACES[4 + j]][:, 0:rest]
        else:
            weight_ref[slab, :, LANES:columns] = jnp.concatenate(
                [spare[PLACES[4 + k]][:, rest:LANES] for k in range(3)], axis=1
            )
    store = pltpu.make_async_copy(weight_ref.at[pl.ds(0, slab_count)], weight_hbm, weight_sem)
    store.start()
    store.wait()
    for store in stores:
        store.wait()


def unpack(source, packed, spare, states, weight_shape, capacity):
    slab_count, part_rows, columns = weight_shape
    vmem = pl.BlockSpec(memory_space=pltpu.VMEM)
    hbm = pl.BlockSpec(memory_space=pltpu.HBM)
    return pl.pallas_call(
        functools.partial(unpack_kernel, capacity),
        in_specs=[vmem] * 7,
        out_specs=[hbm] * 5,
        out_shape=[jax.ShapeDtypeStruct(weight_shape, packed.dtype)]
        + [jax.ShapeDtypeStruct(s.shape, s.dtype) for s in states],
        scratch_shapes=[
            pltpu.VMEM((slab_count + 1, part_rows, columns), packed.dtype),
            pltpu.SemaphoreType.DMA(()),
            pltpu.SemaphoreType.DMA((4,)),
            pltpu.SMEM(source.shape, source.dtype),
            pltpu.SemaphoreType.DMA(()),
        ],
        compiler_params=pltpu.CompilerParams(vmem_limit_bytes=40 << 20),
    )(source, packed, spare, *states)


def per_device(mesh_sizes, grad, owner, counts, master, moment1, moment2, average):
    owner_count = mesh_sizes[0]
    slab_count, part_rows, columns = grad.shape
    capacity = master.shape[0]
    slab_rows = part_rows * owner_count
    max_norm = 0.5 * math.sqrt(slab_count * slab_rows * D)
    layer_slabs = slab_count - counts.shape[0]
    self_index = lax.axis_index("shard")
    states = (master, moment1, moment2, average)

    if part_rows % 16 == 0 and capacity % 4 == 0 and (columns - LANES) * 4 == 3 * LANES and (
        owner_count & (owner_count - 1) == 0 and slab_count <= 256 and capacity <= LANES
    ):
        inputs = (owner.reshape(1, -1), counts, grad) + states
        owner, counts, grad, *states = [
            pltpu.with_memory_space_constraint(x, pltpu.HBM) for x in inputs
        ]
        returned, spare, *states, source = step(
            owner, counts, grad, states, max_norm, mesh_sizes
        )
        return tuple(unpack(source, returned, spare, states, grad.shape, capacity))

    full_counts = jnp.concatenate([jnp.full((layer_slabs,), slab_rows, jnp.int32), counts])
    row_index = self_index * part_rows + jnp.arange(part_rows, dtype=jnp.int32)
    train_live = row_index[None, :] < full_counts[:, None]
    values = grad.astype(jnp.float32)
    part = jnp.sum(jnp.where(train_live[:, :, None], values * values, 0.0))
    part = jnp.broadcast_to(part, (8, LANES))

    place, marked = slot_tables(owner, owner_count, capacity)
    source = jnp.maximum(marked - 1, 0)
    own_marked = lax.dynamic_slice_in_dim(marked, self_index * capacity, capacity)
    own_live = jnp.take(full_counts, jnp.maximum(own_marked - 1, 0), mode="clip")
    limits = jnp.where(own_marked > 0, own_live, -1)

    outgoing = jnp.take(grad, source, axis=0, mode="clip")
    outgoing = outgoing.reshape(owner_count, capacity * part_rows, columns)
    arrived, total = exchange(outgoing, part, 0, mesh_sizes)
    arrived = arrived.reshape(owner_count, capacity, part_rows, columns)
    arrived = arrived.transpose(1, 0, 2, 3).reshape(capacity, slab_rows, columns)
    weights, *new_states = adam(limits, total, arrived, *states, max_norm, None)
    weights = weights.reshape(capacity, owner_count, part_rows, columns)
    weights = weights.transpose(1, 0, 2, 3)
    weights = weights.reshape(owner_count, capacity * part_rows, columns)
    (returned,) = exchange(weights, None, 1, mesh_sizes)
    returned = returned.reshape(owner_count * capacity, part_rows, columns)
    new_weight = jnp.take(returned, place, axis=0, mode="clip")
    return (new_weight, *new_states)


def solution(mesh):
    sizes = (mesh.shape["shard"], mesh.shape["tensor"])
    return jax.shard_map(
        functools.partial(per_device, sizes),
        mesh=mesh,
        in_specs=(
            P(None, "shard", "tensor"),
            P(),
            P(),
            P("shard", "tensor", None),
            P("shard", "tensor", None),
            P("shard", "tensor", None),
            P("shard", "tensor", None),
        ),
        out_specs=(
            P(None, "shard", "tensor"),
            P("shard", "tensor", None),
            P("shard", "tensor", None),
            P("shard", "tensor", None),
            P("shard", "tensor", None),
        ),
        check_vma=False,
    )
```

```python
import functools
import math

import jax
import jax.numpy as jnp
from jax import lax
from jax.experimental import pallas as pl
from jax.experimental.pallas import tpu as pltpu
from jax.sharding import PartitionSpec as P

D = 896
STEP = 20


BETA_ONE = 0.9
BETA_TWO = 0.95
ADAM_EPS = 1e-08
LEARN_RATE = 0.02
WEIGHT_DECAY = 0.1
AVERAGE_DECAY = 0.99

LANES = 128
PLACES = (0, 2, 3, 4, 1, 5, 6)
SPARE_SLOTS = 3
SPARE_BLOCKS = 5
MESH = pl.DeviceIdType.MESH


def slot_tables(owner, owner_count, capacity):
    slab_count = owner.shape[0]
    owner_ids = jnp.arange(owner_count, dtype=jnp.int32)
    slabs = jnp.arange(slab_count, dtype=jnp.int32)
    before = (owner[:, None] == owner[None, :]) & (slabs[None, :] < slabs[:, None])
    slot_rank = jnp.sum(before.astype(jnp.int32), axis=1)
    place = owner * capacity + slot_rank
    slot_ids = jnp.arange(owner_count * capacity, dtype=jnp.int32)
    matched = place[None, :] == slot_ids[:, None]
    marked = jnp.sum(jnp.where(matched, slabs[None, :] + 1, 0), axis=1)
    return (place, marked)


def peer_of(step, count):
    half = count // 2
    away = (step + 1) // 2
    return jnp.where(step % 2 == 1, half - away, half + away)


def subsets(distances):
    found = [()]
    for d in distances:
        found = found + [c + (d,) for c in found]
    return found


def flipped(index, distances):
    for d in distances:
        index = index + d * (1 - 2 * lax.rem(index // d, 2))
    return index


def exchange_kernel(with_sum, with_spare, *refs):
    refs = list(refs)
    out_ref = refs.pop(0)
    spare_in = refs.pop(0) if with_spare and with_sum else None
    part_ref = refs.pop(0) if with_sum else None
    in_ref = refs.pop(0)
    spare_out = refs.pop(0) if with_spare and not with_sum else None
    total_ref = refs.pop(0) if with_sum else None
    if with_sum:
        shard_parts, mid_part, tensor_parts = refs[:3]
        refs = refs[3:]
    local_sem, send_sem, recv_sem = refs[:3]
    refs = refs[3:]
    if with_sum:
        small_send, small_recv, tens_send, tens_recv = refs[:4]
        refs = refs[4:]
    if with_spare:
        spare_local, spare_send, spare_recv = refs[:3]
        refs = refs[3:]
        if not with_sum:
            held, landed = refs
    count = lax.axis_size("shard")
    columns = lax.axis_size("tensor")
    me = lax.axis_index("shard")
    col = lax.axis_index("tensor")

    def each(total, body):
        def step(k, carry):
            body(k)
            return carry
        lax.fori_loop(0, total, step, 0)

    def shard_peer(k):
        return lax.rem(me + peer_of(k, count), count)

    def tensor_peer(k):
        return lax.rem(col + k + 1, columns)

    rows = out_ref.shape[1]
    spare_rows = with_spare
    direct = pl.ds(0, rows - spare_rows)
    beyond = pl.ds(rows - spare_rows, spare_rows)
    distances = []
    while with_spare and 2 ** len(distances) < count:
        distances.append(2 ** len(distances))
    if spare_in is not None:
        keep_own = pltpu.make_async_copy(spare_in, in_ref.at[me, beyond], spare_local)
        keep_own.start()
    if spare_out is not None:
        keep_own = pltpu.make_async_copy(out_ref.at[:, beyond], held, spare_local)
        keep_own.start()
    own = pltpu.make_async_copy(
        out_ref.at[me, direct], in_ref.at[me, direct], local_sem
    )
    own.start()
    barrier = pltpu.get_barrier_semaphore()
    each(count - 1, lambda k: pl.semaphore_signal(
        barrier, inc=1, device_id=(shard_peer(k), col), device_id_type=MESH))
    greeted = count - 1
    if with_sum:
        each(columns - 1, lambda k: pl.semaphore_signal(
            barrier, inc=1, device_id=(me, tensor_peer(k)), device_id_type=MESH))
        greeted += columns - 1
    pl.semaphore_wait(barrier, greeted)

    def small(k):
        peer = shard_peer(k)
        return pltpu.make_async_remote_copy(
            part_ref, shard_parts.at[me], small_send.at[peer], small_recv.at[me],
            device_id=(peer, col), device_id_type=MESH)

    def small_in(k):
        peer = shard_peer(k)
        return pltpu.make_async_remote_copy(
            part_ref, shard_parts.at[peer], small_send.at[peer], small_recv.at[peer],
            device_id=(peer, col), device_id_type=MESH)

    def tens(k):
        peer = tensor_peer(k)
        return pltpu.make_async_remote_copy(
            mid_part, tensor_parts.at[col], tens_send.at[peer], tens_recv.at[col],
            device_id=(me, peer), device_id_type=MESH)

    def tens_in(k):
        peer = tensor_peer(k)
        return pltpu.make_async_remote_copy(
            mid_part, tensor_parts.at[peer], tens_send.at[peer], tens_recv.at[peer],
            device_id=(me, peer), device_id_type=MESH)

    def big(k):
        peer = shard_peer(k)
        return pltpu.make_async_remote_copy(
            out_ref.at[peer, direct], in_ref.at[me, direct], send_sem.at[peer], recv_sem.at[me],
            device_id=(peer, col), device_id_type=MESH)

    def big_in(k):
        peer = shard_peer(k)
        return pltpu.make_async_remote_copy(
            out_ref.at[peer, direct], in_ref.at[peer, direct], send_sem.at[peer], recv_sem.at[peer],
            device_id=(peer, col), device_id_type=MESH)

    def gather(number, chosen, d):
        unit = flipped(me, chosen)
        source = in_ref.at[unit, beyond] if chosen else spare_in
        return pltpu.make_async_remote_copy(
            source, in_ref.at[unit, beyond], spare_send.at[number], spare_recv.at[number],
            device_id=(flipped(me, (d,)), col), device_id_type=MESH)

    def gather_in(number, chosen, d):
        unit = flipped(me, chosen + (d,))
        return pltpu.make_async_remote_copy(
            spare_in, in_ref.at[unit, beyond], spare_send.at[number], spare_recv.at[number],
            device_id=(flipped(me, (d,)), col), device_id_type=MESH)

    def scatter(number, chosen, d):
        return pltpu.make_async_remote_copy(
            held.at[flipped(me, chosen + (d,))], landed.at[number],
            spare_send.at[number], spare_recv.at[number],
            device_id=(flipped(me, (d,)), col), device_id_type=MESH)

    steps = []
    if spare_in is not None:
        for at in range(len(distances)):
            d = distances[-1 - at]
            steps.append((d, subsets(distances[len(distances) - at:])))
    if spare_out is not None:
        for at, d in enumerate(distances):
            steps.append((d, subsets(distances[at + 1:])))
    number = 0
    numbered = []
    for d, chosen in steps:
        numbered.append([(number + i, c, d) for i, c in enumerate(chosen)])
        number += len(chosen)

    def spare_start(step):
        for one in step:
            (gather if spare_in is not None else scatter)(*one).start()

    def spare_finish(step):
        for one in step:
            if spare_in is not None:
                gather_in(*one).wait()
            else:
                scatter(*one).wait()
                mine = flipped(me, one[1])
                added = held[mine].astype(jnp.float32) + landed[one[0]].astype(jnp.float32)
                held[mine] = added.astype(held.dtype)

    if with_sum:
        each(count - 1, lambda k: small(k).start())
    if with_spare:
        if not with_sum:
            keep_own.wait()
        spare_start(numbered[0])
    def sum_shard():
        each(count - 1, lambda k: small_in(k).wait())
        mid_part[...] = part_ref[...]

        def add_shard(k):
            mid_part[...] += shard_parts[shard_peer(k)]
        each(count - 1, add_shard)
        each(columns - 1, lambda k: tens(k).start())

    stages = max(len(numbered), 1)
    share = (count - 1) // stages
    each(share, lambda k: big(k).start())
    for at in range(1, stages):
        spare_finish(numbered[at - 1])
        spare_start(numbered[at])
        if with_sum and at == 1:
            sum_shard()
        more = share if at + 1 < stages else count - 1 - at * share
        each(more, lambda k, at=at: big(k + at * share).start())
    if with_spare:
        spare_finish(numbered[-1])
        if with_sum:
            keep_own.wait()
        else:
            spare_out[...] = held[me]
    if with_sum:
        if stages == 1:
            sum_shard()
        each(columns - 1, lambda k: tens_in(k).wait())
        total_ref[...] = mid_part[...]

        def add_tensor(k):
            total_ref[...] += tensor_parts[tensor_peer(k)]
        each(columns - 1, add_tensor)
    each(count - 1, lambda k: big_in(k).wait())
    own.wait()


def exchange(blocks, part, collective_id, mesh_sizes, spare=None):
    count, columns = mesh_sizes
    with_sum = part is not None
    any_spec = pl.BlockSpec(memory_space=pl.ANY)
    vmem_spec = pl.BlockSpec(memory_space=pltpu.VMEM)
    out_shape = [jax.ShapeDtypeStruct(blocks.shape, blocks.dtype)]
    scratch = [
        pltpu.SemaphoreType.DMA(()),
        pltpu.SemaphoreType.DMA((count,)),
        pltpu.SemaphoreType.DMA((count,)),
    ]
    operands = [blocks]
    in_specs = [any_spec]
    out_specs = [any_spec]
    if spare is not None and with_sum:
        operands.append(spare)
        in_specs.append(any_spec)
    if spare is not None and not with_sum:
        out_shape.append(jax.ShapeDtypeStruct(spare.shape, spare.dtype))
        out_specs.append(vmem_spec)
    if with_sum:
        out_shape.append(jax.ShapeDtypeStruct(part.shape, part.dtype))
        out_specs.append(vmem_spec)
        in_specs.append(vmem_spec)
        operands.append(part)
        scratch = [
            pltpu.VMEM((count,) + part.shape, part.dtype),
            pltpu.VMEM(part.shape, part.dtype),
            pltpu.VMEM((columns,) + part.shape, part.dtype),
        ] + scratch + [
            pltpu.SemaphoreType.DMA((count,)),
            pltpu.SemaphoreType.DMA((count,)),
            pltpu.SemaphoreType.DMA((columns,)),
            pltpu.SemaphoreType.DMA((columns,)),
        ]
    if spare is not None:
        scratch = scratch + [
            pltpu.SemaphoreType.DMA(()),
            pltpu.SemaphoreType.DMA((count,)),
            pltpu.SemaphoreType.DMA((count,)),
        ]
        if not with_sum:
            scratch = scratch + [
                pltpu.VMEM((count,) + spare.shape, spare.dtype),
                pltpu.VMEM((count,) + spare.shape, spare.dtype),
            ]
    spare_rows = 0 if spare is None else spare.shape[0]
    return pl.pallas_call(
        functools.partial(exchange_kernel, with_sum, spare_rows),
        out_shape=out_shape,
        in_specs=in_specs,
        out_specs=out_specs,
        scratch_shapes=scratch,
        compiler_params=pltpu.CompilerParams(
            collective_id=collective_id, has_side_effects=True
        ),
    )(*operands)


def adam_update(gradient, clip_scale, limit, weight_old, first_old, second_old, average_old):
    lane = lax.broadcasted_iota(jnp.int32, gradient.shape, 1)
    live = lane < limit
    keep = lane >= jnp.where(limit < 0, gradient.shape[1], 0)
    clipped = gradient * clip_scale
    first_new = BETA_ONE * first_old + (1.0 - BETA_ONE) * clipped
    second_new = BETA_TWO * second_old + (1.0 - BETA_TWO) * clipped * clipped
    update = (first_new * (1.0 / (1.0 - BETA_ONE**STEP))) / (
        jnp.sqrt(second_new * (1.0 / (1.0 - BETA_TWO**STEP))) + ADAM_EPS
    )
    weight_new = weight_old - LEARN_RATE * (update + WEIGHT_DECAY * weight_old)
    average_new = AVERAGE_DECAY * average_old + (1.0 - AVERAGE_DECAY) * weight_new
    pairs = ((weight_new, weight_old), (first_new, first_old), (second_new, second_old),
             (average_new, average_old))
    return [jnp.where(keep, jnp.where(live, new, old), 0.0) for new, old in pairs]


def picker(rows, columns, shift=0):
    row = lax.broadcasted_iota(jnp.int32, (rows, columns), 0)
    column = lax.broadcasted_iota(jnp.int32, (rows, columns), 1)
    return (row + shift == column).astype(jnp.bfloat16)


def turned(pick, block):
    return lax.dot_general(
        pick, block, (((1,), (1,)), ((), ())), preferred_element_type=jnp.float32
    )


def adam_kernel(max_norm, part_rows, limit_ref, total_ref, grad_ref, *refs):
    old_refs, weight_out, new_refs = refs[:4], refs[4], refs[5:]
    per_step, columns, slab_rows = new_refs[0].shape
    total = total_ref[0:1, :]
    clip_scale = jnp.minimum(1.0, max_norm / (jnp.sqrt(total) + 1e-06))

    def advance(slot, window, gradient):
        limit = limit_ref[pl.program_id(0) * per_step + slot]
        results = adam_update(
            gradient, clip_scale, limit, *[ref[slot, window, :] for ref in old_refs]
        )
        for ref, value in zip(new_refs, results):
            ref[slot, window, :] = value
        return results[0].astype(jnp.bfloat16)

    eye = picker(slab_rows, slab_rows)
    if part_rows is None:
        for slot in range(per_step):
            weight = advance(slot, pl.ds(0, columns),
                             turned(picker(columns, columns), grad_ref[slot]))
            weight_out[slot] = turned(eye, weight).astype(jnp.bfloat16)
        return

    rest = columns - LANES
    share = rest // 3

    def packed(index):
        rows = pl.ds(PLACES[index] * part_rows, part_rows)
        return grad_ref[:, rows, :].reshape(slab_rows, LANES)

    def send(index, weight):
        rows = pl.ds(PLACES[index] * part_rows, part_rows)
        block = turned(eye, weight).astype(jnp.bfloat16)
        weight_out[:, rows, :] = block.reshape(-1, part_rows, LANES)

    main_pick = picker(LANES, LANES)
    rest_pick = picker(rest, LANES)
    share_pick = picker(share, LANES, rest)
    rests = []
    for slot in range(4):
        send(slot, advance(slot, pl.ds(0, LANES), turned(main_pick, packed(slot))))
        if slot < 3:
            gradient = turned(rest_pick, packed(4 + slot))
        else:
            gradient = jnp.concatenate(
                [turned(share_pick, packed(4 + k)) for k in range(3)], axis=0
            )
        rests.append(advance(slot, pl.ds(LANES, rest), gradient))
    for k in range(3):
        piece = rests[3][k * share:(k + 1) * share]
        send(4 + k, jnp.concatenate([rests[k], piece], axis=0))


def adam(limits, total, arrived, master, moment1, moment2, average, max_norm, part_rows):
    capacity, columns, slab_rows = master.shape
    per_step = 1 if part_rows is None else 4
    state = pl.BlockSpec((per_step, columns, slab_rows), lambda s, _: (s, 0, 0))
    if part_rows is None:
        rows = pl.BlockSpec((per_step, slab_rows, columns), lambda s, _: (s, 0, 0))
    else:
        rows = pl.BlockSpec(
            (slab_rows // part_rows, 7 * part_rows, LANES), lambda s, _: (0, s, 0)
        )
    whole = pl.BlockSpec(total.shape, lambda s, _: (0, 0))
    return pl.pallas_call(
        functools.partial(adam_kernel, max_norm, part_rows),
        grid_spec=pltpu.PrefetchScalarGridSpec(
            num_scalar_prefetch=1,
            grid=(capacity // per_step,),
            in_specs=[whole, rows, state, state, state, state],
            out_specs=[rows, state, state, state, state],
        ),
        out_shape=[jax.ShapeDtypeStruct(arrived.shape, jnp.bfloat16)]
        + [jax.ShapeDtypeStruct(master.shape, jnp.float32)] * 4,
        compiler_params=pltpu.CompilerParams(vmem_limit_bytes=60 << 20),
    )(limits, total, arrived, master, moment1, moment2, average)


GROUP = 4
GRAD_CUTS = (1, 3)
EARLY = 1
WEIGHT_CUTS = (1, 3)
LATE = 1
TILES = 7


def batches(groups, cuts):
    cuts = sorted({0, groups, *[min(c, groups) for c in cuts]})
    return [list(range(a, b)) for a, b in zip(cuts, cuts[1:])]


def grad_batches(groups):
    first, *later = batches(groups - 1, GRAD_CUTS)
    return [first, [groups - 1], *later]


def work_order(groups):
    order = list(range(groups - 1))
    order.insert(min(EARLY, groups - 1), groups - 1)
    return order


def slot_table(owner, owner_count):
    slab_count = owner.shape[1]
    wide = (owner_count, slab_count)
    hit = owner == lax.broadcasted_iota(jnp.int32, wide, 0)
    earlier = lax.broadcasted_iota(jnp.int32, (slab_count, slab_count), 0) < (
        lax.broadcasted_iota(jnp.int32, (slab_count, slab_count), 1)
    )
    ranks = jnp.dot(
        hit.astype(jnp.bfloat16), earlier.astype(jnp.bfloat16), preferred_element_type=jnp.float32
    )
    rank = jnp.sum(jnp.where(hit, ranks, 0.0), axis=0, keepdims=True).astype(jnp.int32)
    at_slot = rank == lax.broadcasted_iota(jnp.int32, (LANES, slab_count), 0)
    number = lax.broadcasted_iota(jnp.int32, wide, 1) + 1
    marked = lax.dot_general(
        jnp.where(hit, number, 0).astype(jnp.float32).astype(jnp.bfloat16),
        at_slot.astype(jnp.bfloat16),
        (((1,), (1,)), ((), ())), preferred_element_type=jnp.float32,
    )
    return marked.astype(jnp.int32) - 1


def step_kernel(max_norm, owner_hbm, counts_hbm, grad_hbm, *refs):
    old_hbm, refs = refs[:4], refs[4:]
    returned, spare_out, states, table_ref, refs = refs[0], refs[1], refs[2:6], refs[6], refs[7:]
    slab_ref, refs = refs[0], refs[1:]
    owner_ref, counts_ref, owner_sem, counts_sem, refs = refs[:4] + (refs[4:],)
    owner_load = pltpu.make_async_copy(owner_hbm, owner_ref, owner_sem)
    owner_load.start()
    counts_load = pltpu.make_async_copy(counts_hbm, counts_ref, counts_sem)
    counts_load.start()
    grad_ref, packed_ref, part_ref, refs = refs[:3] + (refs[3:],)
    arrived, weights, shard_parts, mid_part, tensor_parts, held, landed, refs = refs[:7] + (refs[7:],)
    (grad_sem, table_sem, state_sem, own_sem, back_sem, small_send, small_recv, tens_send, tens_recv,
     grad_send, grad_recv, weight_send, weight_recv, gather_send, gather_recv,
     scatter_send, scatter_recv) = refs
    count = lax.axis_size("shard")
    columns = lax.axis_size("tensor")
    me = lax.axis_index("shard")
    col = lax.axis_index("tensor")
    capacity, width, slab_rows = states[0].shape
    part_rows = slab_rows // count
    groups = capacity // GROUP
    group_rows = TILES * part_rows
    spare_rows = spare_out.shape[0]
    slab_count = grad_ref.shape[0]
    emb = counts_ref.shape[0]
    layer_slabs = slab_count - emb
    rest = width - LANES
    share = rest // 3
    direct_rows = packed_ref.shape[1] - spare_rows
    last_rows = direct_rows - (groups - 1) * group_rows
    direct = pl.ds(0, direct_rows)
    beyond = pl.ds(direct_rows, spare_rows)
    last = groups - 1
    weight_parts = batches(groups, WEIGHT_CUTS)
    grad_parts = grad_batches(groups)
    order = work_order(groups)

    def each(total, body):
        def step(k, carry):
            body(k)
            return carry
        lax.fori_loop(0, total, step, 0)

    def shard_peer(k):
        return lax.rem(me + peer_of(k, count), count)

    def tensor_peer(k):
        return lax.rem(col + k + 1, columns)

    def late_peer(k):
        half, front = count // 2, count // 4
        own = jnp.where(me >= half, me, jnp.where(me < front, me, me + half))
        at = jnp.where(k >= own, k + 1, k)
        near = jnp.where(at < front, at, jnp.where(at < front + half, at - front + half, at - half))
        return jnp.where(me >= half, at, near)

    fetch = pltpu.make_async_copy(grad_hbm, grad_ref, grad_sem)
    fetch.start()
    barrier = pltpu.get_barrier_semaphore()
    each(count - 1, lambda k: pl.semaphore_signal(
        barrier, inc=1, device_id=(shard_peer(k), col), device_id_type=MESH))
    each(columns - 1, lambda k: pl.semaphore_signal(
        barrier, inc=1, device_id=(me, tensor_peer(k)), device_id_type=MESH))
    owner_load.wait()
    table_ref[...] = slot_table(owner_ref[...], count)
    tabled = pltpu.make_async_copy(table_ref, slab_ref, table_sem)
    tabled.start()
    counts_load.wait()
    tabled.wait()
    fetch.wait()

    def pack(target, unit, holder, group, tiles, first):
        for j in range(GROUP):
            slab = jnp.clip(slab_ref[holder, group * GROUP + j], 0, slab_count - 1)

            def rows_of(index):
                start = (PLACES[index] - first) * part_rows
                if first == 0:
                    start = group * group_rows + start
                return pl.ds(start, part_rows)
            if PLACES[j] in tiles:
                target[unit, rows_of(j), :] = grad_ref[slab, :, 0:LANES]
            if j < 3:
                if PLACES[4 + j] in tiles:
                    target[unit, rows_of(4 + j), 0:rest] = grad_ref[slab, :, LANES:width]
            else:
                for k in range(3):
                    if PLACES[4 + k] in tiles:
                        begin = LANES + k * share
                        target[unit, rows_of(4 + k), rest:LANES] = (
                            grad_ref[slab, :, begin:begin + share]
                        )

    def tiles_of(group):
        return range(TILES) if group < last else range(last_rows // part_rows)

    def pack_group(group):
        each(count, lambda p: pack(packed_ref, p, p, group, tiles_of(group), 0))

    def small(k, sender):
        peer = shard_peer(k)
        slot = me if sender else peer
        return pltpu.make_async_remote_copy(
            part_ref, shard_parts.at[slot], small_send.at[peer], small_recv.at[slot],
            device_id=(peer, col), device_id_type=MESH)

    def tens(k, sender):
        peer = tensor_peer(k)
        slot = col if sender else peer
        return pltpu.make_async_remote_copy(
            mid_part, tensor_parts.at[slot], tens_send.at[peer], tens_recv.at[slot],
            device_id=(me, peer), device_id_type=MESH)

    def block(parts, source, target, send, recv, peer, number, sender):
        slot = me if sender else peer
        first = parts[number][0] * group_rows
        end = direct_rows if parts[number][-1] == last else (parts[number][-1] + 1) * group_rows
        window = pl.ds(first, end - first)
        return pltpu.make_async_remote_copy(
            source.at[peer, window], target.at[slot, window],
            send.at[number, peer], recv.at[number, slot],
            device_id=(peer, col), device_id_type=MESH)

    def grad_block(k, number, sender):
        return block(
            grad_parts, packed_ref, arrived, grad_send, grad_recv, shard_peer(k), number, sender
        )

    def weight_block(k, number, sender):
        peer = late_peer(k) if number >= LATE else shard_peer(k)
        return block(
            weight_parts, weights, returned, weight_send, weight_recv, peer, number, sender
        )

    distances = []
    while 2 ** len(distances) < count:
        distances.append(2 ** len(distances))

    def numbered(pairs):
        found, number = [], 0
        for d, chosen in pairs:
            found.append([(number + i, c, d) for i, c in enumerate(chosen)])
            number += len(chosen)
        return found
    gather_steps = numbered([
        (distances[-1 - at], subsets(distances[len(distances) - at:]))
        for at in range(len(distances))
    ])
    scatter_steps = numbered([
        (d, subsets(distances[at + 1:])) for at, d in enumerate(distances)
    ])

    def gather(number, chosen, d, sender):
        unit = flipped(me, chosen if sender else chosen + (d,))
        return pltpu.make_async_remote_copy(
            arrived.at[unit, beyond], arrived.at[unit, beyond], gather_send.at[number], gather_recv.at[number],
            device_id=(flipped(me, (d,)), col), device_id_type=MESH)

    def scatter(number, chosen, d):
        return pltpu.make_async_remote_copy(
            held.at[flipped(me, chosen + (d,))], landed.at[number],
            scatter_send.at[number], scatter_recv.at[number],
            device_id=(flipped(me, (d,)), col), device_id_type=MESH)

    def gather_start(at):
        for one in gather_steps[at]:
            gather(*one, True).start()

    def gather_finish(at):
        for one in gather_steps[at]:
            gather(*one, True).wait_send()
            gather(*one, False).wait_recv()

    def scatter_start(at):
        for one in scatter_steps[at]:
            scatter(*one).start()

    def scatter_finish(at):
        for one in scatter_steps[at]:
            scatter(*one).wait()
            mine = flipped(me, one[1])
            added = held[mine].astype(jnp.float32) + landed[one[0]].astype(jnp.float32)
            held[mine] = added.astype(held.dtype)

    def squares(i, carry):
        values = grad_ref[i].astype(jnp.float32)
        return carry + values * values
    acc = lax.fori_loop(
        0, layer_slabs, squares, jnp.zeros((part_rows, width), jnp.float32), unroll=10
    )
    row = lax.broadcasted_iota(jnp.int32, (part_rows, width), 0) + me * part_rows
    for e in range(emb):
        values = grad_ref[layer_slabs + e].astype(jnp.float32)
        acc += jnp.where(row < counts_ref[e], values * values, 0.0)
    part_ref[...] = jnp.broadcast_to(jnp.sum(acc, keepdims=True), part_ref.shape)
    pl.semaphore_wait(barrier, count + columns - 2)
    each(count - 1, lambda k: small(k, True).start())

    def pack_first(k):
        peer = shard_peer(k)
        for g in grad_parts[0]:
            pack(packed_ref, peer, peer, g, tiles_of(g), 0)
        grad_block(k, 0, True).start()
    each(count - 1, pack_first)
    for g in grad_parts[0]:
        pack(packed_ref, me, me, g, tiles_of(g), 0)

    loads = [pltpu.make_async_copy(old, new, state_sem.at[i])
             for i, (old, new) in enumerate(zip(old_hbm, states))]
    for load in loads:
        load.start()

    fullest = 0
    for o in range(1, count):
        fullest = jnp.where(slab_ref[o, capacity - SPARE_SLOTS] >= 0, o, fullest)
    spare_tiles = range(last_rows // part_rows, TILES)
    pack(held, 0, fullest, last, spare_tiles, last_rows // part_rows)
    arrived[me, beyond, :] = held[0]
    gather_start(0)

    def add_shard(k):
        small(k, False).wait()
        mid_part[...] += shard_parts[shard_peer(k)]

    mid_part[...] = part_ref[...]
    each(count - 1, add_shard)
    each(columns - 1, lambda k: tens(k, True).start())

    for number in range(1, len(grad_parts)):
        for g in grad_parts[number]:
            pack_group(g)
        each(count - 1, lambda k, number=number: grad_block(k, number, True).start())
    own = pltpu.make_async_copy(packed_ref.at[me, direct], arrived.at[me, direct], own_sem)
    own.start()

    gather_finish(0)
    gather_start(1)
    own.wait()
    for load in loads:
        load.wait()
    total = mid_part[0:1, :]
    each(columns - 1, lambda k: tens(k, False).wait())
    for k in range(columns - 1):
        total = total + tensor_parts[tensor_peer(k), 0:1, :]
    clip_scale = jnp.minimum(1.0, max_norm / (jnp.sqrt(total) + 1e-06))
    gather_finish(1)
    gather_start(2)

    eye = picker(slab_rows, slab_rows)

    def compute(group):
        base = group * group_rows

        def rows_of(index):
            return pl.ds(pl.multiple_of(base + PLACES[index] * part_rows, part_rows), part_rows)

        def advance(slot, window, gradient):
            place = group * GROUP + slot
            slab = slab_ref[me, place]
            live = counts_ref[jnp.clip(slab - layer_slabs, 0, emb - 1)]
            limit = jnp.where(slab < 0, -1, jnp.where(slab < layer_slabs, slab_rows, live))
            results = adam_update(
                gradient, clip_scale, limit, *[ref[place, window, :] for ref in states]
            )
            for ref, value in zip(states, results):
                ref[place, window, :] = value
            return results[0].astype(jnp.bfloat16)

        def packed(index):
            return arrived[:, rows_of(index), :].reshape(slab_rows, LANES)

        def send(index, weight):
            done = turned(eye, weight).astype(jnp.bfloat16)
            weights[:, rows_of(index), :] = done.reshape(count, part_rows, LANES)

        rest_pick = picker(rest, LANES)
        share_pick = picker(share, LANES, rest)
        rests = []
        for slot in range(GROUP):
            send(slot, advance(slot, pl.ds(0, LANES), turned(eye, packed(slot))))
            if slot < 3:
                gradient = turned(rest_pick, packed(4 + slot))
            else:
                gradient = jnp.concatenate(
                    [turned(share_pick, packed(4 + k)) for k in range(3)], axis=0
                )
            rests.append(advance(slot, pl.ds(LANES, rest), gradient))
        for k in range(3):
            piece = rests[3][k * share:(k + 1) * share]
            send(4 + k, jnp.concatenate([rests[k], piece], axis=0))

    back = pltpu.make_async_copy(weights.at[me, direct], returned.at[me, direct], back_sem)

    def turn(t, carry):
        group = 0
        for at, g in enumerate(order):
            group = jnp.where(t == at, g, group)
        for number, batch in enumerate(grad_parts):
            @pl.when(t == min(order.index(g) for g in batch))
            def _():
                each(count - 1, lambda k: grad_block(k, number, False).wait())

        @pl.when(group == last)
        def _():
            gather_finish(2)

        compute(group)

        @pl.when(group == last)
        def _():
            held[...] = weights[:, beyond, :]
            scatter_start(0)
        for number, batch in enumerate(weight_parts):
            @pl.when(t == max(order.index(g) for g in batch))
            def _():
                if number + 1 < len(weight_parts):
                    each(count - 1, lambda k: weight_block(k, number, True).start())
                else:
                    each(1, lambda k: weight_block(k, number, True).start())
        for at in range(1, len(distances)):
            @pl.when(t == groups - len(distances) + at)
            def _():
                scatter_finish(at - 1)
                scatter_start(at)
        return carry

    lax.fori_loop(0, groups, turn, 0)
    last_part = len(weight_parts) - 1
    each(1, lambda k: weight_block(k, last_part, True).wait_send())
    each(count - 1 - 1, lambda k: weight_block(k + 1, last_part, True).start())
    back.start()
    scatter_finish(len(distances) - 1)
    spare_out[...] = held[me]
    for number in range(len(weight_parts) - 1):
        each(count - 1, lambda k, number=number: weight_block(k, number, False).wait())
    final = len(weight_parts) - 1
    each(count - 1, lambda k: weight_block(k, final, False).wait_recv())
    each(count - 1 - 1, lambda k: weight_block(k + 1, final, False).wait_send())
    back.wait()


def step(owner, counts, grad, states, max_norm, mesh_sizes):
    count, columns = mesh_sizes
    capacity, width, slab_rows = states[0].shape
    part_rows = grad.shape[1]
    groups = capacity // GROUP
    grads = (len(grad_batches(groups)), count)
    sends = (len(batches(groups, WEIGHT_CUTS)), count)
    packed = (count, groups * TILES * part_rows, LANES)
    spare = (SPARE_BLOCKS * part_rows, LANES)
    vmem = pl.BlockSpec(memory_space=pltpu.VMEM)
    hbm = pl.BlockSpec(memory_space=pltpu.HBM)
    dma = pltpu.SemaphoreType.DMA
    return pl.pallas_call(
        functools.partial(step_kernel, max_norm),
        in_specs=[hbm] * 7,
        out_specs=[vmem] * 7,
        out_shape=[pltpu.VMEM(packed, grad.dtype), pltpu.VMEM(spare, grad.dtype)]
        + [pltpu.VMEM(s.shape, s.dtype) for s in states]
        + [pltpu.VMEM((count, LANES), jnp.int32)],
        scratch_shapes=[
            pltpu.SMEM((count, LANES), jnp.int32),
            pltpu.VMEM(owner.shape, owner.dtype),
            pltpu.SMEM(counts.shape, counts.dtype),
            dma(()), dma(()),
            pltpu.VMEM(grad.shape, grad.dtype),
            pltpu.VMEM(packed, grad.dtype),
            pltpu.VMEM((1, LANES), jnp.float32),
            pltpu.VMEM(packed, grad.dtype),
            pltpu.VMEM(packed, grad.dtype),
            pltpu.VMEM((count, 1, LANES), jnp.float32),
            pltpu.VMEM((1, LANES), jnp.float32),
            pltpu.VMEM((columns, 1, LANES), jnp.float32),
            pltpu.VMEM((count,) + spare, grad.dtype),
            pltpu.VMEM((count,) + spare, grad.dtype),
            dma(()), dma(()), dma((4,)), dma(()), dma(()),
            dma((count,)), dma((count,)), dma((columns,)), dma((columns,)),
            dma(grads), dma(grads), dma(sends), dma(sends),
            dma((count,)), dma((count,)), dma((count,)), dma((count,)),
        ],
        compiler_params=pltpu.CompilerParams(
            collective_id=2, has_side_effects=True, vmem_limit_bytes=40 << 20
        ),
    )(owner, counts, grad, *states)


def unpack_kernel(capacity, table_ref, packed_ref, spare_ref, *refs):
    fresh, weight_hbm, kept, weight_ref, weight_sem, kept_sem, source_ref, source_sem = (
        refs[:4], refs[4], refs[5:9], refs[9], refs[10], refs[11], refs[12], refs[13]
    )
    load = pltpu.make_async_copy(table_ref, source_ref, source_sem)
    load.start()
    stores = [pltpu.make_async_copy(new, out, kept_sem.at[i])
              for i, (new, out) in enumerate(zip(fresh, kept))]
    for store in stores:
        store.start()
    load.wait()
    slab_count, part_rows, columns = weight_hbm.shape
    rest = columns - LANES
    share = rest // 3
    groups = capacity // 4

    def unpack(t, carry):
        p = t // groups
        g = t % groups
        base = g * (7 * part_rows)

        def piece(index):
            rows = pl.ds(pl.multiple_of(base + PLACES[index] * part_rows, part_rows), part_rows)
            return packed_ref[p, rows, :]
        blocks = [piece(index) for index in range(7)]
        for j in range(4):
            slab = source_ref[p, g * 4 + j]
            slab = jnp.where(slab < 0, slab_count, slab)
            weight_ref[slab, :, 0:LANES] = blocks[j]
            if j < 3:
                weight_ref[slab, :, LANES:columns] = blocks[4 + j][:, 0:rest]
            else:
                weight_ref[slab, :, LANES:columns] = jnp.concatenate(
                    [blocks[4 + k][:, rest:LANES] for k in range(3)], axis=1
                )
        return carry
    lax.fori_loop(0, packed_ref.shape[0] * groups, unpack, 0, unroll=2)
    fullest = 0
    for p in range(1, packed_ref.shape[0]):
        first_spare = source_ref[p, capacity - SPARE_SLOTS]
        fullest = jnp.where(first_spare >= 0, p, fullest)
    last = (groups - 1) * (7 * part_rows)
    spare = [None, None] + [
        spare_ref[pl.ds(k * part_rows, part_rows), :] for k in range(SPARE_BLOCKS)
    ]
    spare[1] = packed_ref[fullest, pl.ds(last + part_rows, part_rows), :]
    for j in range(1, 4):
        slab = source_ref[fullest, capacity - 4 + j]
        slab = jnp.where(slab < 0, slab_count, slab)
        weight_ref[slab, :, 0:LANES] = spare[PLACES[j]]
        if j < 3:
            weight_ref[slab, :, LANES:columns] = spare[PLACES[4 + j]][:, 0:rest]
        else:
            weight_ref[slab, :, LANES:columns] = jnp.concatenate(
                [spare[PLACES[4 + k]][:, rest:LANES] for k in range(3)], axis=1
            )
    store = pltpu.make_async_copy(weight_ref.at[pl.ds(0, slab_count)], weight_hbm, weight_sem)
    store.start()
    store.wait()
    for store in stores:
        store.wait()


def unpack(source, packed, spare, states, weight_shape, capacity):
    slab_count, part_rows, columns = weight_shape
    vmem = pl.BlockSpec(memory_space=pltpu.VMEM)
    hbm = pl.BlockSpec(memory_space=pltpu.HBM)
    return pl.pallas_call(
        functools.partial(unpack_kernel, capacity),
        in_specs=[vmem] * 7,
        out_specs=[hbm] * 5,
        out_shape=[jax.ShapeDtypeStruct(weight_shape, packed.dtype)]
        + [jax.ShapeDtypeStruct(s.shape, s.dtype) for s in states],
        scratch_shapes=[
            pltpu.VMEM((slab_count + 1, part_rows, columns), packed.dtype),
            pltpu.SemaphoreType.DMA(()),
            pltpu.SemaphoreType.DMA((4,)),
            pltpu.SMEM(source.shape, source.dtype),
            pltpu.SemaphoreType.DMA(()),
        ],
        compiler_params=pltpu.CompilerParams(vmem_limit_bytes=40 << 20),
    )(source, packed, spare, *states)


def per_device(mesh_sizes, grad, owner, counts, master, moment1, moment2, average):
    owner_count = mesh_sizes[0]
    slab_count, part_rows, columns = grad.shape
    capacity = master.shape[0]
    slab_rows = part_rows * owner_count
    max_norm = 0.5 * math.sqrt(slab_count * slab_rows * D)
    layer_slabs = slab_count - counts.shape[0]
    self_index = lax.axis_index("shard")
    states = (master, moment1, moment2, average)

    if part_rows % 16 == 0 and capacity % 4 == 0 and (columns - LANES) * 4 == 3 * LANES and (
        owner_count & (owner_count - 1) == 0 and slab_count <= 256 and capacity <= LANES
    ):
        inputs = (owner.reshape(1, -1), counts, grad) + states
        owner, counts, grad, *states = [
            pltpu.with_memory_space_constraint(x, pltpu.HBM) for x in inputs
        ]
        returned, spare, *states, source = step(
            owner, counts, grad, states, max_norm, mesh_sizes
        )
        return tuple(unpack(source, returned, spare, states, grad.shape, capacity))

    full_counts = jnp.concatenate([jnp.full((layer_slabs,), slab_rows, jnp.int32), counts])
    row_index = self_index * part_rows + jnp.arange(part_rows, dtype=jnp.int32)
    train_live = row_index[None, :] < full_counts[:, None]
    values = grad.astype(jnp.float32)
    part = jnp.sum(jnp.where(train_live[:, :, None], values * values, 0.0))
    part = jnp.broadcast_to(part, (8, LANES))

    place, marked = slot_tables(owner, owner_count, capacity)
    source = jnp.maximum(marked - 1, 0)
    own_marked = lax.dynamic_slice_in_dim(marked, self_index * capacity, capacity)
    own_live = jnp.take(full_counts, jnp.maximum(own_marked - 1, 0), mode="clip")
    limits = jnp.where(own_marked > 0, own_live, -1)

    outgoing = jnp.take(grad, source, axis=0, mode="clip")
    outgoing = outgoing.reshape(owner_count, capacity * part_rows, columns)
    arrived, total = exchange(outgoing, part, 0, mesh_sizes)
    arrived = arrived.reshape(owner_count, capacity, part_rows, columns)
    arrived = arrived.transpose(1, 0, 2, 3).reshape(capacity, slab_rows, columns)
    weights, *new_states = adam(limits, total, arrived, *states, max_norm, None)
    weights = weights.reshape(capacity, owner_count, part_rows, columns)
    weights = weights.transpose(1, 0, 2, 3)
    weights = weights.reshape(owner_count, capacity * part_rows, columns)
    (returned,) = exchange(weights, None, 1, mesh_sizes)
    returned = returned.reshape(owner_count * capacity, part_rows, columns)
    new_weight = jnp.take(returned, place, axis=0, mode="clip")
    return (new_weight, *new_states)


def solution(mesh):
    sizes = (mesh.shape["shard"], mesh.shape["tensor"])
    return jax.shard_map(
        functools.partial(per_device, sizes),
        mesh=mesh,
        in_specs=(
            P(None, "shard", "tensor"),
            P(),
            P(),
            P("shard", "tensor", None),
            P("shard", "tensor", None),
            P("shard", "tensor", None),
            P("shard", "tensor", None),
        ),
        out_specs=(
            P(None, "shard", "tensor"),
            P("shard", "tensor", None),
            P("shard", "tensor", None),
            P("shard", "tensor", None),
            P("shard", "tensor", None),
        ),
        check_vma=False,
    )
```
